32 devices in a mesh: batch: 16 (over z, x, core), seq: 2 (over y).
Axes of the slice: x: 2, y: 2, z: 4, core: 2. Of those that a mesh axis runs over, the one named last changes fastest.
Arguments:
- inputs: bfloat16 [16, 512, 768], P('batch', 'seq'), may hold values from -6 to 6
- out_grad: bfloat16 [16, 512, 768], P('batch', 'seq'), may hold values from -6 to 6
- masked: int32 [16, 512], P('batch', 'seq'), may hold values from 0 to 1, as said below
- w_qkv: bfloat16 [2, 768, 2304], replicated, may hold values from -0.21875 to 0.21875
- bias_qv: bfloat16 [2, 2, 768], replicated, may hold values from -3 to 3
- w_out: bfloat16 [2, 768, 768], replicated, may hold values from -1.75 to 1.75
- bias_out: bfloat16 [2, 768], replicated, may hold values from -1.1953125 to 1.1953125
- gain_one: bfloat16 [2, 768], replicated, may hold values from 0.5 to 1.5
- shift_one: bfloat16 [2, 768], replicated, may hold values from -1.1953125 to 1.1953125
- w_up: bfloat16 [2, 768, 3072], replicated, may hold values from -0.21875 to 0.21875
- bias_up: bfloat16 [2, 3072], replicated, may hold values from -3 to 3
- w_down: bfloat16 [2, 3072, 768], replicated, may hold values from -0.109375 to 0.109375
- bias_down: bfloat16 [2, 768], replicated, may hold values from -1.1953125 to 1.1953125
- gain_two: bfloat16 [2, 768], replicated, may hold values from 0.5 to 1.5
- shift_two: bfloat16 [2, 768], replicated, may hold values from -1.1953125 to 1.1953125
Outputs:
- block_one: bfloat16 [16, 512, 768], P('batch', 'seq')
- block_two: bfloat16 [16, 512, 768], P('batch', 'seq')
- grad_inputs: bfloat16 [16, 512, 768], P('batch', 'seq')
- grad_w_qkv: float32 [2, 768, 2304], P(None, 'batch')
- grad_bias_qv: float32 [2, 2, 768], P(None, None, 'batch')
- grad_w_out: float32 [2, 768, 768], P(None, 'batch')
- grad_bias_out: float32 [2, 768], P(None, 'batch')
- grad_gain_one: float32 [2, 768], P(None, 'batch')
- grad_shift_one: float32 [2, 768], P(None, 'batch')
- grad_w_up: float32 [2, 768, 3072], P(None, 'batch')
- grad_bias_up: float32 [2, 3072], P(None, 'batch')
- grad_w_down: float32 [2, 3072, 768], P(None, 'batch')
- grad_bias_down: float32 [2, 768], P(None, 'batch')
- grad_gain_two: float32 [2, 768], P(None, 'batch')
- grad_shift_two: float32 [2, 768], P(None, 'batch')
The draws below stay inside these ranges and needn't reach their ends.
Inputs may be any that keep to these rules, and one draw needn't show every extreme that they name: The share of masked positions varies from sequence to sequence; some sequence has all of its 512 positions masked.
All inputs are finite; a program needn't handle non-finite values.
Results may differ from the reference program's by a relative error of at most 0.017.
Values may be sent and summed in bfloat16 or wider, within the bound.
No kernel may reach another device: no remote copies, remote signals or barrier semaphores. Data moves between devices by JAX's collectives and lax.ppermute only.
A program may use at most 192 MiB of HBM per device.

```python
import math
import jax
import jax.numpy as jnp
from jax import lax

D = 768
HEADS = 12
HEAD_DIM = 64
FF = 3072
LEN = 512
LAYERS = 2
SEQS = 16


def draw_masked(key, part):
    rate_key = jax.random.fold_in(key, 11)
    cell_key = jax.random.fold_in(key, 12)
    pick_key = jax.random.fold_in(key, 13)
    rates = jax.random.randint(rate_key, (SEQS, 1), 2, 29)
    cells = jax.random.randint(cell_key, (SEQS, LEN), 0, 100)
    chosen = jax.random.randint(pick_key, (), 0, SEQS)
    full_row = jnp.arange(SEQS, dtype=jnp.int32)[:, None] == chosen
    picked = jnp.logical_or(cells < rates, full_row)
    return jnp.where(picked, 1, 0).astype(jnp.int32)


def shard_levels(stream_key, shape, cuts, smallest, high):
    def one(dim, blocks):
        draws = jax.random.uniform(jax.random.fold_in(jax.random.fold_in(stream_key, 6), dim), (blocks,), jnp.float32, smallest / len(cuts), high / len(cuts))
        return jnp.repeat(jnp.exp(draws), shape[dim] // blocks).reshape((-1,) + (1,) * (len(shape) - dim - 1))

    loudness = one(*cuts[0])
    for cut in cuts[1:]:
        loudness = loudness * one(*cut)
    return loudness


def scatter_about(stream_key, shape, deviation, reach, cuts=(), kind=jnp.bfloat16):
    level = shard_levels(stream_key, shape, cuts, -0.22, 0.18) if cuts else 1.0
    drawn = jax.random.normal(stream_key, shape, jnp.float32) * deviation * level
    return jnp.minimum(jnp.maximum(drawn, -reach), reach).astype(kind)


def setup_inputs(seed: int = 0) -> dict:
    seeds = jax.random.split(jax.random.key(seed), 16)
    return {
        "inputs": scatter_about(seeds[0], (SEQS, LEN, D), 1.0, 6.0, ((0, 16), (1, 2))),
        "out_grad": scatter_about(seeds[1], (SEQS, LEN, D), 1.0, 6.0, ((0, 16), (1, 2))),
        "masked": draw_masked(jax.random.fold_in(seeds[15], 71), 0),
        "w_qkv": scatter_about(seeds[3], (LAYERS, D, 3 * D), D ** -0.5, 0.21875),
        "bias_qv": scatter_about(seeds[4], (LAYERS, 2, D), 0.5, 3.0),
        "w_out": scatter_about(seeds[5], (LAYERS, D, D), (D // 64) ** -0.5, 1.75),
        "bias_out": scatter_about(seeds[6], (LAYERS, D), 0.2, 1.1953125),
        "gain_one": jnp.clip(1.0 + 0.1 * jax.random.normal(seeds[7], (LAYERS, D), jnp.float32), 0.5, 1.5).astype(jnp.bfloat16),
        "shift_one": scatter_about(seeds[8], (LAYERS, D), 0.2, 1.1953125),
        "w_up": scatter_about(seeds[9], (LAYERS, D, FF), D ** -0.5, 0.21875),
        "bias_up": scatter_about(seeds[10], (LAYERS, FF), 0.5, 3.0),
        "w_down": scatter_about(seeds[11], (LAYERS, FF, D), FF ** -0.5, 0.109375),
        "bias_down": scatter_about(seeds[12], (LAYERS, D), 0.2, 1.1953125),
        "gain_two": jnp.clip(1.0 + 0.1 * jax.random.normal(seeds[13], (LAYERS, D), jnp.float32), 0.5, 1.5).astype(jnp.bfloat16),
        "shift_two": scatter_about(seeds[14], (LAYERS, D), 0.2, 1.1953125),
    }


@jax.custom_vjp
def low(v):
    return lax.optimization_barrier(v.astype(jnp.bfloat16)).astype(jnp.float32)

@jax.custom_vjp
def low_back(v):
    return v

def low_keep(v):
    return (low(v), None)

def low_pass(kept, grad):
    return (grad,)

def back_keep(v):
    return (v, None)

def back_low(kept, grad):
    return (low(grad),)
low.defvjp(low_keep, low_pass)
low_back.defvjp(back_keep, back_low)
highest = lax.Precision.HIGHEST
norm_eps = 1e-06

def layer_norm(values, norm_gain, norm_shift):
    center = values - lax.optimization_barrier(jnp.mean(values, -1, keepdims=True))
    spread = lax.optimization_barrier(jnp.mean(center * center, -1, keepdims=True))
    return center * lax.rsqrt(spread + norm_eps) * norm_gain + norm_shift

def one_layer(inputs, weights):
    w_qkv, bias_qv, w_out, bias_out, gain_one, shift_one, w_up, bias_up, w_down, bias_down, gain_two, shift_two = weights
    seq_count, row_count, model_width = inputs.shape
    low_in = low(inputs)
    bias_all = jnp.concatenate([bias_qv[0], jnp.zeros_like(bias_qv[0]), bias_qv[1]])
    projected = jnp.einsum('srd,de->sre', low_in, w_qkv, precision=highest) + bias_all
    projected = low_back(low(projected))
    per_head = projected.reshape(seq_count, row_count, 3, HEADS, HEAD_DIM)
    queries = per_head[:, :, 0]
    key_rows = per_head[:, :, 1]
    values = per_head[:, :, 2]
    scores = jnp.einsum('sqhd,skhd->shqk', queries, key_rows, precision=highest) * HEAD_DIM ** (-0.5)
    scores = low_back(scores)
    row_top = lax.optimization_barrier(jnp.max(scores, -1, keepdims=True))
    shifted = jnp.exp(scores - row_top)
    attn_prob = shifted / lax.optimization_barrier(jnp.sum(shifted, -1, keepdims=True))
    context = jnp.einsum('shqk,skhd->sqhd', low(attn_prob), values, precision=highest)
    context = low_back(low(context.reshape(seq_count, row_count, model_width)))
    attn_out = low_back(jnp.einsum('srd,de->sre', context, w_out, precision=highest) + bias_out)
    hidden = layer_norm(inputs + attn_out, gain_one, shift_one)
    pre_act = low_back(jnp.einsum('srd,df->srf', low(hidden), w_up, precision=highest) + bias_up)
    activated = low(jax.nn.gelu(pre_act, approximate=False))
    ffn_out = low_back(jnp.einsum('srf,fd->srd', activated, w_down, precision=highest) + bias_down)
    return layer_norm(hidden + ffn_out, gain_two, shift_two)

def reference(inputs, out_grad, masked, w_qkv, bias_qv, w_out, bias_out, gain_one, shift_one, w_up, bias_up, w_down, bias_down, gain_two, shift_two):
    stacked = tuple((param.astype(jnp.float32) for param in (w_qkv, bias_qv, w_out, bias_out, gain_one, shift_one, w_up, bias_up, w_down, bias_down, gain_two, shift_two)))
    group_size = math.gcd(SEQS, max(1, 4096 // LEN))

    def all_layers(seq_block, params):
        current = seq_block
        results = []
        for layer_idx in range(LAYERS):
            current = one_layer(current, tuple((param[layer_idx] for param in params)))
            results.append(current)
        return (results[0], results[-1])

    def whole_net(start_rows, params):
        blocks = start_rows.reshape(SEQS // group_size, group_size, LEN, D)
        first_out, second = lax.map(jax.checkpoint(lambda seq_block: all_layers(seq_block, params)), blocks)
        return (first_out.reshape(SEQS, LEN, D), second.reshape(SEQS, LEN, D))
    start_rows = inputs.astype(jnp.float32)
    (first_out, second), pull_back = jax.vjp(whole_net, start_rows, stacked)
    cotangent = out_grad.astype(jnp.float32) * masked.astype(jnp.float32)[..., None]
    grad_in, grad_params = pull_back((jnp.zeros_like(first_out), cotangent))
    return (first_out.astype(jnp.bfloat16), second.astype(jnp.bfloat16), grad_in.astype(jnp.bfloat16), grad_params[0], grad_params[1], grad_params[2], grad_params[3], grad_params[4], grad_params[5], grad_params[6], grad_params[7], grad_params[8], grad_params[9], grad_params[10], grad_params[11])
```

```python
import jax
import jax.numpy as jnp
from jax import lax
from jax.sharding import PartitionSpec as P

HEAD_DIM = 64
AXES = ("batch", "seq")
norm_eps = 1e-06
f32 = jnp.float32
bf16 = jnp.bfloat16


def layer_norm(values, norm_gain, norm_shift):
    center = values - jnp.mean(values, -1, keepdims=True)
    spread = jnp.mean(center * center, -1, keepdims=True)
    return center * lax.rsqrt(spread + norm_eps) * norm_gain + norm_shift


def gelu_exact(values):
    return jax.nn.gelu(values, approximate=False)


def mm(a, b, dims=((1,), (0,))):
    return lax.dot_general(a, b, (dims, ((), ())), preferred_element_type=f32)


class Wires:
    def __init__(self, batch, seq):
        self.batch, self.seq = batch, seq
        self.bits = (batch // 2).bit_length() - 1
        where = [(i, j) for i in range(batch) for j in range(seq)]

        def table(move):
            out = []
            for i, j in where:
                p, q = move(i, j)
                out.append((i * seq + j, p * seq + q))
            return out

        self.core = table(lambda i, j: (i ^ 1, j))
        self.row = table(lambda i, j: (i, 1 - j))
        self.turn = table(lambda i, j: (i - i % 2 + j, i % 2))
        self.chip = [table(lambda i, j, k=k: (i ^ (2 << k), j)) for k in range(self.bits)]
        self.b = lax.axis_index("batch")
        self.y = lax.axis_index("seq")
        self.c = self.b % 2

    def swap_core(self, v):
        return lax.ppermute(v, AXES, self.core)

    def swap_row(self, v):
        return lax.ppermute(v, AXES, self.row)

    def swap_turn(self, v):
        return lax.ppermute(v, AXES, self.turn)

    def swap_chip(self, v, k):
        return lax.ppermute(v, AXES, self.chip[k])

    def bit(self, k):
        return (self.b >> (k + 1)) & 1


def pick(v, idx, axis):
    return lax.dynamic_index_in_dim(v, idx, axis, keepdims=False)


def add(a, b):
    return a.astype(f32) + b.astype(f32)


def reduce_rows(wires, grad, order, row_first):
    rows, cols = grad.shape
    part = rows // wires.batch
    v = grad.reshape((2,) * wires.bits + (2, part, cols))
    left = list(range(wires.bits))[::-1]
    if row_first:
        ax = wires.bits
        got = wires.swap_row(pick(v, 1 - wires.y, ax))
        v = add(pick(v, wires.y, ax), got).astype(bf16)
    for k in order:
        ax = left.index(k)
        left.pop(ax)
        got = wires.swap_chip(pick(v, 1 - wires.bit(k), ax), k)
        v = add(pick(v, wires.bit(k), ax), got).astype(bf16)
    if row_first:
        other = wires.swap_row(v)
        first = wires.y == 0
        v = jnp.stack([jnp.where(first, v, other), jnp.where(first, other, v)])
    else:
        v = add(v, wires.swap_row(v)).astype(bf16)
    mine = pick(v, wires.c, 0).astype(f32)
    got = wires.swap_core(pick(v, 1 - wires.c, 0)).astype(f32)
    return jnp.stack([jnp.where(wires.c == 0, mine, got), jnp.where(wires.c == 0, got, mine)], 1)


def reduce_small(wires, v):
    v = add(v, wires.swap_row(v))
    v = v.reshape((2,) * (wires.bits + 1) + (-1,))
    got = wires.swap_core(pick(v, 1 - wires.c, wires.bits))
    v = pick(v, wires.c, wires.bits) + got
    for k in range(wires.bits):
        ax = wires.bits - 1 - k
        got = wires.swap_chip(pick(v, 1 - wires.bit(k), ax), k)
        v = pick(v, wires.bit(k), ax) + got
    return v


def own_cols(w, c, groups):
    rows, cols = w.shape
    return pick(w.reshape(rows, groups, 2, cols // groups // 2), c, 2).reshape(rows, cols // 2)


def layer_forward(wires, x, xb, weights):
    (w_qkv, bias_qv, w_out, bias_out, gain_one, shift_one, w_up, bias_up, w_down, bias_down, gain_two, shift_two) = weights
    rows, width = x.shape
    c = wires.c
    half = width // 2
    heads = half // HEAD_DIM
    xf = jnp.concatenate([xb, wires.swap_core(xb)])
    w_own = own_cols(w_qkv, c, 3)
    bias_all = jnp.stack([bias_qv[0], jnp.zeros_like(bias_qv[0]), bias_qv[1]]).astype(f32)
    bias_own = pick(bias_all.reshape(3, 2, half), c, 1).reshape(3 * half)
    proj = (mm(xf, w_own) + bias_own).astype(bf16).reshape(2 * rows, 3, heads, HEAD_DIM)
    q, k, v = proj[:, 0], proj[:, 1], proj[:, 2]
    scores = jnp.einsum("qhd,khd->hqk", q, k, preferred_element_type=f32) * HEAD_DIM ** (-0.5)
    top = jnp.max(scores, -1, keepdims=True)
    shifted = jnp.exp(scores - top)
    total = jnp.sum(shifted, -1, keepdims=True)
    prob = (shifted / total).astype(bf16)
    lse = top + jnp.log(total)
    ctx = jnp.einsum("hqk,khd->qhd", prob, v, preferred_element_type=f32).astype(bf16).reshape(2 * rows, half)
    got = wires.swap_core(ctx)
    got = jnp.concatenate([got[rows:], got[:rows]])
    ctxf = jnp.where(c == 0, jnp.concatenate([ctx, got], 1), jnp.concatenate([got, ctx], 1))
    mixed = x + mm(ctxf[:rows], w_out) + bias_out.astype(f32)
    hidden = layer_norm(mixed, gain_one.astype(f32), shift_one.astype(f32))
    hb = hidden.astype(bf16)
    pre = mm(hb, w_up) + bias_up.astype(f32)
    act = gelu_exact(pre).astype(bf16)
    summed = hidden + mm(act, w_down) + bias_down.astype(f32)
    y = layer_norm(summed, gain_two.astype(f32), shift_two.astype(f32))
    hf = jnp.concatenate([hb, wires.swap_core(hb)])
    actf = jnp.concatenate([act, wires.swap_core(act)])
    return y, (xf, w_own, q, k, v, lse, ctxf, mixed, hf, pre, actf, summed)


def layer_backward(wires, gy, stored, weights):
    (w_qkv, bias_qv, w_out, bias_out, gain_one, shift_one, w_up, bias_up, w_down, bias_down, gain_two, shift_two) = weights
    xf, w_own, q, k, v, lse, ctxf, mixed, hf, pre, actf, summed = stored
    c = wires.c
    rows, width = gy.shape
    half = width // 2
    _, pull_two = jax.vjp(layer_norm, summed, gain_two.astype(f32), shift_two.astype(f32))
    gsum, ggain2, gshift2 = pull_two(gy)
    gf = gsum.astype(bf16)
    gbias_down = jnp.sum(gf.astype(f32), 0)
    gact = mm(gf, w_down, ((1,), (1,)))
    _, pull_gelu = jax.vjp(gelu_exact, pre)
    gpre = pull_gelu(gact)[0].astype(bf16)
    gbias_up = jnp.sum(gpre.astype(f32), 0)
    ghid = gsum + mm(gpre, w_up, ((1,), (1,)))
    _, pull_one = jax.vjp(layer_norm, mixed, gain_one.astype(f32), shift_one.astype(f32))
    gmix, ggain1, gshift1 = pull_one(ghid)
    gattn = gmix.astype(bf16)
    gbias_out = jnp.sum(gattn.astype(f32), 0)

    def halves(g):
        g2 = g.reshape(rows, 2, -1)
        return jnp.concatenate([pick(g2, c, 1), wires.swap_core(pick(g2, 1 - c, 1))])

    gattnf = jnp.concatenate([gattn, wires.swap_core(gattn)])
    gw_down = mm(actf, halves(gf), ((0,), (0,))).astype(bf16)
    gw_up = mm(hf, halves(gpre), ((0,), (0,))).astype(bf16)
    gattn_own = pick(gattnf.reshape(2 * rows, 2, half), c, 1)
    gw_out = mm(ctxf, gattn_own, ((0,), (0,))).astype(bf16)
    w_rows = pick(w_out.reshape(2, half, width), c, 0)
    gctx = mm(gattnf, w_rows, ((1,), (1,))).astype(bf16).reshape(2 * rows, -1, HEAD_DIM)
    scale = HEAD_DIM ** (-0.5)
    scores = jnp.einsum("qhd,khd->hqk", q, k, preferred_element_type=f32) * scale
    prob = jnp.exp(scores - lse)
    gv = jnp.einsum("hqk,qhd->khd", prob.astype(bf16), gctx, preferred_element_type=f32)
    gp = jnp.einsum("qhd,khd->hqk", gctx, v, preferred_element_type=f32)
    inner = jnp.sum(prob * gp, -1, keepdims=True)
    gs = (prob * (gp - inner)).astype(bf16)
    gq = jnp.einsum("hqk,khd->qhd", gs, k, preferred_element_type=f32) * scale
    gk = jnp.einsum("hqk,qhd->khd", gs, q, preferred_element_type=f32) * scale
    gproj = jnp.stack([gq, gk, gv], 1).astype(bf16).reshape(2 * rows, 3 * half)
    gsums = jnp.sum(gproj.astype(f32), 0).reshape(3, half)
    gqv = jnp.stack([gsums[0], gsums[2]])
    zero = jnp.zeros_like(gqv)
    gbias_qv = jnp.where(c == 0, jnp.concatenate([gqv, zero], 1), jnp.concatenate([zero, gqv], 1))
    gw_qkv = mm(xf, gproj, ((0,), (0,))).astype(bf16)
    got = wires.swap_core(gproj[rows:])
    w_oth = own_cols(w_qkv, 1 - c, 3)
    gx = gmix + mm(gproj[:rows], w_own, ((1,), (1,))) + mm(got, w_oth, ((1,), (1,)))
    nb = wires.batch
    small = jnp.concatenate(
        [g.reshape(nb, -1) for g in (gbias_qv[0], gbias_qv[1], gbias_out, ggain1, gshift1, gbias_up, gbias_down, ggain2, gshift2)], 1
    )
    bits = list(range(wires.bits))
    part = width // nb
    down = reduce_rows(wires, gw_down, bits[1:] + bits[:1], False).reshape(-1, width)
    up = reduce_rows(wires, gw_up, bits, False).reshape(part, -1)
    tail = reduce_rows(wires, jnp.concatenate([gw_qkv, gw_out], 1), bits, True)
    qkv = tail[:, :, : 3 * half].reshape(part, 2, 3, half).transpose(0, 2, 1, 3).reshape(part, 3 * width)
    out = tail[:, :, 3 * half :].reshape(part, width)
    return gx, small, (qkv, out, up, down)


def local(inputs, out_grad, masked, *stacked):
    wires = Wires(lax.axis_size("batch"), lax.axis_size("seq"))
    layers = stacked[0].shape[0]
    xb = wires.swap_turn(inputs[0])
    gy = wires.swap_turn((out_grad * masked.astype(bf16)[..., None])[0])
    x = xb.astype(f32)
    saved, outs = [], []
    for l in range(layers):
        weights = tuple(p[l] for p in stacked)
        x, st = layer_forward(wires, x, xb, weights)
        xb = x.astype(bf16)
        saved.append(st)
        outs.append(wires.swap_turn(xb)[None])
    gy = gy.astype(f32)
    smalls, bigs = [None] * layers, [None] * layers
    for l in reversed(range(layers)):
        weights = tuple(p[l] for p in stacked)
        gy, smalls[l], bigs[l] = layer_backward(wires, gy, saved[l], weights)
    grad_in = wires.swap_turn(gy.astype(bf16))[None]
    small = reduce_small(wires, jnp.concatenate(smalls, 1)).reshape(layers, -1)
    qkv, out, up, down = (jnp.stack([g[i] for g in bigs]) for i in range(4))
    p = stacked[0].shape[1] // wires.batch
    cut = [0, 2 * p, 3 * p, 4 * p, 5 * p]
    up_part = stacked[7].shape[1] // wires.batch
    pieces, at = [], 0
    for n in (2 * p, p, p, p, up_part, p, p, p):
        pieces.append(small[:, at : at + n])
        at += n
    bqv, bout, g1, s1, bup, bdown, g2, s2 = pieces
    return (outs[0], outs[-1], grad_in, qkv, bqv.reshape(layers, 2, p), out, bout, g1, s1, up, bup, down, bdown, g2, s2)


def solution(mesh):
    tok = P("batch", "seq", None)
    in_specs = (tok, tok, P("batch", "seq")) + (P(),) * 12
    mat, vec = P(None, "batch", None), P(None, "batch")
    out_specs = (tok, tok, tok, mat, P(None, None, "batch"), mat, vec, vec, vec, mat, vec, mat, vec, vec, vec)
    return jax.shard_map(local, mesh=mesh, in_specs=in_specs, out_specs=out_specs, check_vma=False)
```

```python
import math

import jax
import jax.numpy as jnp
from jax import lax
from jax.experimental import pallas as pl
from jax.experimental.pallas import tpu as pltpu
from jax.sharding import PartitionSpec as P

HEAD_DIM = 64
AXES = ("batch", "seq")
norm_eps = 1e-06
f32 = jnp.float32
bf16 = jnp.bfloat16
ANY = pl.BlockSpec(memory_space=pl.ANY)
HBM = pl.BlockSpec(memory_space=pltpu.HBM)
VM = pl.BlockSpec(memory_space=pltpu.VMEM)
SM = pl.BlockSpec(memory_space=pltpu.SMEM)
ROOT_HALF = 0.7071067811865476
INV_ROOT_TAU = 0.3989422804014327
EASE = 1


def mm(a, b, dims=((1,), (0,))):
    return lax.dot_general(a, b, (dims, ((), ())), preferred_element_type=f32)


NT = ((1,), (1,))
TN = ((0,), (0,))


class Mover:
    def __init__(self, sems):
        self.sems, self.used = sems, 0

    def go(self, src, dst):
        copy = pltpu.make_async_copy(src, dst, self.sems.at[self.used])
        self.used += 1
        copy.start()
        return copy


class Row:
    def __init__(self):
        self.extra = []

    def before_next(self, *values):
        self.extra.extend(values)


ROW = Row()


def kernel_call(body, name, args, specs, outs, out_specs, scratch, sems, flops, moved):
    extra = tuple(ROW.extra)
    n, m = len(args), len(args) + len(extra)
    held = sum(math.prod(v.shape) * jnp.dtype(v.dtype).itemsize for v in scratch)
    limit = held + ((2 << 20) if name == "merge" else (12 << 20))
    args = tuple(
        pltpu.with_memory_space_constraint(a, pltpu.HBM) if spec is HBM else a for a, spec in zip(args, specs)
    )
    out = pl.pallas_call(
        lambda *refs: body(*refs[:n], *refs[m:]),
        name=name,
        out_shape=outs,
        in_specs=specs + [ANY] * len(extra),
        out_specs=out_specs,
        scratch_shapes=list(scratch) + [pltpu.SemaphoreType.DMA((sems,))],
        compiler_params=pltpu.CompilerParams(vmem_limit_bytes=limit),
        cost_estimate=pl.CostEstimate(flops=flops // EASE, bytes_accessed=moved // EASE, transcendentals=0),
    )(*args, *extra)
    ROW.extra = [out[0] if isinstance(out, (tuple, list)) else out]
    return out


def merge(keep, got):
    n = max(keep.shape[0] // 2, 1)
    rest = keep.shape[1:]
    parts = keep.shape[0] // n

    def body(k, g, *refs):
        outs, (k_v, g_v, sems) = refs[:parts], refs[parts:]
        mv = Mover(sems)
        at = [pl.ds((parts - 1 - i) * n, n) for i in range(parts)]
        come = [(mv.go(k.at[a], k_v.at[a]), mv.go(g.at[a], g_v.at[a])) for a in at]
        gone = []
        for i, a in enumerate(at):
            for c in come[i]:
                c.wait()

            def one(j, _):
                j = j + (parts - 1 - i) * n
                k_v[j] = (k_v[j].astype(f32) + g_v[j].astype(f32)).astype(bf16)
                return 0

            lax.fori_loop(0, n, one, 0)
            gone.append(mv.go(k_v.at[a], outs[i]))
        for c in gone:
            c.wait()

    outs = (jax.ShapeDtypeStruct((n,) + rest, bf16),) * parts
    return kernel_call(body, "merge", (keep, got), [ANY, ANY], outs, (ANY,) * parts, [pltpu.VMEM(keep.shape, bf16)] * 2, 3 * parts, 5 * 10**9, 0)


def normed(z):
    center = z - jnp.mean(z, -1, keepdims=True)
    rstd = lax.rsqrt(jnp.mean(center * center, -1, keepdims=True) + norm_eps)
    return center * rstd, rstd


def norm_back(g, z, gain):
    xhat, rstd = normed(z)
    gx = g * gain
    m1 = jnp.mean(gx, -1, keepdims=True)
    m2 = jnp.mean(gx * xhat, -1, keepdims=True)
    return rstd * (gx - m1 - xhat * m2), g * xhat


def phi_parts(u):
    cdf = 0.5 * (1.0 + lax.erf(u * ROOT_HALF))
    return cdf, cdf + u * (jnp.exp(-0.5 * u * u) * INV_ROOT_TAU)


def attn_fwd(info, l, xo, xt, w_qkv, bias_qv):
    rows, width = xo.shape
    half = width // 2
    heads = half // HEAD_DIM
    toks = 2 * rows

    def body(info, xo, xt, w, bias, qkv_o, pt_o, ctx_o, x_v, w_v, qkv_v, pt_v, ctx_v, sems):
        mv = Mover(sems)
        c = info[0]
        cx = [mv.go(xo, x_v.at[pl.ds(0, rows)]), mv.go(xt, x_v.at[pl.ds(rows, rows)])]
        cw = []
        for p in range(3):
            at = pl.multiple_of(p * width + c * half, 128)
            cw.append(mv.go(w.at[l, :, pl.ds(at, half)], w_v.at[p]))
        for k in cx:
            k.wait()
        at = pl.multiple_of(c * half, 128)
        for p in range(3):
            cw[p].wait()
            val = mm(x_v[...], w_v[p])
            if p != 1:
                val = val + bias[l, pl.ds(p // 2, 1), pl.ds(at, half)].astype(f32)
            val = val.astype(bf16)
            if p == 0:
                val = (val.astype(f32) * HEAD_DIM ** (-0.5)).astype(bf16)
            qkv_v[:, p * half : (p + 1) * half] = val
        out = [mv.go(qkv_v, qkv_o)]
        lane = lax.broadcasted_iota(jnp.int32, (toks, 2 * HEAD_DIM), 1) < HEAD_DIM

        def pair(i, _):
            at = pl.multiple_of(i * 2 * HEAD_DIM, 128)
            q = qkv_v[:, pl.ds(at, 128)]
            k = qkv_v[:, pl.ds(pl.multiple_of(half + at, 128), 128)]
            v = qkv_v[:, pl.ds(pl.multiple_of(2 * half + at, 128), 128)]
            both = []
            for h in range(2):
                qm = jnp.where(lane == (h == 0), q, jnp.zeros_like(q))
                st = mm(k, qm, NT)
                top = jnp.max(st, 0, keepdims=True)
                e = jnp.exp(st - top)
                p = (e / jnp.sum(e, 0, keepdims=True)).astype(bf16)
                pt_v[2 * i + h] = p
                both.append(mm(p, v, TN))
            ctx_v[:, pl.ds(at, 128)] = jnp.where(lane, both[0], both[1]).astype(bf16)
            return 0

        lax.fori_loop(0, heads // 2, pair, 0)
        out += [mv.go(ctx_v, ctx_o), mv.go(pt_v, pt_o)]
        for k in out:
            k.wait()

    S = jax.ShapeDtypeStruct
    outs = (S((toks, 3 * half), bf16), S((heads, toks, toks), bf16), S((toks, half), bf16))
    return kernel_call(
        body, "attn_fwd", (info, xo, xt, w_qkv, bias_qv), [SM, ANY, ANY, HBM, VM], outs, (ANY,) * 3,
        [pltpu.VMEM((toks, width), bf16), pltpu.VMEM((3, width, half), bf16), pltpu.VMEM((toks, 3 * half), bf16),
         pltpu.VMEM((heads, toks, toks), bf16), pltpu.VMEM((toks, half), bf16)],
        8, 2 * toks * width * 3 * half + 8 * heads * toks * toks * 128, 8 << 20,
    )


def ffn_fwd(info, l, x, ctx, got, weights, cut=6):
    w_out, bias_out, gain_one, shift_one, w_up, bias_up, w_down, bias_down, gain_two, shift_two = weights
    rows, width = x.shape
    half = width // 2
    ff = w_up.shape[2]
    step = ff // cut

    def body(info, x, ctx, got, wo, bo, g1, s1, wu, bu, wd, bd, g2, s2,
             hb_o, dg_o, mixed_o, summed_o, y_o, yb_o,
             x_v, c_v, wo_v, wu_v, wd_v, hb_v, dg_v, mixed_v, hid_v, y_v, yb_v, sems):
        mv = Mover(sems)
        c = info[0]
        first = [mv.go(ctx.at[pl.ds(0, rows)], c_v.at[0])]
        at = [pl.multiple_of(c * half, 128), pl.multiple_of((1 - c) * half, 128)]
        first += [mv.go(wo.at[l, pl.ds(at[i], half)], wo_v.at[i]) for i in range(2)]
        first += [mv.go(got.at[pl.ds(rows, rows)], c_v.at[1]), mv.go(x, x_v)]
        cu, cd = [], []
        for j in range(cut):
            cu.append(mv.go(wu.at[l, :, pl.ds(j * step, step)], wu_v.at[j]))
            cd.append(mv.go(wd.at[l, pl.ds(j * step, step)], wd_v.at[j]))
        for k in first:
            k.wait()
        mixed = x_v[...] + mm(c_v[0], wo_v[0]) + mm(c_v[1], wo_v[1]) + bo[pl.ds(l, 1)].astype(f32)
        mixed_v[...] = mixed
        out = [mv.go(mixed_v, mixed_o)]
        hid = normed(mixed)[0] * g1[pl.ds(l, 1)].astype(f32) + s1[pl.ds(l, 1)].astype(f32)
        hid_v[...] = hid
        hb_v[...] = hid.astype(bf16)
        out.append(mv.go(hb_v, hb_o))
        acc = None
        for j in range(cut):
            cu[j].wait()
            u = mm(hb_v[...], wu_v[j]) + bu[pl.ds(l, 1), j * step : (j + 1) * step].astype(f32)
            cdf, slope = phi_parts(u)
            dg_v[:, j * step : (j + 1) * step] = slope.astype(bf16)
            cd[j].wait()
            part = mm((u * cdf).astype(bf16), wd_v[j])
            acc = part if acc is None else acc + part
        out.append(mv.go(dg_v, dg_o))
        summed = hid_v[...] + acc + bd[pl.ds(l, 1)].astype(f32)
        x_v[...] = summed
        out.append(mv.go(x_v, summed_o))
        y = normed(summed)[0] * g2[pl.ds(l, 1)].astype(f32) + s2[pl.ds(l, 1)].astype(f32)
        y_v[...] = y
        yb_v[...] = y.astype(bf16)
        out += [mv.go(yb_v, yb_o), mv.go(y_v, y_o)]
        for k in out:
            k.wait()

    S = jax.ShapeDtypeStruct
    full, low = S((rows, width), f32), S((rows, width), bf16)
    outs = (low, S((rows, ff), bf16), full, full, full, low)
    V = pltpu.VMEM
    return kernel_call(
        body, "ffn_fwd",
        (info, x, ctx, got, w_out, bias_out, gain_one, shift_one, w_up, bias_up, w_down, bias_down, gain_two, shift_two),
        [SM, ANY, ANY, ANY, HBM, VM, VM, VM, HBM, VM, HBM, VM, VM, VM], outs, (ANY,) * 6,
        [V((rows, width), f32), V((2, rows, half), bf16), V((2, half, width), bf16), V((cut, width, step), bf16),
         V((cut, step, width), bf16), V((rows, width), bf16), V((rows, ff), bf16), V((rows, width), f32),
         V((rows, width), f32), V((rows, width), f32), V((rows, width), bf16)],
        11 + 2 * cut, 2 * rows * width * (width + 2 * ff), 12 << 20,
    )


def ffn_bwd(info, l, flow, summed, mixed, dg, weights, cut=6):
    w_up, w_down, gain_one, gain_two = weights
    rows, width = summed.shape
    half = width // 2
    ff = w_up.shape[2]
    step = ff // cut
    chained = len(flow) > 1

    def body(*refs):
        info = refs[0]
        fl = refs[1 : 1 + len(flow)]
        (sm, mi, dgr, wu, wd, g1, g2, gf_o, ga_o, gm_o, small_o, gbup_o,
         gy_v, sm_v, mi_v, dg_v, wu_v, wd_v, gf_v, ga_v, gm_v) = refs[1 + len(flow) : 22 + len(flow)]
        sems = refs[-1]
        mv = Mover(sems)
        if chained:
            gp_v, wq_v = refs[22 + len(flow) : 24 + len(flow)]
            c = info[0]
            fc = [mv.go(fl[0], gy_v), mv.go(fl[1].at[pl.ds(0, rows)], gp_v.at[0])]
            wq = []
            for i in range(2):
                who = c if i == 0 else 1 - c
                for p in range(3):
                    at = pl.multiple_of(p * width + who * half, 128)
                    wq.append(mv.go(fl[3].at[l + 1, :, pl.ds(at, half)], wq_v.at[i, p]))
            fc.append(mv.go(fl[2], gp_v.at[1]))
        else:
            fc = [mv.go(fl[0], gf_v)]
        fc += [mv.go(sm, sm_v)]
        cd, cu, cg = [], [], []
        for j in range(cut):
            cols = pl.ds(j * step, step)
            cd.append(mv.go(wd.at[l, cols], wd_v.at[j]))
            cg.append(mv.go(dgr.at[:, cols], dg_v.at[j]))
            cu.append(mv.go(wu.at[l, :, cols], wu_v.at[j]))
        cm = mv.go(mi, mi_v)
        for k in fc:
            k.wait()
        if chained:
            gy = gy_v[...]
            for i in range(2):
                for p in range(3):
                    wq[3 * i + p].wait()
                    gy = gy + mm(gp_v[i, :, p * half : (p + 1) * half], wq_v[i, p], NT)
        else:
            gy = gf_v[...].astype(f32)
        gsum, gterm = norm_back(gy, sm_v[...], g2[pl.ds(l, 1)].astype(f32))
        small_o[1:2] = jnp.sum(gterm, 0, keepdims=True)
        small_o[2:3] = jnp.sum(gy, 0, keepdims=True)
        gf = gsum.astype(bf16)
        gf_v[...] = gf
        small_o[0:1] = jnp.sum(gf.astype(f32), 0, keepdims=True)
        out = [mv.go(gf_v, gf_o)]
        gm_v[...] = gsum
        acc = None
        for j in range(cut):
            cd[j].wait()
            cg[j].wait()
            gpre = (mm(gf_v[...], wd_v[j], NT) * dg_v[j].astype(f32)).astype(bf16)
            gbup_o[:, j * step : (j + 1) * step] = jnp.sum(gpre.astype(f32), 0, keepdims=True)
            cu[j].wait()
            part = mm(gpre, wu_v[j], NT)
            acc = part if acc is None else acc + part
        ghid = gm_v[...] + acc
        cm.wait()
        gmix, gterm = norm_back(ghid, mi_v[...], g1[pl.ds(l, 1)].astype(f32))
        ga = gmix.astype(bf16)
        ga_v[...] = ga
        out.append(mv.go(ga_v, ga_o))
        gm_v[...] = gmix
        out.append(mv.go(gm_v, gm_o))
        small_o[3:4] = jnp.sum(gterm, 0, keepdims=True)
        small_o[4:5] = jnp.sum(ghid, 0, keepdims=True)
        small_o[5:6] = jnp.sum(ga.astype(f32), 0, keepdims=True)
        small_o[6:8] = jnp.zeros((2, width), f32)
        for k in out:
            k.wait()

    S, V = jax.ShapeDtypeStruct, pltpu.VMEM
    low = S((rows, width), bf16)
    outs = (low, low, S((rows, width), f32), S((8, width), f32), S((1, ff), f32))
    scratch = [V((rows, width), f32), V((rows, width), f32), V((rows, width), f32), V((cut, rows, step), bf16),
               V((cut, width, step), bf16), V((cut, step, width), bf16), V((rows, width), bf16), V((rows, width), bf16),
               V((rows, width), f32)]
    if chained:
        scratch += [V((2, rows, 3 * half), bf16), V((2, 3, width, half), bf16)]
    return kernel_call(
        body, "ffn_bwd", (info,) + tuple(flow) + (summed, mixed, dg, w_up, w_down, gain_one, gain_two),
        [SM] + [ANY, ANY, ANY, HBM][: len(flow)] + [ANY] * 3 + [HBM, HBM, VM, VM], outs, (ANY, ANY, ANY, VM, VM), scratch,
        15 + 3 * cut, 2 * rows * width * (2 * ff + (3 * width if chained else 0)), 15 << 20,
    )


def chain_end(info, l, flow):
    gmix, gproj, got, w_qkv = flow
    rows, width = gmix.shape
    half = width // 2

    def body(info, gm, gp, gt, w, o_ref, gy_v, gp_v, wq_v, o_v, sems):
        mv = Mover(sems)
        c = info[0]
        wq = []
        fc = [mv.go(gm, gy_v), mv.go(gp.at[pl.ds(0, rows)], gp_v.at[0]), mv.go(gt, gp_v.at[1])]
        for i in range(2):
            who = c if i == 0 else 1 - c
            for p in range(3):
                at = pl.multiple_of(p * width + who * half, 128)
                wq.append(mv.go(w.at[l, :, pl.ds(at, half)], wq_v.at[i, p]))
        for k in fc:
            k.wait()
        gy = gy_v[...]
        for i in range(2):
            for p in range(3):
                wq[3 * i + p].wait()
                gy = gy + mm(gp_v[i, :, p * half : (p + 1) * half], wq_v[i, p], NT)
        o_v[...] = gy.astype(bf16)
        k = mv.go(o_v, o_ref)
        k.wait()

    S, V = jax.ShapeDtypeStruct, pltpu.VMEM
    return kernel_call(
        body, "chain_end", (info,) + tuple(flow), [SM, ANY, ANY, ANY, HBM], S((rows, width), bf16), ANY,
        [V((rows, width), f32), V((2, rows, 3 * half), bf16), V((2, 3, width, half), bf16), V((rows, width), bf16)],
        10, 2 * rows * width * 3 * width, 5 << 20,
    )


def attn_bwd(info, l, go, gt, w_out, qkv, pt):
    rows, width = go.shape
    half = width // 2
    heads = half // HEAD_DIM
    toks = 2 * rows

    def body(info, go, gt, wo, qkv, pt, gp_o, gb_o, ga_v, wo_v, qkv_v, pt_v, gc_v, gp_v, sems):
        mv = Mover(sems)
        c = info[0]
        at = pl.multiple_of(c * half, 128)
        fc = [mv.go(wo.at[l, pl.ds(at, half)], wo_v), mv.go(go, ga_v.at[pl.ds(0, rows)]), mv.go(gt, ga_v.at[pl.ds(rows, rows)])]
        cq = mv.go(qkv, qkv_v)
        cp = mv.go(pt, pt_v)
        for k in fc:
            k.wait()
        gc_v[...] = mm(ga_v[...], wo_v[...], NT).astype(bf16)
        cq.wait()
        cp.wait()
        lane = lax.broadcasted_iota(jnp.int32, (toks, 2 * HEAD_DIM), 1) < HEAD_DIM

        def pair(i, _):
            at = pl.multiple_of(i * 2 * HEAD_DIM, 128)
            at_k, at_v = pl.multiple_of(half + at, 128), pl.multiple_of(2 * half + at, 128)
            q = qkv_v[:, pl.ds(at, 128)]
            k = qkv_v[:, pl.ds(at_k, 128)]
            v = qkv_v[:, pl.ds(at_v, 128)]
            gc = gc_v[:, pl.ds(at, 128)]
            res = []
            for h in range(2):
                gm = jnp.where(lane == (h == 0), gc, jnp.zeros_like(gc))
                pb = pt_v[2 * i + h]
                t = mm(v, gm, NT)
                p = pb.astype(f32)
                inner = jnp.sum(p * t, 0, keepdims=True)
                gs = (p * (t - inner)).astype(bf16)
                res.append((mm(gs, k, TN), mm(gs, q), mm(pb, gc)))
            gq = jnp.where(lane, res[0][0], res[1][0]) * HEAD_DIM ** (-0.5)
            gk = jnp.where(lane, res[0][1], res[1][1])
            gv = jnp.where(lane, res[0][2], res[1][2])
            gq, gk, gv = gq.astype(bf16), gk.astype(bf16), gv.astype(bf16)
            gp_v[:, pl.ds(at, 128)] = gq
            gp_v[:, pl.ds(at_k, 128)] = gk
            gp_v[:, pl.ds(at_v, 128)] = gv
            gb_o[0:1, pl.ds(at, 128)] = jnp.sum(gq.astype(f32), 0, keepdims=True)
            gb_o[1:2, pl.ds(at, 128)] = jnp.sum(gv.astype(f32), 0, keepdims=True)
            return 0

        lax.fori_loop(0, heads // 2, pair, 0)
        k = mv.go(gp_v, gp_o)
        k.wait()

    S, V = jax.ShapeDtypeStruct, pltpu.VMEM
    return kernel_call(
        body, "attn_bwd", (info, go, gt, w_out, qkv, pt), [SM, ANY, ANY, HBM, ANY, ANY],
        (S((toks, 3 * half), bf16), S((2, half), f32)), (ANY, VM),
        [V((toks, width), bf16), V((half, width), bf16), V((toks, 3 * half), bf16), V((heads, toks, toks), bf16),
         V((toks, half), bf16), V((toks, 3 * half), bf16)],
        6, 2 * toks * width * half + 20 * heads * toks * toks * 128, 7 << 20,
    )


def place(j, me, order):
    d = jnp.bitwise_xor(j, me)
    n = len(order)
    p = 0
    for i, k in enumerate(order):
        p = p + (jnp.bitwise_and(jnp.right_shift(d, k), 1) << (n - 1 - i))
    return p


def arranged(v, me, order):
    n = len(order)
    rest = v.shape[1:]
    v = v.reshape((2,) * n + rest)
    for k in range(n):
        ax = n - 1 - k
        v = jnp.where(((me >> k) & 1) == 1, jnp.flip(v, ax), v)
    v = v.transpose([n - 1 - k for k in order] + list(range(n, n + len(rest))))
    return v.reshape((2**n,) + rest)


def own_units(info, w_up, chips):
    layers, width, ff = w_up.shape
    part = ff // chips // 4
    fo = ff // 4
    strip = 128

    def body(info, w, o_ref, w_v, o_v, sems):
        mv = Mover(sems)
        cw = [mv.go(w.at[l], w_v.at[l]) for l in range(layers)]
        out = []
        for l in range(layers):
            cw[l].wait()
            for s in range(4):

                @pl.when(info[3] == s)
                def _():
                    def some(r, _):
                        at = pl.ds(pl.multiple_of(r * strip, strip), strip)
                        for i in range(chips):
                            o_v[l, at, i * part : (i + 1) * part] = w_v[l, at, (4 * i + s) * part : (4 * i + s + 1) * part]
                        return 0

                    lax.fori_loop(0, width // strip, some, 0)

            out.append(mv.go(o_v.at[l], o_ref.at[l]))
        for k in out:
            k.wait()

    S, V = jax.ShapeDtypeStruct, pltpu.VMEM
    return kernel_call(
        body, "own_units", (info, w_up), [SM, HBM], S((layers, width, fo), bf16), ANY,
        [V((layers, width, ff), bf16), V((layers, width, fo), bf16)], 2 * layers, 0, 12 << 20,
    )


def ffn_grads(info, l, hs, gs, wu_own, w_down, b_own, small, gbup, gqv, order, fast):
    rows, width = hs[0].shape
    layers, _, fo = wu_own.shape
    n = len(hs)
    chips = 2 ** len(order)
    part, unit = width // chips, fo // chips

    def body(*refs):
        info = refs[0]
        hr, gr = refs[1 : 1 + n], refs[1 + n : 1 + 2 * n]
        wu, wd, b, sm, bup, gqv, so, ko, h_v, g_v, wu_v, wd_v, act_v, gp_v, o_v, sm_v, sems = refs[1 + 2 * n :]
        mv = Mover(sems)
        cu = mv.go(wu.at[l], wu_v)
        ch = [mv.go(hr[i], h_v.at[pl.ds(i * rows, rows)]) for i in range(n)]
        if fast:
            cd = []
            for i in range(chips):
                at = pl.multiple_of((4 * i + info[3]) * unit, unit)
                cd.append(mv.go(wd.at[l, pl.ds(at, unit)], wd_v.at[pl.ds(i * unit, unit)]))
        else:
            cd = [mv.go(wd.at[l], wd_v)]
        cg = [mv.go(gr[i], g_v.at[pl.ds(i * rows, rows)]) for i in range(n)]
        cu.wait()
        for i in range(n):
            at = pl.ds(i * rows, rows)
            ch[i].wait()
            u = mm(h_v[at], wu_v[...]) + b[l].astype(f32)
            cdf, slope = phi_parts(u)
            act_v[at] = (u * cdf).astype(bf16)
            if i == 0:
                for k in cd:
                    k.wait()
            cg[i].wait()
            gp_v[at] = (mm(g_v[at], wd_v[...], NT) * slope).astype(bf16)
        up = mm(h_v[...], gp_v[...], TN).astype(bf16)
        if fast:
            for j in range(chips):
                o_v[place(j, info[1], order), :part] = up[j * part : (j + 1) * part]
        else:
            o_v[:width] = up
        down = mm(act_v[...], g_v[...], TN).astype(bf16)
        if fast:
            sm_v[...] = sm[...]
            sm_v[6:8, pl.ds(pl.multiple_of(info[0] * (width // 2), 128), width // 2)] = gqv[...]
            whole = sm_v[...]
            for j in range(chips):
                p = place(j, info[1], order)
                o_v[p, part : part + unit] = down[j * unit : (j + 1) * unit]
                o_v[p, part + unit :] = jnp.concatenate(
                    [
                        jnp.concatenate([whole[:, j * part : (j + 1) * part], jnp.zeros((8, width - part), f32)], 1),
                        jnp.concatenate([bup[:, 4 * j * unit : 4 * (j + 1) * unit], jnp.zeros((1, width - 4 * unit), f32)], 1),
                        jnp.zeros((7, width), f32),
                    ]
                ).astype(bf16)
            halfway = chips // 2
            out = [mv.go(o_v.at[pl.ds(halfway, halfway)], so), mv.go(o_v.at[pl.ds(0, halfway)], ko)]
        else:
            o_v[width:] = down
            out = [mv.go(o_v.at[pl.ds(0, width)], so), mv.go(o_v.at[pl.ds(width, fo)], ko)]
        for k in out:
            k.wait()

    S, V = jax.ShapeDtypeStruct, pltpu.VMEM
    tok = V((n * rows, width), bf16)
    hid = V((n * rows, fo), bf16)
    if fast:
        outs = (S((chips // 2, part + unit + 16, width), bf16),) * 2
        o_v = V((chips, part + unit + 16, width), bf16)
    else:
        outs = (S((width, fo), bf16), S((fo, width), bf16))
        o_v = V((width + fo, width), bf16)
    got = kernel_call(
        body, "ffn_grads", (info,) + tuple(hs) + tuple(gs) + (wu_own, w_down, b_own, small, gbup, gqv), [SM] + [ANY] * (2 * n) + [HBM, HBM] + [VM] * 4,
        outs, (ANY, ANY), [tok, tok, V((width, fo), bf16), V((fo, width), bf16), hid, hid, o_v, V((8, width), f32)],
        2 * n + 4 + chips, 8 * n * rows * width * fo, 8 << 20,
    )
    if fast:
        return got
    zero = jnp.zeros_like(gqv)
    gqv = jnp.where(info[0] == 0, jnp.concatenate([gqv, zero], 1), jnp.concatenate([zero, gqv], 1))
    small = jnp.concatenate([small[:6], gqv]).reshape(8, chips, part).transpose(1, 0, 2)
    small = jnp.concatenate([jnp.pad(small, ((0, 0), (0, 0), (0, width - part))),
                             jnp.pad(gbup.reshape(chips, 1, 4 * unit), ((0, 0), (0, 7), (0, width - 4 * unit)))], 1)
    both = jnp.concatenate([got[0].reshape(chips, part, fo), got[1].reshape(chips, unit, width), small.astype(bf16)], 1)
    both = arranged(both, info[1], order)
    return both[chips // 2 :], both[: chips // 2]


def proj_grads(info, xo, xt, ctx, got, go, gt, gproj, parts, fast):
    rows, width = xo.shape
    half = width // 2
    toks = 2 * rows
    chips = 2 ** len(parts[0][1])
    part = width // chips // 2

    def shapes(groups, row_first):
        cols = len(groups) * half
        return (2, chips, part, cols) if row_first else (2, chips // 2, 2, part, cols)

    def body(info, xo, xt, ctx, got, go, gt, gp, *refs):
        n = len(parts)
        outs, (x_v, gp_v, c_v, ga_v), o_vs, sems = refs[: 2 * n], refs[2 * n : 2 * n + 4], refs[2 * n + 4 : -1], refs[-1]
        mv = Mover(sems)
        c, me, y = info[0], info[1], info[2]
        top, low = pl.ds(0, rows), pl.ds(rows, rows)
        cols = pl.ds(pl.multiple_of(c * half, 128), half)
        cc = [mv.go(ctx, c_v.at[0]), mv.go(got.at[low], c_v.at[1, top]), mv.go(got.at[top], c_v.at[1, low]),
              mv.go(go.at[:, cols], ga_v.at[top]), mv.go(gt.at[:, cols], ga_v.at[low])]
        cx = [mv.go(xo, x_v.at[top]), mv.go(xt, x_v.at[low]), mv.go(gp, gp_v)]
        started = {"c": False, "x": False}

        def need(which, copies):
            if not started[which]:
                for k in copies:
                    k.wait()
                started[which] = True

        out = []
        for s, (groups, order, row_first) in enumerate(parts):
            for g, group in enumerate(groups):
                at = slice(g * half, (g + 1) * half)
                if group < 3:
                    need("x", cx)
                    blocks = [(0, mm(x_v[...], gp_v[:, group * half : (group + 1) * half], TN).astype(bf16))]
                else:
                    need("c", cc)
                    blocks = [((c if i == 0 else 1 - c) * (chips // 2), mm(c_v[i], ga_v[...], TN).astype(bf16)) for i in range(2)]
                for base, val in blocks:
                    for j in range(val.shape[0] // part):
                        piece = val[j * part : (j + 1) * part]
                        p = place(base + j // 2, me, order)
                        if row_first:
                            o_vs[s][jnp.bitwise_xor(j % 2, y), p, :, at] = piece
                        else:
                            o_vs[s][jnp.right_shift(p, len(order) - 1), jnp.bitwise_and(p, chips // 2 - 1), j % 2, :, at] = piece
            out += [mv.go(o_vs[s].at[1], outs[2 * s]), mv.go(o_vs[s].at[0], outs[2 * s + 1])]
        need("c", cc)
        need("x", cx)
        for k in out:
            k.wait()

    def slow(info, xo, xt, ctx, got, go, gt, gp, o_ref, x_v, gp_v, c_v, ga_v, o_v, sems):
        mv = Mover(sems)
        c = info[0]
        top, low = pl.ds(0, rows), pl.ds(rows, rows)
        cols = pl.ds(pl.multiple_of(c * half, 128), half)
        cc = [mv.go(ctx, c_v.at[0]), mv.go(got.at[low], c_v.at[1, top]), mv.go(got.at[top], c_v.at[1, low]),
              mv.go(go.at[:, cols], ga_v.at[top]), mv.go(gt.at[:, cols], ga_v.at[low]),
              mv.go(xo, x_v.at[top]), mv.go(xt, x_v.at[low]), mv.go(gp, gp_v)]
        for k in cc:
            k.wait()
        o_v[:, : 3 * half] = mm(x_v[...], gp_v[...], TN).astype(bf16)
        for i in range(2):
            who = c if i == 0 else 1 - c
            o_v[pl.ds(pl.multiple_of(who * half, 128), half), 3 * half :] = mm(c_v[i], ga_v[...], TN).astype(bf16)
        mv.go(o_v, o_ref).wait()

    S, V = jax.ShapeDtypeStruct, pltpu.VMEM
    scratch = [V((toks, width), bf16), V((toks, 3 * half), bf16), V((2, toks, half), bf16), V((toks, half), bf16)]
    args = (info, xo, xt, ctx, got, go, gt, gproj)
    specs = [SM] + [ANY] * 7
    flops = 2 * toks * width * 4 * half
    if fast:
        full = [shapes(groups, row_first) for groups, _, row_first in parts]
        outs = tuple(S(f[1:], bf16) for f in full for _ in range(2))
        res = kernel_call(body, "proj_grads", args, specs, outs, (ANY,) * len(outs), scratch + [V(f, bf16) for f in full], 8 + len(outs), flops, 6 << 20)
        return [(res[2 * s], res[2 * s + 1]) for s in range(len(parts))]
    res = kernel_call(slow, "proj_grads", args, specs, S((width, 4 * half), bf16), ANY, scratch + [V((width, 4 * half), bf16)], 9, flops, 6 << 20)
    out = []
    for groups, order, row_first in parts:
        v = jnp.concatenate([res[:, g * half : (g + 1) * half] for g in groups], 1)
        v = arranged(v.reshape(chips, 2, part, -1), info[1], order)
        if row_first:
            v = v.transpose(1, 0, 2, 3)
            v = jnp.where(info[2] == 1, jnp.flip(v, 0), v)
            out.append((v[1], v[0]))
        else:
            out.append((v[chips // 2 :], v[: chips // 2]))
    return out


class Wires:
    def __init__(self, batch, seq):
        self.batch, self.seq = batch, seq
        self.chips = batch // 2
        self.bits = self.chips.bit_length() - 1
        where = [(i, j) for i in range(batch) for j in range(seq)]

        def table(move):
            out = []
            for i, j in where:
                p, q = move(i, j)
                out.append((i * seq + j, p * seq + q))
            return out

        self.core = table(lambda i, j: (i ^ 1, j))
        self.row = table(lambda i, j: (i, 1 - j))
        self.turn = table(lambda i, j: (i - i % 2 + j, i % 2))
        self.chip = [table(lambda i, j, k=k: (i ^ (2 << k), j)) for k in range(self.bits)]
        self.b = lax.axis_index("batch")
        self.y = lax.axis_index("seq")
        self.c = self.b % 2

    def swap_core(self, v):
        return lax.ppermute(v, AXES, self.core)

    def swap_row(self, v):
        return lax.ppermute(v, AXES, self.row)

    def swap_turn(self, v):
        return lax.ppermute(v, AXES, self.turn)

    def swap_chip(self, v, k):
        return lax.ppermute(v, AXES, self.chip[k])

    def bit(self, k):
        return (self.b >> (k + 1)) & 1


def pick(v, idx, axis):
    return lax.dynamic_index_in_dim(v, idx, axis, keepdims=False)


def add(a, b):
    return a.astype(f32) + b.astype(f32)


def order_two(flag, mine, got, axis):
    return jnp.stack([jnp.where(flag == 0, mine, got), jnp.where(flag == 0, got, mine)], axis)


class Clock:
    def __init__(self):
        self.now, self.free, self.alive = 0.0, {}, []

    def busy(self, link, us):
        begin = max(self.now, self.free.get(link, 0.0))
        self.free[link] = begin + us
        return begin + us

    def work(self, us):
        self.now += us

    def catch_up(self):
        for s in sorted(self.alive, key=lambda s: s.ready):
            if s.ready <= self.now:
                s.step()

    def drain(self):
        while self.alive:
            min(self.alive, key=lambda s: s.ready).step()


class Stream:
    def __init__(self, wires, clock, send, keep, order, row_first):
        self.wires, self.clock, self.keep, self.row_first = wires, clock, keep, row_first
        self.todo = list(order)
        clock.alive.append(self)
        self.send(send, row_first)

    def send(self, v, row=False):
        us = v.size * 2 / 1e6 * 22.0
        if row:
            self.got, link = self.wires.swap_row(v), "y"
        else:
            k = self.todo.pop(0)
            self.got = self.wires.swap_chip(v, k)
            link = "x" if k == 0 else "z"
            us *= max(1, 1 << (k - 1)) if k else 1
        self.clock.work(1.4)
        self.ready = self.clock.busy(link, us) + 2.0

    def step(self):
        clock = self.clock
        clock.now = max(clock.now, self.ready)
        clock.work(1.2 + self.keep.size * 2 / 1e6)
        shape = self.keep.shape
        flat = (shape[0], -1, shape[-1])
        out = merge(self.keep.reshape(flat), self.got.reshape(flat))
        if not self.todo:
            self.sum = out[0].reshape(shape[1:])
            clock.alive.remove(self)
            return
        send, self.keep = (v.reshape((shape[0] // 2,) + shape[1:]) for v in out)
        self.send(send)


def finish_proj(wires, v, row_first):
    if row_first:
        v = order_two(wires.y, v, wires.swap_row(v), 0)
    else:
        v = add(v, wires.swap_row(v)).astype(bf16)
    got = wires.swap_core(pick(v, 1 - wires.c, 0))
    return order_two(wires.c, pick(v, wires.c, 0), got, 1).astype(f32)


def finish_ffn(wires, v, part, unit):
    width = v.shape[1]
    other = wires.swap_row(v)
    both = order_two(wires.y, v, other, 0)
    down = both[:, part : part + unit].reshape(-1, width).astype(f32)
    small = add(v[part + unit :], other[part + unit :]).astype(bf16)
    up = both[:, :part].reshape(2, 2, part // 2, width)
    got = wires.swap_core(jnp.concatenate([pick(up, 1 - wires.c, 1).reshape(part, width), small]))
    small = add(small, got[part:])
    up = order_two(wires.c, pick(up, wires.c, 1), got[:part].reshape(2, part // 2, width), 0)
    up = up.reshape(2, 2, part // 2, wires.chips, unit)
    up = up.transpose(2, 3, 0, 1, 4).reshape(part // 2, 4 * width).astype(f32)
    vecs = pick(small[:8, :part].reshape(8, 2, part // 2), wires.c, 1)
    return up, down, vecs, pick(small[8, : 4 * unit].reshape(2, 2 * unit), wires.c, 0)


def local(inputs, out_grad, masked, w_qkv, bias_qv, w_out, bias_out, gain_one, shift_one, w_up, bias_up, w_down, bias_down, gain_two, shift_two):
    wires = Wires(lax.axis_size("batch"), lax.axis_size("seq"))
    layers, width, ff = w_up.shape
    half = width // 2
    chips, bits = wires.chips, wires.bits
    fo, unit, part = ff // 4, ff // chips // 4, width // chips
    fast = part % 32 == 0
    share = wires.c * 2 + wires.y
    info = jnp.stack([wires.c, wires.b // 2, wires.y, share]).astype(jnp.int32)
    rows = inputs.shape[1]
    ROW.extra = []
    xb = wires.swap_turn(inputs[0])
    b_own = pick(bias_up.reshape(layers, chips, 4, unit), share, 2).reshape(layers, 1, fo)
    if fast:
        wu_own, wd_own = own_units(info, w_up, chips), w_down
    else:
        wu_own = pick(w_up.reshape(layers, width, chips, 4, unit), share, 3).reshape(layers, width, fo)
        wd_own = pick(w_down.reshape(layers, chips, 4, unit, width), share, 2).reshape(layers, fo, width)
    gy = wires.swap_turn((out_grad * masked.astype(bf16)[..., None])[0])
    x = xb.astype(f32)
    saved, outs, hs = [], [], []
    tail = (w_out, bias_out, gain_one, shift_one, w_up, bias_up, w_down, bias_down, gain_two, shift_two)
    clock = Clock()
    for l in range(layers):
        xt = wires.swap_core(xb)
        qkv, pt, ctx = attn_fwd(info, l, xb, xt, w_qkv, bias_qv)
        if l == 0:
            ROW.before_next(gy)
        else:
            ROW.before_next(*hs[-1], outs[-1])
        got = wires.swap_core(ctx)
        hb, dg, mixed, summed, x, yb = ffn_fwd(info, l, x, ctx, got, tail)
        hy = wires.swap_row(hb)
        hs.append((hb, hy, wires.swap_core(hb), wires.swap_core(hy)))
        saved.append((xb, xt, qkv, pt, ctx, got, dg, mixed, summed))
        outs.append(wires.swap_turn(yb)[None])
        xb = yb
    low = list(range(bits))
    turned = low[1:2] + low[:1] + low[2:]
    plan = [
        (turned, [((0, 1, 2, 3), low, True)]),
    ] + [(turned, [((0, 1, 2, 3), low, True)])] * (layers - 1)
    streams = [None] * layers
    flow = (gy,)
    for l in reversed(range(layers)):
        xb, xt, qkv, pt, ctx, got, dg, mixed, summed = saved[l]
        gf, ga, gm, small, gbup = ffn_bwd(info, l, flow, summed, mixed, dg, (w_up, w_down, gain_one, gain_two))
        if l == layers - 1:
            ROW.before_next(*hs[-1], outs[-1])
        gat = wires.swap_core(ga)
        gfy = wires.swap_row(gf)
        gs = (gf, gfy, wires.swap_core(gf), wires.swap_core(gfy))
        gproj, gqv = attn_bwd(info, l, ga, gat, w_out, qkv, pt)
        flow = (gm, gproj, wires.swap_core(gproj[rows:]), w_qkv)
        clock.work(30.0 if l < layers - 1 else 0.0)
        clock.catch_up()
        res = proj_grads(info, xb, xt, ctx, got, ga, gat, gproj, plan[l][1], fast)
        clock.work(6.2)
        ps = [Stream(wires, clock, s, k, p[1], p[2]) for (s, k), p in zip(res, plan[l][1])]
        clock.catch_up()
        s, k = ffn_grads(info, l, hs[l], gs, wu_own, wd_own, b_own, small, gbup, gqv, plan[l][0], fast)
        clock.work(11.5)
        fs = Stream(wires, clock, s, k, plan[l][0], False)
        clock.catch_up()
        streams[l] = (fs, ps)
    end = chain_end(info, 0, flow)
    clock.work(5.5)
    grad_in = wires.swap_turn(end)[None]
    clock.drain()
    bigs = []
    half2 = part // 2
    for l in range(layers):
        fs, ps = streams[l]
        up, down, vecs, bup = finish_ffn(wires, fs.sum, part, unit)
        pieces = {}
        for s, (groups, _, row_first) in zip(ps, plan[l][1]):
            v = finish_proj(wires, s.sum, row_first)
            for i, g in enumerate(groups):
                pieces[g] = v[:, :, i * half : (i + 1) * half].reshape(half2, width)
        bigs.append((jnp.concatenate([pieces[g] for g in range(3)], 1), pieces[3], up, down, vecs, bup))
    qkv, out, up, down, vecs, bup = (jnp.stack([g[i] for g in bigs]) for i in range(6))
    gdn, gg2, gs2, gg1, gs1, gbo = (vecs[:, i] for i in range(6))
    return (outs[0], outs[-1], grad_in, qkv, vecs[:, 6:8], out, gbo, gg1, gs1, up, bup, down, gdn, gg2, gs2)


def solution(mesh):
    tok = P("batch", "seq", None)
    in_specs = (tok, tok, P("batch", "seq")) + (P(),) * 12
    mat, vec = P(None, "batch", None), P(None, "batch")
    out_specs = (tok, tok, tok, mat, P(None, None, "batch"), mat, vec, vec, vec, mat, vec, mat, vec, vec, vec)
    return jax.shard_map(local, mesh=mesh, in_specs=in_specs, out_specs=out_specs, check_vma=False)
```

```python
import math

import jax
import jax.numpy as jnp
from jax import lax
from jax.experimental import pallas as pl
from jax.experimental.pallas import tpu as pltpu
from jax.sharding import PartitionSpec as P

HEAD_DIM = 64
AXES = ("batch", "seq")
norm_eps = 1e-06
f32 = jnp.float32
bf16 = jnp.bfloat16
ANY = pl.BlockSpec(memory_space=pl.ANY)
HBM = pl.BlockSpec(memory_space=pltpu.HBM)
VM = pl.BlockSpec(memory_space=pltpu.VMEM)
SM = pl.BlockSpec(memory_space=pltpu.SMEM)
ROOT_HALF = 0.7071067811865476
INV_ROOT_TAU = 0.3989422804014327
TAKES = {"own_units": 24.0, "attn_fwd": 7.5, "ffn_fwd": 9.0, "ffn_turn": 13.0, "ffn_bwd": 12.0, "attn_bwd": 7.5, "ffn_grads": 10.5, "proj_grads": 18, "chain_end": 4.5, "merge": 7.0, "pack": 3.0, "unpack": 5.0}
PACE = 0.5


def mm(a, b, dims=((1,), (0,))):
    return lax.dot_general(a, b, (dims, ((), ())), preferred_element_type=f32)


NT = ((1,), (1,))
TN = ((0,), (0,))


class Mover:
    def __init__(self, sems):
        self.sems, self.used = sems, 0

    def go(self, src, dst):
        copy = pltpu.make_async_copy(src, dst, self.sems.at[self.used])
        self.used += 1
        copy.start()
        return copy


class Row:
    def __init__(self):
        self.extra = []

    def before_next(self, *values):
        self.extra.extend(values)


ROW = Row()


def kernel_call(body, name, args, specs, outs, out_specs, scratch, sems, flops, moved):
    extra = tuple(ROW.extra)
    n, m = len(args), len(args) + len(extra)
    held = sum(math.prod(v.shape) * jnp.dtype(v.dtype).itemsize for v in scratch)
    limit = held + ((2 << 20) if name == "merge" else (12 << 20))
    args = tuple(
        pltpu.with_memory_space_constraint(a, pltpu.HBM) if spec is HBM else a for a, spec in zip(args, specs)
    )
    out = pl.pallas_call(
        lambda *refs: body(*refs[:n], *refs[m:]),
        name=name,
        out_shape=outs,
        in_specs=specs + [ANY] * len(extra),
        out_specs=out_specs,
        scratch_shapes=list(scratch) + [pltpu.SemaphoreType.DMA((sems,))],
        compiler_params=pltpu.CompilerParams(vmem_limit_bytes=limit),
        cost_estimate=pl.CostEstimate(flops=int(PACE * TAKES[name] * 1.15e9), bytes_accessed=moved, transcendentals=0),
    )(*args, *extra)
    ROW.extra = [out[0] if isinstance(out, (tuple, list)) else out]
    return out


def merge(keep, got):
    n = max(keep.shape[0] // 2, 1)
    rest = keep.shape[1:]
    parts = keep.shape[0] // n

    def body(k, g, *refs):
        outs, (k_v, g_v, sems) = refs[:parts], refs[parts:]
        mv = Mover(sems)
        at = [pl.ds((parts - 1 - i) * n, n) for i in range(parts)]
        come = [(mv.go(k.at[a], k_v.at[a]), mv.go(g.at[a], g_v.at[a])) for a in at]
        gone = []
        for i, a in enumerate(at):
            for c in come[i]:
                c.wait()

            def one(j, _):
                j = j + (parts - 1 - i) * n
                k_v[j] = (k_v[j].astype(f32) + g_v[j].astype(f32)).astype(bf16)
                return 0

            lax.fori_loop(0, n, one, 0)
            gone.append(mv.go(k_v.at[a], outs[i]))
        for c in gone:
            c.wait()

    outs = (jax.ShapeDtypeStruct((n,) + rest, bf16),) * parts
    return kernel_call(body, "merge", (keep, got), [ANY, ANY], outs, (ANY,) * parts, [pltpu.VMEM(keep.shape, bf16)] * 2, 3 * parts, 5 * 10**9, 0)


def normed(z):
    center = z - jnp.mean(z, -1, keepdims=True)
    rstd = lax.rsqrt(jnp.mean(center * center, -1, keepdims=True) + norm_eps)
    return center * rstd, rstd


def norm_back(g, z, gain):
    xhat, rstd = normed(z)
    gx = g * gain
    m1 = jnp.mean(gx, -1, keepdims=True)
    m2 = jnp.mean(gx * xhat, -1, keepdims=True)
    return rstd * (gx - m1 - xhat * m2), g * xhat


def phi_parts(u):
    cdf = 0.5 * (1.0 + lax.erf(u * ROOT_HALF))
    return cdf, cdf + u * (jnp.exp(-0.5 * u * u) * INV_ROOT_TAU)


def attn_fwd(info, l, xo, xt, w_qkv, bias_qv):
    rows, width = xo.shape
    half = width // 2
    heads = half // HEAD_DIM
    toks = 2 * rows

    def body(info, xo, xt, w, bias, qkv_o, pt_o, ctx_o, x_v, w_v, qkv_v, pt_v, ctx_v, sems):
        mv = Mover(sems)
        c = info[0]
        cx = [mv.go(xo, x_v.at[pl.ds(0, rows)]), mv.go(xt, x_v.at[pl.ds(rows, rows)])]
        cw = []
        for p in range(3):
            at = pl.multiple_of(p * width + c * half, 128)
            cw.append(mv.go(w.at[l, :, pl.ds(at, half)], w_v.at[p]))
        for k in cx:
            k.wait()
        at = pl.multiple_of(c * half, 128)
        for p in range(3):
            cw[p].wait()
            val = mm(x_v[...], w_v[p])
            if p != 1:
                val = val + bias[l, pl.ds(p // 2, 1), pl.ds(at, half)].astype(f32)
            val = val.astype(bf16)
            if p == 0:
                val = (val.astype(f32) * HEAD_DIM ** (-0.5)).astype(bf16)
            qkv_v[:, p * half : (p + 1) * half] = val
        out = [mv.go(qkv_v, qkv_o)]
        lane = lax.broadcasted_iota(jnp.int32, (toks, 2 * HEAD_DIM), 1) < HEAD_DIM

        for i in range(heads // 2):
            at = i * 2 * HEAD_DIM
            q = qkv_v[:, at : at + 128]
            k = qkv_v[:, half + at : half + at + 128]
            v = qkv_v[:, 2 * half + at : 2 * half + at + 128]
            both = []
            for h in range(2):
                qm = jnp.where(lane == (h == 0), q, jnp.zeros_like(q))
                st = mm(k, qm, NT)
                top = jnp.max(st, 0, keepdims=True)
                e = jnp.exp(st - top)
                p = (e / jnp.sum(e, 0, keepdims=True)).astype(bf16)
                pt_v[2 * i + h] = p
                both.append(mm(p, v, TN))
            ctx_v[:, at : at + 128] = jnp.where(lane, both[0], both[1]).astype(bf16)
            now = pl.ds(2 * i, 2)
            out.append(mv.go(pt_v.at[now], pt_o.at[now]))
        out.append(mv.go(ctx_v, ctx_o))
        for k in out:
            k.wait()

    S = jax.ShapeDtypeStruct
    outs = (pltpu.HBM((toks, 3 * half), bf16), pltpu.HBM((heads, toks, toks), bf16), S((toks, half), bf16))
    return kernel_call(
        body, "attn_fwd", (info, xo, xt, w_qkv, bias_qv), [SM, ANY, ANY, HBM, VM], outs, (ANY,) * 3,
        [pltpu.VMEM((toks, width), bf16), pltpu.VMEM((3, width, half), bf16), pltpu.VMEM((toks, 3 * half), bf16),
         pltpu.VMEM((heads, toks, toks), bf16), pltpu.VMEM((toks, half), bf16)],
        8 + heads // 2, 2 * toks * width * 3 * half + 8 * heads * toks * toks * 128, 8 << 20,
    )


def ffn_fwd(info, l, x, ctx, got, weights, gy=None, cut=6):
    w_out, bias_out, gain_one, shift_one, w_up, bias_up, w_down, bias_down, gain_two, shift_two = weights
    rows, width = x.shape
    half = width // 2
    ff = w_up.shape[2]
    step = ff // cut
    turn = gy is not None

    def body(info, x, ctx, got, wo, bo, g1, s1, wu, bu, wd, bd, g2, s2, *refs):
        if turn:
            gy_r, yb_o, pair_o, ga_o, gm_o, small_o, gbup_o = refs[:7]
            x_v, c_v, wo_v, wu_v, wd_v, hb_v, dg_v, mixed_v, yb_v, low_v, gf_v, gm_v, sems = refs[7:]
        else:
            hb_o, dg_o, mixed_o, summed_o, yb_o = refs[:5]
            x_v, c_v, wo_v, wu_v, wd_v, hb_v, dg_v, mixed_v, yb_v, sems = refs[5:]
        mv = Mover(sems)
        c = info[0]
        cx = mv.go(x, hb_v if l == 0 else x_v)
        first = [mv.go(ctx.at[pl.ds(0, rows)], c_v.at[0])]
        at = [pl.multiple_of(c * half, 128), pl.multiple_of((1 - c) * half, 128)]
        first += [mv.go(wo.at[l, pl.ds(at[i], half)], wo_v.at[i]) for i in range(2)]
        first += [mv.go(got.at[pl.ds(rows, rows)], c_v.at[1])]
        cu, cd = [], []
        for j in range(cut):
            cu.append(mv.go(wu.at[l, :, pl.ds(j * step, step)], wu_v.at[j]))
            cd.append(mv.go(wd.at[l, pl.ds(j * step, step)], wd_v.at[j]))
        if turn:
            cg = mv.go(gy_r, low_v)
        cx.wait()
        if l == 0:
            xin = hb_v[...].astype(f32)
        else:
            xin = normed(x_v[...])[0] * g2[l - 1 : l].astype(f32) + s2[l - 1 : l].astype(f32)
        for k in first:
            k.wait()
        mixed = xin + mm(c_v[0], wo_v[0]) + mm(c_v[1], wo_v[1]) + bo[l : l + 1].astype(f32)
        mixed_v[...] = mixed
        out = [] if turn else [mv.go(mixed_v, mixed_o)]
        hid = normed(mixed)[0] * g1[l : l + 1].astype(f32) + s1[l : l + 1].astype(f32)
        x_v[...] = hid
        hb_v[...] = hid.astype(bf16)
        out.append(mv.go(hb_v, pair_o.at[0] if turn else hb_o))
        acc = None
        for j in range(cut):
            cols = slice(j * step, (j + 1) * step)
            cu[j].wait()
            u = mm(hb_v[...], wu_v[j]) + bu[l : l + 1, cols].astype(f32)
            cdf, slope = phi_parts(u)
            dg_v[j] = slope.astype(dg_v.dtype)
            if not turn:
                out.append(mv.go(dg_v.at[j], dg_o.at[:, pl.ds(j * step, step)]))
            cd[j].wait()
            part = mm((u * cdf).astype(bf16), wd_v[j])
            acc = part if acc is None else acc + part
        summed = x_v[...] + acc + bd[l : l + 1].astype(f32)
        x_v[...] = summed
        if not turn:
            out.append(mv.go(x_v, summed_o))
        gain = g2[l : l + 1].astype(f32)
        y = normed(summed)[0] * gain + s2[l : l + 1].astype(f32)
        yb_v[...] = y.astype(bf16)
        out.append(mv.go(yb_v, yb_o))
        if turn:
            cg.wait()
            gy = low_v[...].astype(f32)
            gsum, gterm = norm_back(gy, x_v[...], gain)
            small_o[1:2] = jnp.sum(gterm, 0, keepdims=True)
            small_o[2:3] = jnp.sum(gy, 0, keepdims=True)
            gf = gsum.astype(bf16)
            gf_v[...] = gf
            small_o[0:1] = jnp.sum(gf.astype(f32), 0, keepdims=True)
            out.append(mv.go(gf_v, pair_o.at[1]))
            gm_v[...] = gsum
            acc = None
            for j in range(cut):
                gpre = (mm(gf_v[...], wd_v[j], NT) * dg_v[j].astype(f32)).astype(bf16)
                gbup_o[:, j * step : (j + 1) * step] = jnp.sum(gpre.astype(f32), 0, keepdims=True)
                part = mm(gpre, wu_v[j], NT)
                acc = part if acc is None else acc + part
            ghid = gm_v[...] + acc
            gmix, gterm = norm_back(ghid, mixed_v[...], g1[l : l + 1].astype(f32))
            ga = gmix.astype(bf16)
            low_v[...] = ga
            out.append(mv.go(low_v, ga_o))
            gm_v[...] = gmix
            out.append(mv.go(gm_v, gm_o))
            small_o[3:4] = jnp.sum(gterm, 0, keepdims=True)
            small_o[4:5] = jnp.sum(ghid, 0, keepdims=True)
            small_o[5:6] = jnp.sum(ga.astype(f32), 0, keepdims=True)
            small_o[6:8] = jnp.zeros((2, width), f32)
        for k in out:
            k.wait()

    S, V = jax.ShapeDtypeStruct, pltpu.VMEM
    full, low = S((rows, width), f32), S((rows, width), bf16)
    scratch = [V((rows, width), f32), V((2, rows, half), bf16), V((2, half, width), bf16), V((cut, width, step), bf16),
               V((cut, step, width), bf16), V((rows, width), bf16), V((cut, rows, step), bf16), V((rows, width), f32),
               V((rows, width), bf16)]
    args = (info, x, ctx, got, w_out, bias_out, gain_one, shift_one, w_up, bias_up, w_down, bias_down, gain_two, shift_two)
    specs = [SM, ANY, ANY, ANY, HBM, VM, VM, VM, HBM, VM, HBM, VM, VM, VM]
    if turn:
        outs = (low, S((2, rows, width), bf16), low, full, S((8, width), f32), S((1, ff), f32))
        out_specs = (ANY, ANY, ANY, ANY, VM, VM)
        scratch += [V((rows, width), bf16), V((rows, width), bf16), V((rows, width), f32)]
        args, specs = args + (gy,), specs + [ANY]
    else:
        outs, out_specs = (low, pltpu.HBM((rows, ff), bf16), pltpu.HBM((rows, width), f32), full, low), (ANY,) * 5
    return kernel_call(
        body, "ffn_turn" if turn else "ffn_fwd", args, specs, outs, out_specs, scratch, 14 + 3 * cut, 0, 12 << 20,
    )


def ffn_bwd(info, l, flow, summed, mixed, dg, weights, cut=6):
    w_up, w_down, gain_one, gain_two = weights
    rows, width = summed.shape
    half = width // 2
    ff = w_up.shape[2]
    step = ff // cut
    chained = len(flow) > 1

    def body(*refs):
        info = refs[0]
        fl = refs[1 : 1 + len(flow)]
        (sm, mi, dgr, wu, wd, g1, g2, gf_o, ga_o, gm_o, small_o, gbup_o,
         gy_v, sm_v, mi_v, dg_v, wu_v, wd_v, gf_v, ga_v, gm_v) = refs[1 + len(flow) : 22 + len(flow)]
        sems = refs[-1]
        mv = Mover(sems)
        if chained:
            gp_v, wq_v = refs[22 + len(flow) : 24 + len(flow)]
            c = info[0]
            fc = [mv.go(fl[0], gy_v), mv.go(fl[1].at[pl.ds(0, rows)], gp_v.at[0])]
            wq = []
            for i in range(2):
                who = c if i == 0 else 1 - c
                for p in range(3):
                    at = pl.multiple_of(p * width + who * half, 128)
                    wq.append(mv.go(fl[3].at[l + 1, :, pl.ds(at, half)], wq_v.at[i, p]))
            fc.append(mv.go(fl[2], gp_v.at[1]))
        else:
            fc = [mv.go(fl[0], gf_v)]
        fc += [mv.go(sm, sm_v)]
        cd, cu, cg = [], [], []
        for j in range(cut):
            cols = pl.ds(j * step, step)
            cd.append(mv.go(wd.at[l, cols], wd_v.at[j]))
            cg.append(mv.go(dgr.at[:, cols], dg_v.at[j]))
            cu.append(mv.go(wu.at[l, :, cols], wu_v.at[j]))
        cm = mv.go(mi, mi_v)
        for k in fc:
            k.wait()
        if chained:
            gy = gy_v[...]
            for i in range(2):
                for p in range(3):
                    wq[3 * i + p].wait()
                    gy = gy + mm(gp_v[i, :, p * half : (p + 1) * half], wq_v[i, p], NT)
        else:
            gy = gf_v[...].astype(f32)
        gsum, gterm = norm_back(gy, sm_v[...], g2[pl.ds(l, 1)].astype(f32))
        small_o[1:2] = jnp.sum(gterm, 0, keepdims=True)
        small_o[2:3] = jnp.sum(gy, 0, keepdims=True)
        gf = gsum.astype(bf16)
        gf_v[...] = gf
        small_o[0:1] = jnp.sum(gf.astype(f32), 0, keepdims=True)
        out = [mv.go(gf_v, gf_o)]
        gm_v[...] = gsum
        acc = None
        for j in range(cut):
            cd[j].wait()
            cg[j].wait()
            gpre = (mm(gf_v[...], wd_v[j], NT) * dg_v[j].astype(f32)).astype(bf16)
            gbup_o[:, j * step : (j + 1) * step] = jnp.sum(gpre.astype(f32), 0, keepdims=True)
            cu[j].wait()
            part = mm(gpre, wu_v[j], NT)
            acc = part if acc is None else acc + part
        ghid = gm_v[...] + acc
        cm.wait()
        gmix, gterm = norm_back(ghid, mi_v[...], g1[pl.ds(l, 1)].astype(f32))
        ga = gmix.astype(bf16)
        ga_v[...] = ga
        out.append(mv.go(ga_v, ga_o))
        gm_v[...] = gmix
        out.append(mv.go(gm_v, gm_o))
        small_o[3:4] = jnp.sum(gterm, 0, keepdims=True)
        small_o[4:5] = jnp.sum(ghid, 0, keepdims=True)
        small_o[5:6] = jnp.sum(ga.astype(f32), 0, keepdims=True)
        small_o[6:8] = jnp.zeros((2, width), f32)
        for k in out:
            k.wait()

    S, V = jax.ShapeDtypeStruct, pltpu.VMEM
    low = S((rows, width), bf16)
    outs = (low, low, S((rows, width), f32), S((8, width), f32), S((1, ff), f32))
    scratch = [V((rows, width), f32), V((rows, width), f32), V((rows, width), f32), V((cut, rows, step), bf16),
               V((cut, width, step), bf16), V((cut, step, width), bf16), V((rows, width), bf16), V((rows, width), bf16),
               V((rows, width), f32)]
    if chained:
        scratch += [V((2, rows, 3 * half), bf16), V((2, 3, width, half), bf16)]
    return kernel_call(
        body, "ffn_bwd", (info,) + tuple(flow) + (summed, mixed, dg, w_up, w_down, gain_one, gain_two),
        [SM] + [ANY, ANY, ANY, HBM][: len(flow)] + [ANY, HBM, HBM, HBM, HBM, VM, VM], outs, (ANY, ANY, ANY, VM, VM), scratch,
        15 + 3 * cut, 2 * rows * width * (2 * ff + (3 * width if chained else 0)), 15 << 20,
    )


def chain_end(info, l, flow):
    gmix, gproj, got, w_qkv = flow
    rows, width = gmix.shape
    half = width // 2

    def body(info, gm, gp, gt, w, o_ref, gy_v, gp_v, wq_v, o_v, sems):
        mv = Mover(sems)
        c = info[0]
        wq = []
        fc = [mv.go(gm, gy_v), mv.go(gp.at[pl.ds(0, rows)], gp_v.at[0]), mv.go(gt, gp_v.at[1])]
        for i in range(2):
            who = c if i == 0 else 1 - c
            for p in range(3):
                at = pl.multiple_of(p * width + who * half, 128)
                wq.append(mv.go(w.at[l, :, pl.ds(at, half)], wq_v.at[i, p]))
        for k in fc:
            k.wait()
        gy = gy_v[...]
        for i in range(2):
            for p in range(3):
                wq[3 * i + p].wait()
                gy = gy + mm(gp_v[i, :, p * half : (p + 1) * half], wq_v[i, p], NT)
        o_v[...] = gy.astype(bf16)
        k = mv.go(o_v, o_ref)
        k.wait()

    S, V = jax.ShapeDtypeStruct, pltpu.VMEM
    return kernel_call(
        body, "chain_end", (info,) + tuple(flow), [SM, ANY, ANY, ANY, HBM], S((rows, width), bf16), ANY,
        [V((rows, width), f32), V((2, rows, 3 * half), bf16), V((2, 3, width, half), bf16), V((rows, width), bf16)],
        10, 2 * rows * width * 3 * width, 5 << 20,
    )


def attn_bwd(info, l, go, gt, w_out, qkv, pt):
    rows, width = go.shape
    half = width // 2
    heads = half // HEAD_DIM
    toks = 2 * rows

    def body(info, go, gt, wo, qkv, pt, gp_o, gt_o, gb_o, ga_v, wo_v, qkv_v, pt_v, gc_v, gp_v, sems):
        mv = Mover(sems)
        c = info[0]
        at = pl.multiple_of(c * half, 128)
        fc = [mv.go(wo.at[l, pl.ds(at, half)], wo_v), mv.go(go, ga_v.at[pl.ds(0, rows)]), mv.go(gt, ga_v.at[pl.ds(rows, rows)])]
        cq = mv.go(qkv, qkv_v)
        cp = [mv.go(pt.at[pl.ds(2 * i, 2)], pt_v.at[pl.ds(2 * i, 2)]) for i in range(heads // 2)]
        for k in fc:
            k.wait()
        gc_v[...] = mm(ga_v[...], wo_v[...], NT).astype(bf16)
        cq.wait()
        lane = lax.broadcasted_iota(jnp.int32, (toks, 2 * HEAD_DIM), 1) < HEAD_DIM

        for i in range(heads // 2):
            cp[i].wait()
            at = i * 2 * HEAD_DIM
            at_k, at_v = half + at, 2 * half + at
            q = qkv_v[:, pl.ds(at, 128)]
            k = qkv_v[:, pl.ds(at_k, 128)]
            v = qkv_v[:, pl.ds(at_v, 128)]
            gc = gc_v[:, pl.ds(at, 128)]
            res = []
            for h in range(2):
                gm = jnp.where(lane == (h == 0), gc, jnp.zeros_like(gc))
                pb = pt_v[2 * i + h]
                t = mm(v, gm, NT)
                p = pb.astype(f32)
                inner = jnp.sum(p * t, 0, keepdims=True)
                gs = (p * (t - inner)).astype(bf16)
                res.append((mm(gs, k, TN), mm(gs, q), mm(pb, gc)))
            gq = jnp.where(lane, res[0][0], res[1][0]) * HEAD_DIM ** (-0.5)
            gk = jnp.where(lane, res[0][1], res[1][1])
            gv = jnp.where(lane, res[0][2], res[1][2])
            gq, gk, gv = gq.astype(bf16), gk.astype(bf16), gv.astype(bf16)
            gp_v[:, pl.ds(at, 128)] = gq
            gp_v[:, pl.ds(at_k, 128)] = gk
            gp_v[:, pl.ds(at_v, 128)] = gv
            gb_o[0:1, pl.ds(at, 128)] = jnp.sum(gq.astype(f32), 0, keepdims=True)
            gb_o[1:2, pl.ds(at, 128)] = jnp.sum(gv.astype(f32), 0, keepdims=True)
        low = pl.ds(rows, rows)
        for k in [mv.go(gp_v, gp_o), mv.go(gp_v.at[low], gt_o)]:
            k.wait()

    S, V = jax.ShapeDtypeStruct, pltpu.VMEM
    return kernel_call(
        body, "attn_bwd", (info, go, gt, w_out, qkv, pt), [SM, ANY, ANY, HBM, HBM, HBM],
        (S((toks, 3 * half), bf16), S((rows, 3 * half), bf16), S((2, half), f32)), (ANY, ANY, VM),
        [V((toks, width), bf16), V((half, width), bf16), V((toks, 3 * half), bf16), V((heads, toks, toks), bf16),
         V((toks, half), bf16), V((toks, 3 * half), bf16)],
        8 + heads, 2 * toks * width * half + 20 * heads * toks * toks * 128, 7 << 20,
    )


def place(j, me, order):
    d = jnp.bitwise_xor(j, me)
    n = len(order)
    p = 0
    for i, k in enumerate(order):
        p = p + (jnp.bitwise_and(jnp.right_shift(d, k), 1) << (n - 1 - i))
    return p


def arranged(v, me, order):
    n = len(order)
    rest = v.shape[1:]
    v = v.reshape((2,) * n + rest)
    for k in range(n):
        ax = n - 1 - k
        v = jnp.where(((me >> k) & 1) == 1, jnp.flip(v, ax), v)
    v = v.transpose([n - 1 - k for k in order] + list(range(n, n + len(rest))))
    return v.reshape((2**n,) + rest)


def own_units(info, l, w_up, chips):
    _, width, ff = w_up.shape
    part = ff // chips // 4
    fo = ff // 4
    strip = 128

    def body(info, w, o_ref, w_v, o_v, sems):
        mv = Mover(sems)
        mv.go(w.at[l], w_v).wait()
        for s in range(4):

            @pl.when(info[3] == s)
            def _():
                def some(r, _):
                    at = pl.ds(pl.multiple_of(r * strip, strip), strip)
                    for i in range(chips):
                        o_v[at, i * part : (i + 1) * part] = w_v[at, (4 * i + s) * part : (4 * i + s + 1) * part]
                    return 0

                lax.fori_loop(0, width // strip, some, 0)

        mv.go(o_v, o_ref).wait()

    S, V = jax.ShapeDtypeStruct, pltpu.VMEM
    return kernel_call(
        body, "own_units", (info, w_up), [SM, HBM], S((width, fo), bf16), ANY,
        [V((width, ff), bf16), V((width, fo), bf16)], 2, 0, 6 << 20,
    )


def ffn_grads(info, l, hs, gs, wu_own, w_down, b_own, small, gbup, gqv, orders, fast):
    rows, width = hs[0].shape[-2:]
    fo = wu_own.shape[1]
    n = len(hs)
    paired = gs is None
    gs = () if paired else tuple(gs)
    m = n + len(gs)
    chips = 2 ** len(orders[0])
    part, unit = width // chips, fo // chips
    split = len(orders) == 2

    def body(*refs):
        info = refs[0]
        if paired:
            hr, gr = [r.at[0] for r in refs[1 : 1 + n]], [r.at[1] for r in refs[1 : 1 + n]]
        else:
            hr, gr = refs[1 : 1 + n], refs[1 + n : 1 + 2 * n]
        wu, wd, b, sm, bup, gqv = refs[1 + m : 7 + m]
        ends = refs[7 + m : 7 + m + 2 * len(orders)] if fast else refs[7 + m : 9 + m]
        h_v, g_v, wu_v, wd_v, act_v, gp_v, *o_vs, sm_v, sems = refs[7 + m + len(ends) :]
        o_v = o_vs[0]
        mv = Mover(sems)
        cu = mv.go(wu, wu_v)
        ch = [mv.go(hr[i], h_v.at[pl.ds(i * rows, rows)]) for i in range(n)]
        if fast:
            cd = []
            for i in range(chips):
                at = pl.multiple_of((4 * i + info[3]) * unit, unit)
                cd.append(mv.go(wd.at[l, pl.ds(at, unit)], wd_v.at[pl.ds(i * unit, unit)]))
        else:
            cd = [mv.go(wd.at[l], wd_v)]
        cg = [mv.go(gr[i], g_v.at[pl.ds(i * rows, rows)]) for i in range(n)]
        cu.wait()
        for i in range(n):
            at = pl.ds(i * rows, rows)
            ch[i].wait()
            u = mm(h_v[at], wu_v[...]) + b[l].astype(f32)
            cdf, slope = phi_parts(u)
            act_v[at] = (u * cdf).astype(bf16)
            if i == 0:
                for k in cd:
                    k.wait()
            cg[i].wait()
            gp_v[at] = (mm(g_v[at], wd_v[...], NT) * slope).astype(bf16)
        up = mm(h_v[...], gp_v[...], TN).astype(bf16)
        if fast:
            for j in range(chips):
                o_v[place(j, info[1], orders[0]), :part] = up[j * part : (j + 1) * part]
            if split:
                halfway = chips // 2
                out = [mv.go(o_v.at[pl.ds(halfway, halfway)], ends[0]), mv.go(o_v.at[pl.ds(0, halfway)], ends[1])]
        else:
            o_v[:width] = up
        down = mm(act_v[...], g_v[...], TN).astype(bf16)
        if fast:
            sm_v[...] = sm[...]
            sm_v[6:8, pl.ds(pl.multiple_of(info[0] * (width // 2), 128), width // 2)] = gqv[...]
            whole = sm_v[...]
            low_v, top = o_vs[-1], 0 if split else part
            for j in range(chips):
                p = place(j, info[1], orders[-1])
                low_v[p, top : top + unit] = down[j * unit : (j + 1) * unit]
                low_v[p, top + unit :] = jnp.concatenate(
                    [
                        jnp.concatenate([whole[:, j * part : (j + 1) * part], jnp.zeros((8, width - part), f32)], 1),
                        jnp.concatenate([bup[:, 4 * j * unit : 4 * (j + 1) * unit], jnp.zeros((1, width - 4 * unit), f32)], 1),
                        jnp.zeros((7, width), f32),
                    ]
                ).astype(bf16)
            halfway = chips // 2
            out = out if split else []
            out += [mv.go(low_v.at[pl.ds(halfway, halfway)], ends[-2]), mv.go(low_v.at[pl.ds(0, halfway)], ends[-1])]
        else:
            o_v[width:] = down
            out = [mv.go(o_v.at[pl.ds(0, width)], ends[0]), mv.go(o_v.at[pl.ds(width, fo)], ends[1])]
        for k in out:
            k.wait()

    S, V = jax.ShapeDtypeStruct, pltpu.VMEM
    tok = V((n * rows, width), bf16)
    hid = V((n * rows, fo), bf16)
    if fast:
        sizes = (part, unit + 16) if split else (part + unit + 16,)
        outs = tuple(S((chips // 2, n_rows, width), bf16) for n_rows in sizes for _ in range(2))
        o_vs = [V((chips, n_rows, width), bf16) for n_rows in sizes]
    else:
        outs = (S((width, fo), bf16), S((fo, width), bf16))
        o_vs = [V((width + fo, width), bf16)]
    got = kernel_call(
        body, "ffn_grads", (info,) + tuple(hs) + gs + (wu_own, w_down, b_own, small, gbup, gqv), [SM] + [ANY] * m + [HBM, HBM] + [VM] * 4,
        outs, (ANY,) * len(outs), [tok, tok, V((width, fo), bf16), V((fo, width), bf16), hid, hid] + o_vs + [V((8, width), f32)],
        2 * n + 6 + chips, 8 * n * rows * width * fo, 8 << 20,
    )
    if fast:
        return [(got[2 * i], got[2 * i + 1]) for i in range(len(orders))]
    zero = jnp.zeros_like(gqv)
    gqv = jnp.where(info[0] == 0, jnp.concatenate([gqv, zero], 1), jnp.concatenate([zero, gqv], 1))
    small = jnp.concatenate([small[:6], gqv]).reshape(8, chips, part).transpose(1, 0, 2)
    small = jnp.concatenate([jnp.pad(small, ((0, 0), (0, 0), (0, width - part))),
                             jnp.pad(gbup.reshape(chips, 1, 4 * unit), ((0, 0), (0, 7), (0, width - 4 * unit)))], 1)
    both = [[got[0].reshape(chips, part, fo)], [got[1].reshape(chips, unit, width), small.astype(bf16)]]
    if not split:
        both = [both[0] + both[1]]
    both = [arranged(jnp.concatenate(v, 1), info[1], order) for v, order in zip(both, orders)]
    return [(v[chips // 2 :], v[: chips // 2]) for v in both]


def proj_grads(info, xo, xt, ctx, got, go, gt, gproj, order, fast):
    rows, width = xo.shape
    half = width // 2
    toks = 2 * rows
    chips = 2 ** len(order)
    part = width // chips

    def body(info, xo, xt, ctx, got, go, gt, gp, *refs):
        outs, (x_v, gp_v, c_v, ga_v, o_v, sems) = refs[:-6], refs[-6:]
        mv = Mover(sems)
        c, me, y = info[0], info[1], info[2]
        top, low = pl.ds(0, rows), pl.ds(rows, rows)
        cols = pl.ds(pl.multiple_of(c * half, 128), half)
        cx = [mv.go(xo, x_v.at[top]), mv.go(xt, x_v.at[low]), mv.go(gp, gp_v)]
        cc = [mv.go(ctx, c_v.at[0]), mv.go(got.at[low], c_v.at[1, top]), mv.go(got.at[top], c_v.at[1, low]),
              mv.go(go.at[:, cols], ga_v.at[top]), mv.go(gt.at[:, cols], ga_v.at[low])]
        for k in cx:
            k.wait()
        for g in range(4):
            if g < 3:
                blocks = [(0, mm(x_v[...], gp_v[:, g * half : (g + 1) * half], TN).astype(bf16))]
            else:
                for k in cc:
                    k.wait()
                blocks = [(c if i == 0 else 1 - c, mm(c_v[i], ga_v[...], TN).astype(bf16)) for i in range(2)]
            at = slice(g % 2 * half, (g % 2 + 1) * half)
            for who, val in blocks:
                if fast:
                    for j in range(val.shape[0] // part):
                        p = place(who * (chips // 2) + j, me, order)
                        o_v[jnp.bitwise_xor(g // 2, y), p, :, at] = val[j * part : (j + 1) * part]
                elif g < 3:
                    o_v[g // 2, :, at] = val
                else:
                    o_v[1, pl.ds(pl.multiple_of(who * half, 128), half), at] = val
        out = [mv.go(o_v.at[1], outs[0]), mv.go(o_v.at[0], outs[1])] if fast else [mv.go(o_v, outs[0])]
        for k in out:
            k.wait()

    S, V = jax.ShapeDtypeStruct, pltpu.VMEM
    shape = (2, chips, part, width) if fast else (2, width, width)
    res = kernel_call(
        body, "proj_grads", (info, xo, xt, ctx, got, go, gt, gproj), [SM] + [ANY] * 7,
        (S(shape[1:], bf16),) * 2 if fast else S(shape, bf16), (ANY, ANY) if fast else ANY,
        [V((toks, width), bf16), V((toks, 3 * half), bf16), V((2, toks, half), bf16), V((toks, half), bf16), V(shape, bf16)],
        10, 2 * toks * width * 4 * half, 6 << 20,
    )
    if fast:
        return res
    v = res.reshape(2, chips, part, width)
    v = jnp.where(info[2] == 1, v[::-1], v)
    return arranged(v[1], info[1], order), arranged(v[0], info[1], order)


def pack(info, ends, part, unit, fast):
    width = ends[0][0].shape[-1]
    hp = part // 2
    if not fast:
        v = jnp.concatenate([add(k[0], g[0]).astype(bf16) for k, g in ends])
        up, low, proj = v[:part].reshape(2, hp, width), v[part : part + unit + 16], v[part + unit + 16 :].reshape(2, hp, width)
        mine, other = pick(up, info[0], 0), pick(up, 1 - info[0], 0)
        return (jnp.concatenate([mine, low, pick(proj, info[0], 0)]), jnp.concatenate([other, low[unit:], pick(proj, 1 - info[0], 0)]))
    n = len(ends)

    def body(info, *refs):
        ks, gs, row_o, col_o = refs[:n], refs[n : 2 * n], refs[2 * n], refs[2 * n + 1]
        k_v, g_v, row_v, col_v, sems = refs[2 * n + 2 :]
        mv = Mover(sems)
        at, come = 0, []
        for k, g in zip(ks, gs):
            now = pl.ds(at, k.shape[1])
            come += [mv.go(k.at[0], k_v.at[now]), mv.go(g.at[0], g_v.at[now])]
            at += k.shape[1]
        for c in come:
            c.wait()
        v = (k_v[...].astype(f32) + g_v[...].astype(f32)).astype(bf16)
        first = info[0] == 0
        lo = part + unit + 16
        up0, up1, pr0, pr1 = v[:hp], v[hp:part], v[lo : lo + hp], v[lo + hp :]
        row_v[:hp] = jnp.where(first, up0, up1)
        row_v[hp : hp + unit + 16] = v[part:lo]
        row_v[hp + unit + 16 :] = jnp.where(first, pr0, pr1)
        col_v[:hp] = jnp.where(first, up1, up0)
        col_v[hp : hp + 16] = v[lo - 16 : lo]
        col_v[hp + 16 :] = jnp.where(first, pr1, pr0)
        for c in [mv.go(col_v, col_o), mv.go(row_v, row_o)]:
            c.wait()

    total = sum(k.shape[1] for k, _ in ends)
    S, V = jax.ShapeDtypeStruct, pltpu.VMEM
    shapes = [(part + unit + 16, width), (part + 16, width)]
    return kernel_call(
        body, "pack", (info,) + tuple(k for k, _ in ends) + tuple(g for _, g in ends), [SM] + [ANY] * (2 * n),
        tuple(S(v, bf16) for v in shapes), (ANY, ANY), [V((total, width), bf16)] * 2 + [V(v, bf16) for v in shapes], 2 * n + 2, 0, 0,
    )


def unpack(info, rounds, part, unit, chips, fast):
    layers = len(rounds)
    width = rounds[0][0].shape[-1]
    hp, half = part // 2, width // 2
    lo = hp + unit + 16
    if not fast:
        res = []
        for own, row, core, diag in rounds:
            def quarters(a, b):
                mine = order_two(info[2], own[a], row[a], 0)
                other = order_two(info[2], core[b], diag[b], 0)
                return order_two(info[0], mine, other, 0)

            up = quarters(slice(0, hp), slice(0, hp)).reshape(2, 2, hp, chips, unit)
            up = up.transpose(2, 3, 0, 1, 4).reshape(hp, 4 * width).astype(f32)
            proj = quarters(slice(lo, lo + hp), slice(hp + 16, part + 16)).reshape(2, 2, hp, 2, half)
            proj = proj.transpose(2, 1, 3, 0, 4).reshape(hp, 4 * width).astype(f32)
            down = order_two(info[2], own[hp : hp + unit], row[hp : hp + unit], 0).reshape(2 * unit, width).astype(f32)
            small = add(own[lo - 16 : lo], row[lo - 16 : lo]) + add(core[hp : hp + 16], diag[hp : hp + 16])
            vecs = pick(small[:8, :part].reshape(8, 2, hp), info[0], 1)
            bup = pick(small[8, : 4 * unit].reshape(2, 2 * unit), info[0], 0)
            res.append((proj[:, : 3 * width], proj[:, 3 * width :], up, down, bup, vecs[6:8]) + tuple(vecs[i] for i in range(6)))
        return tuple(jnp.stack([r[i] for r in res]) for i in range(12))

    def body(info, *refs):
        src, outs = refs[: 4 * layers], refs[4 * layers : 4 * layers + 12]
        big_v, small_v, q_v, d_v, sems = refs[4 * layers + 12 :]
        mv = Mover(sems)
        come = []
        for l in range(layers):
            for i in range(4):
                to = big_v.at[l, i] if i < 2 else small_v.at[l, i - 2]
                come.append(mv.go(src[4 * l + i], to))
        qkv, out, up, down, bup, gqv = outs[:6]
        c, y, share = info[0], info[2], info[3]
        first = c == 0
        for l in range(layers):
            for k in come[4 * l : 4 * l + 4]:
                k.wait()
            diag = 3 - share
            for p, (a, b) in enumerate(((0, 0), (lo, hp + 16))):
                q_v[p, share] = big_v[l, 0, a : a + hp]
                q_v[p, 2 * c + 1 - y] = big_v[l, 1, a : a + hp]
                q_v[p, 2 * (1 - c) + y] = small_v[l, 0, b : b + hp]
                q_v[p, diag] = small_v[l, 1, b : b + hp]
            d_v[y] = big_v[l, 0, hp : hp + unit]
            d_v[1 - y] = big_v[l, 1, hp : hp + unit]
            for q in range(4):
                whole = q_v[0, q].astype(f32)
                for i in range(chips):
                    up[l, :, (4 * i + q) * unit : (4 * i + q + 1) * unit] = whole[:, i * unit : (i + 1) * unit]
                whole = q_v[1, q].astype(f32)
                at = q // 2 * half
                if q % 2 == 0:
                    qkv[l, :, at : at + half] = whole[:, :half]
                    qkv[l, :, width + at : width + at + half] = whole[:, half:]
                else:
                    qkv[l, :, 2 * width + at : 2 * width + at + half] = whole[:, :half]
                    out[l, :, at : at + half] = whole[:, half:]
            for i in range(2):
                down[l, i * unit : (i + 1) * unit] = d_v[i].astype(f32)
            small = (big_v[l, 0, lo - 16 : lo].astype(f32) + big_v[l, 1, lo - 16 : lo].astype(f32)) + (
                small_v[l, 0, hp : hp + 16].astype(f32) + small_v[l, 1, hp : hp + 16].astype(f32))
            vecs = jnp.where(first, small[:8, :hp], small[:8, hp:part])
            bup[l : l + 1] = jnp.where(first, small[8:9, : 2 * unit], small[8:9, 2 * unit : 4 * unit])
            gqv[l] = vecs[6:8]
            for i in range(6):
                outs[6 + i][l : l + 1] = vecs[i : i + 1]

    S, V = jax.ShapeDtypeStruct, pltpu.VMEM
    outs = [(layers, hp, 3 * width), (layers, hp, width), (layers, hp, 4 * width), (layers, 2 * unit, width), (layers, 2 * unit), (layers, 2, hp)]
    outs += [(layers, hp)] * 6
    args = (info,) + tuple(v for r in rounds for v in r)
    return kernel_call(
        body, "unpack", args, [SM] + [ANY] * (4 * layers), tuple(S(v, f32) for v in outs), (VM,) * 12,
        [V((layers, 2, part + unit + 16, width), bf16), V((layers, 2, part + 16, width), bf16), V((2, 4, hp, width), bf16), V((2, unit, width), bf16)],
        4 * layers, 0, 0,
    )


class Wires:
    def __init__(self, batch, seq):
        self.batch, self.seq = batch, seq
        self.chips = batch // 2
        self.bits = self.chips.bit_length() - 1
        where = [(i, j) for i in range(batch) for j in range(seq)]

        def table(move):
            out = []
            for i, j in where:
                p, q = move(i, j)
                out.append((i * seq + j, p * seq + q))
            return out

        self.core = table(lambda i, j: (i ^ 1, j))
        self.row = table(lambda i, j: (i, 1 - j))
        self.diag = table(lambda i, j: (i ^ 1, 1 - j))
        self.turn = table(lambda i, j: (i - i % 2 + j, i % 2))
        self.chip = [table(lambda i, j, k=k: (i ^ (2 << k), j)) for k in range(self.bits)]
        self.b = lax.axis_index("batch")
        self.y = lax.axis_index("seq")
        self.c = self.b % 2

    def swap_core(self, v):
        return lax.ppermute(v, AXES, self.core)

    def swap_row(self, v):
        return lax.ppermute(v, AXES, self.row)

    def swap_diag(self, v):
        return lax.ppermute(v, AXES, self.diag)

    def swap_turn(self, v):
        return lax.ppermute(v, AXES, self.turn)

    def swap_chip(self, v, k):
        return lax.ppermute(v, AXES, self.chip[k])

    def bit(self, k):
        return (self.b >> (k + 1)) & 1


def pick(v, idx, axis):
    return lax.dynamic_index_in_dim(v, idx, axis, keepdims=False)


def add(a, b):
    return a.astype(f32) + b.astype(f32)


def order_two(flag, mine, got, axis):
    return jnp.stack([jnp.where(flag == 0, mine, got), jnp.where(flag == 0, got, mine)], axis)


class Clock:
    def __init__(self):
        self.now, self.free, self.alive = 0.0, {}, []

    def busy(self, link, us):
        begin = max(self.now, self.free.get(link, 0.0))
        self.free[link] = begin + us
        return begin + us

    def work(self, us):
        self.now += us

    def catch_up(self):
        for s in sorted(self.alive, key=lambda s: s.ready):
            if s.ready <= self.now:
                s.step()

    def drain(self):
        while self.alive:
            min(self.alive, key=lambda s: s.ready).step()


class Stream:
    def __init__(self, wires, clock, send, keep, order, row_first):
        self.wires, self.clock, self.keep, self.end = wires, clock, keep, None
        self.todo = list(order)
        clock.alive.append(self)
        self.send(send, row_first)

    def send(self, v, row=False):
        us = v.size * 2 / 1e6 * 22.0
        if row:
            self.got, link = self.wires.swap_row(v), "y"
        else:
            k = self.todo.pop(0)
            self.got = self.wires.swap_chip(v, k)
            link = "x" if k == 0 else "z"
            us *= max(1, 1 << (k - 1)) if k else 1
        self.clock.work(1.4)
        self.ready = self.clock.busy(link, us) + 2.0

    def step(self):
        clock = self.clock
        clock.now = max(clock.now, self.ready)
        if not self.todo:
            self.end = (self.keep, self.got)
            clock.alive.remove(self)
            return
        clock.work(1.2 + self.keep.size * 2 / 1e6)
        send, self.keep = merge(self.keep, self.got)
        self.send(send)


def local(inputs, out_grad, masked, w_qkv, bias_qv, w_out, bias_out, gain_one, shift_one, w_up, bias_up, w_down, bias_down, gain_two, shift_two):
    wires = Wires(lax.axis_size("batch"), lax.axis_size("seq"))
    layers, width, ff = w_up.shape
    half = width // 2
    chips, bits = wires.chips, wires.bits
    fo, unit, part = ff // 4, ff // chips // 4, width // chips
    fast = part % 32 == 0
    share = wires.c * 2 + wires.y
    info = jnp.stack([wires.c, wires.b // 2, wires.y, share]).astype(jnp.int32)
    rows = inputs.shape[1]
    ROW.extra = []
    xb = wires.swap_turn(inputs[0])
    b_own = pick(bias_up.reshape(layers, chips, 4, unit), share, 2).reshape(layers, 1, fo)
    if fast:
        wu_own, wd_own = [own_units(info, l, w_up, chips) for l in range(layers)], w_down
    else:
        wu_own = pick(w_up.reshape(layers, width, chips, 4, unit), share, 3).reshape(layers, width, fo)
        wd_own = pick(w_down.reshape(layers, chips, 4, unit, width), share, 2).reshape(layers, fo, width)
    gy = wires.swap_turn((out_grad * masked.astype(bf16)[..., None])[0])
    x = xb
    saved, outs, hs = [], [], []
    tail = (w_out, bias_out, gain_one, shift_one, w_up, bias_up, w_down, bias_down, gain_two, shift_two)
    clock = Clock()
    for l in range(layers):
        xt = wires.swap_core(xb)
        qkv, pt, ctx = attn_fwd(info, l, xb, xt, w_qkv, bias_qv)
        if l == 0:
            ROW.before_next(gy)
        else:
            ROW.before_next(*hs[-1], outs[-1])
        got = wires.swap_core(ctx)
        last = l == layers - 1
        if last:
            yb, pair, ga, gm, small, gbup = ffn_fwd(info, l, x, ctx, got, tail, gy)
            saved.append((xb, xt, qkv, pt, ctx, got))
            turned_back = (pair, ga, gm, small, gbup)
        else:
            hb, dg, mixed, x, yb = ffn_fwd(info, l, x, ctx, got, tail)
            hy = wires.swap_row(hb)
            hs.append((hb, hy, wires.swap_core(hb), wires.swap_core(hy)))
            saved.append((xb, xt, qkv, pt, ctx, got, dg, mixed, x))
        outs.append(wires.swap_turn(yb)[None])
        xb = yb
    low = list(range(bits))
    turned = low[1:2] + low[:1] + low[2:]
    plan = [((low, turned), low)] + [((turned,), low)] * (layers - 1)
    streams = [None] * layers
    for l in reversed(range(layers)):
        xb, xt, qkv, pt, ctx, got = saved[l][:6]
        if l == layers - 1:
            pair, ga, gm, small, gbup = turned_back
            gat = wires.swap_core(ga)
            py = wires.swap_row(pair)
            both = (pair, py, wires.swap_core(pair), wires.swap_core(py)), None
        else:
            dg, mixed, summed = saved[l][6:]
            gf, ga, gm, small, gbup = ffn_bwd(info, l, flow, summed, mixed, dg, (w_up, w_down, gain_one, gain_two))
            gat = wires.swap_core(ga)
            gfy = wires.swap_row(gf)
            both = hs[l], (gf, gfy, wires.swap_core(gf), wires.swap_core(gfy))
        gproj, gptail, gqv = attn_bwd(info, l, ga, gat, w_out, qkv, pt)
        if l == layers - 1:
            ROW.before_next(outs[-1])
        flow = (gm, gproj, wires.swap_core(gptail), w_qkv)
        clock.work(28.0 if l < layers - 1 else 0.0)
        clock.catch_up()
        send, keep = proj_grads(info, xb, xt, ctx, got, ga, gat, gproj, plan[l][1], fast)
        clock.work(4.5)
        ps = [Stream(wires, clock, send, keep, plan[l][1], True)]
        clock.catch_up()
        res = ffn_grads(info, l, *both, wu_own[l], wd_own, b_own, small, gbup, gqv, plan[l][0], fast)
        clock.work(10.5)
        fs = [Stream(wires, clock, s, k, order, False) for (s, k), order in zip(res, plan[l][0])]
        clock.catch_up()
        streams[l] = fs + ps
    end = chain_end(info, 0, flow)
    clock.work(5.5)
    grad_in = wires.swap_turn(end)[None]
    rounds = [None] * layers
    while not all(rounds):
        if clock.alive:
            min(clock.alive, key=lambda s: s.ready).step()
        for l in range(layers):
            if rounds[l] is None and all(s.end for s in streams[l]):
                row, col = pack(info, [s.end for s in streams[l]], part, unit, fast)
                rounds[l] = (row, wires.swap_row(row), wires.swap_core(col), wires.swap_diag(col))
                clock.work(5.0)
                clock.busy("y", 11.0)
    qkv, out, up, down, bup, gqv, gdn, gg2, gs2, gg1, gs1, gbo = unpack(info, rounds, part, unit, chips, fast)
    return (outs[0], outs[-1], grad_in, qkv, gqv, out, gbo, gg1, gs1, up, bup, down, gdn, gg2, gs2)


def solution(mesh):
    tok = P("batch", "seq", None)
    in_specs = (tok, tok, P("batch", "seq")) + (P(),) * 12
    mat, vec = P(None, "batch", None), P(None, "batch")
    out_specs = (tok, tok, tok, mat, P(None, None, "batch"), mat, vec, vec, vec, mat, vec, mat, vec, vec, vec)
    return jax.shard_map(local, mesh=mesh, in_specs=in_specs, out_specs=out_specs, check_vma=False)
```

```python
import math

import jax
import jax.numpy as jnp
from jax import lax
from jax.experimental import pallas as pl
from jax.experimental.pallas import tpu as pltpu
from jax.sharding import PartitionSpec as P

HEAD_DIM = 64
AXES = ("batch", "seq")
norm_eps = 1e-06
f32 = jnp.float32
bf16 = jnp.bfloat16
ANY = pl.BlockSpec(memory_space=pl.ANY)
HBM = pl.BlockSpec(memory_space=pltpu.HBM)
VM = pl.BlockSpec(memory_space=pltpu.VMEM)
SM = pl.BlockSpec(memory_space=pltpu.SMEM)
ROOT_HALF = 0.7071067811865476
INV_ROOT_TAU = 0.3989422804014327
TAKES = {"own_units": 24.0, "attn_fwd": 7.5, "ffn_fwd": 9.0, "ffn_turn": 13.0, "ffn_bwd": 12.0, "attn_bwd": 7.5, "ffn_grads": 10.5, "proj_grads": 18, "chain_end": 4.5, "merge": 7.0, "masked_grad": 2.0, "pack": 3.0, "unpack": 5.0}
PACE = 0.5


def mm(a, b, dims=((1,), (0,))):
    return lax.dot_general(a, b, (dims, ((), ())), preferred_element_type=f32)


NT = ((1,), (1,))
TN = ((0,), (0,))


class Mover:
    def __init__(self, sems):
        self.sems, self.used = sems, 0

    def go(self, src, dst):
        copy = pltpu.make_async_copy(src, dst, self.sems.at[self.used])
        self.used += 1
        copy.start()
        return copy


class Row:
    def __init__(self):
        self.extra = []

    def before_next(self, *values):
        self.extra.extend(values)


ROW = Row()


def kernel_call(body, name, args, specs, outs, out_specs, scratch, sems, flops, moved):
    extra = tuple(ROW.extra)
    n, m = len(args), len(args) + len(extra)
    held = sum(math.prod(v.shape) * jnp.dtype(v.dtype).itemsize for v in scratch)
    limit = held + ((2 << 20) if name == "merge" else (12 << 20))
    args = tuple(
        pltpu.with_memory_space_constraint(a, pltpu.HBM) if spec is HBM else a for a, spec in zip(args, specs)
    )
    out = pl.pallas_call(
        lambda *refs: body(*refs[:n], *refs[m:]),
        name=name,
        out_shape=outs,
        in_specs=specs + [ANY] * len(extra),
        out_specs=out_specs,
        scratch_shapes=list(scratch) + [pltpu.SemaphoreType.DMA((sems,))],
        compiler_params=pltpu.CompilerParams(vmem_limit_bytes=limit),
        cost_estimate=pl.CostEstimate(flops=int(PACE * TAKES[name] * 1.15e9), bytes_accessed=moved, transcendentals=0),
    )(*args, *extra)
    ROW.extra = [out[0] if isinstance(out, (tuple, list)) else out]
    return out


def merge(keep, got):
    n = max(keep.shape[0] // 2, 1)
    rest = keep.shape[1:]
    parts = keep.shape[0] // n

    def body(k, g, *refs):
        outs, (k_v, g_v, sems) = refs[:parts], refs[parts:]
        mv = Mover(sems)
        at = [pl.ds((parts - 1 - i) * n, n) for i in range(parts)]
        come = [(mv.go(k.at[a], k_v.at[a]), mv.go(g.at[a], g_v.at[a])) for a in at]
        gone = []
        for i, a in enumerate(at):
            for c in come[i]:
                c.wait()

            def one(j, _):
                j = j + (parts - 1 - i) * n
                k_v[j] = (k_v[j].astype(f32) + g_v[j].astype(f32)).astype(bf16)
                return 0

            lax.fori_loop(0, n, one, 0)
            gone.append(mv.go(k_v.at[a], outs[i]))
        for c in gone:
            c.wait()

    outs = (jax.ShapeDtypeStruct((n,) + rest, bf16),) * parts
    return kernel_call(body, "merge", (keep, got), [ANY, ANY], outs, (ANY,) * parts, [pltpu.VMEM(keep.shape, bf16)] * 2, 3 * parts, 5 * 10**9, 0)


def normed(z):
    center = z - jnp.mean(z, -1, keepdims=True)
    rstd = lax.rsqrt(jnp.mean(center * center, -1, keepdims=True) + norm_eps)
    return center * rstd, rstd


def norm_back(g, z, gain):
    xhat, rstd = normed(z)
    gx = g * gain
    m1 = jnp.mean(gx, -1, keepdims=True)
    m2 = jnp.mean(gx * xhat, -1, keepdims=True)
    return rstd * (gx - m1 - xhat * m2), g * xhat


def phi_parts(u):
    cdf = 0.5 * (1.0 + lax.erf(u * ROOT_HALF))
    return cdf, cdf + u * (jnp.exp(-0.5 * u * u) * INV_ROOT_TAU)


def masked_grad(grad, masked):
    rows, width = grad.shape

    def body(g, m, o, sems):
        col = jnp.broadcast_to(m[...].astype(f32), (8, rows)).T[:, :1]
        o[...] = (g[...].astype(f32) * col).astype(bf16)

    return kernel_call(body, "masked_grad", (grad, masked), [VM, VM], jax.ShapeDtypeStruct((rows, width), bf16), VM, [], 1, 0, 0)


def attn_fwd(info, l, xo, xt, w_qkv, bias_qv):
    rows, width = xo.shape
    half = width // 2
    heads = half // HEAD_DIM
    toks = 2 * rows

    def body(info, xo, xt, w, bias, qkv_o, pt_o, ctx_o, x_v, w_v, qkv_v, pt_v, ctx_v, sems):
        mv = Mover(sems)
        c = info[0]
        cx = [mv.go(xo, x_v.at[pl.ds(0, rows)]), mv.go(xt, x_v.at[pl.ds(rows, rows)])]
        cw = []
        for p in range(3):
            at = pl.multiple_of(p * width + c * half, 128)
            cw.append(mv.go(w.at[l, :, pl.ds(at, half)], w_v.at[p]))
        for k in cx:
            k.wait()
        at = pl.multiple_of(c * half, 128)
        for p in range(3):
            cw[p].wait()
            val = mm(x_v[...], w_v[p])
            if p != 1:
                val = val + bias[l, pl.ds(p // 2, 1), pl.ds(at, half)].astype(f32)
            val = val.astype(bf16)
            if p == 0:
                val = (val.astype(f32) * HEAD_DIM ** (-0.5)).astype(bf16)
            qkv_v[:, p * half : (p + 1) * half] = val
        out = [mv.go(qkv_v, qkv_o)]
        lane = lax.broadcasted_iota(jnp.int32, (toks, 2 * HEAD_DIM), 1) < HEAD_DIM

        for i in range(heads // 2):
            at = i * 2 * HEAD_DIM
            q = qkv_v[:, at : at + 128]
            k = qkv_v[:, half + at : half + at + 128]
            v = qkv_v[:, 2 * half + at : 2 * half + at + 128]
            both = []
            for h in range(2):
                qm = jnp.where(lane == (h == 0), q, jnp.zeros_like(q))
                st = mm(k, qm, NT)
                top = jnp.max(st, 0, keepdims=True)
                e = jnp.exp(st - top)
                p = (e / jnp.sum(e, 0, keepdims=True)).astype(bf16)
                pt_v[2 * i + h] = p
                both.append(mm(p, v, TN))
            ctx_v[:, at : at + 128] = jnp.where(lane, both[0], both[1]).astype(bf16)
            now = pl.ds(2 * i, 2)
            out.append(mv.go(pt_v.at[now], pt_o.at[now]))
        out.append(mv.go(ctx_v, ctx_o))
        for k in out:
            k.wait()

    S = jax.ShapeDtypeStruct
    outs = (pltpu.HBM((toks, 3 * half), bf16), pltpu.HBM((heads, toks, toks), bf16), S((toks, half), bf16))
    return kernel_call(
        body, "attn_fwd", (info, xo, xt, w_qkv, bias_qv), [SM, ANY, ANY, HBM, VM], outs, (ANY,) * 3,
        [pltpu.VMEM((toks, width), bf16), pltpu.VMEM((3, width, half), bf16), pltpu.VMEM((toks, 3 * half), bf16),
         pltpu.VMEM((heads, toks, toks), bf16), pltpu.VMEM((toks, half), bf16)],
        8 + heads // 2, 2 * toks * width * 3 * half + 8 * heads * toks * toks * 128, 8 << 20,
    )


def ffn_fwd(info, l, x, ctx, got, weights, gy=None, cut=6):
    w_out, bias_out, gain_one, shift_one, w_up, bias_up, w_down, bias_down, gain_two, shift_two = weights
    rows, width = x.shape
    half = width // 2
    ff = w_up.shape[2]
    step = ff // cut
    turn = gy is not None

    def body(info, x, ctx, got, wo, bo, g1, s1, wu, bu, wd, bd, g2, s2, *refs):
        if turn:
            gy_r, yb_o, pair_o, ga_o, gm_o, small_o, gbup_o = refs[:7]
            x_v, c_v, wo_v, wu_v, wd_v, hb_v, dg_v, mixed_v, yb_v, low_v, gf_v, gm_v, sems = refs[7:]
        else:
            hb_o, dg_o, mixed_o, summed_o, yb_o = refs[:5]
            x_v, c_v, wo_v, wu_v, wd_v, hb_v, dg_v, mixed_v, yb_v, sems = refs[5:]
        mv = Mover(sems)
        c = info[0]
        cx = mv.go(x, hb_v if l == 0 else x_v)
        first = [mv.go(ctx.at[pl.ds(0, rows)], c_v.at[0])]
        at = [pl.multiple_of(c * half, 128), pl.multiple_of((1 - c) * half, 128)]
        first += [mv.go(wo.at[l, pl.ds(at[i], half)], wo_v.at[i]) for i in range(2)]
        first += [mv.go(got.at[pl.ds(rows, rows)], c_v.at[1])]
        cu, cd = [], []
        for j in range(cut):
            cu.append(mv.go(wu.at[l, :, pl.ds(j * step, step)], wu_v.at[j]))
            cd.append(mv.go(wd.at[l, pl.ds(j * step, step)], wd_v.at[j]))
        if turn:
            cg = mv.go(gy_r, low_v)
        cx.wait()
        if l == 0:
            xin = hb_v[...].astype(f32)
        else:
            xin = normed(x_v[...])[0] * g2[l - 1 : l].astype(f32) + s2[l - 1 : l].astype(f32)
        for k in first:
            k.wait()
        mixed = xin + mm(c_v[0], wo_v[0]) + mm(c_v[1], wo_v[1]) + bo[l : l + 1].astype(f32)
        mixed_v[...] = mixed
        out = [] if turn else [mv.go(mixed_v, mixed_o)]
        hid = normed(mixed)[0] * g1[l : l + 1].astype(f32) + s1[l : l + 1].astype(f32)
        x_v[...] = hid
        hb_v[...] = hid.astype(bf16)
        out.append(mv.go(hb_v, pair_o.at[0] if turn else hb_o))
        acc = None
        for j in range(cut):
            cols = slice(j * step, (j + 1) * step)
            cu[j].wait()
            u = mm(hb_v[...], wu_v[j]) + bu[l : l + 1, cols].astype(f32)
            cdf, slope = phi_parts(u)
            dg_v[j] = slope.astype(dg_v.dtype)
            if not turn:
                out.append(mv.go(dg_v.at[j], dg_o.at[:, pl.ds(j * step, step)]))
            cd[j].wait()
            part = mm((u * cdf).astype(bf16), wd_v[j])
            acc = part if acc is None else acc + part
        summed = x_v[...] + acc + bd[l : l + 1].astype(f32)
        x_v[...] = summed
        if not turn:
            out.append(mv.go(x_v, summed_o))
        gain = g2[l : l + 1].astype(f32)
        y = normed(summed)[0] * gain + s2[l : l + 1].astype(f32)
        yb_v[...] = y.astype(bf16)
        out.append(mv.go(yb_v, yb_o))
        if turn:
            cg.wait()
            gy = low_v[...].astype(f32)
            gsum, gterm = norm_back(gy, x_v[...], gain)
            small_o[1:2] = jnp.sum(gterm, 0, keepdims=True)
            small_o[2:3] = jnp.sum(gy, 0, keepdims=True)
            gf = gsum.astype(bf16)
            gf_v[...] = gf
            small_o[0:1] = jnp.sum(gf.astype(f32), 0, keepdims=True)
            out.append(mv.go(gf_v, pair_o.at[1]))
            gm_v[...] = gsum
            acc = None
            for j in range(cut):
                gpre = (mm(gf_v[...], wd_v[j], NT) * dg_v[j].astype(f32)).astype(bf16)
                gbup_o[:, j * step : (j + 1) * step] = jnp.sum(gpre.astype(f32), 0, keepdims=True)
                part = mm(gpre, wu_v[j], NT)
                acc = part if acc is None else acc + part
            ghid = gm_v[...] + acc
            gmix, gterm = norm_back(ghid, mixed_v[...], g1[l : l + 1].astype(f32))
            ga = gmix.astype(bf16)
            low_v[...] = ga
            out.append(mv.go(low_v, ga_o))
            gm_v[...] = gmix
            out.append(mv.go(gm_v, gm_o))
            small_o[3:4] = jnp.sum(gterm, 0, keepdims=True)
            small_o[4:5] = jnp.sum(ghid, 0, keepdims=True)
            small_o[5:6] = jnp.sum(ga.astype(f32), 0, keepdims=True)
            small_o[6:8] = jnp.zeros((2, width), f32)
        for k in out:
            k.wait()

    S, V = jax.ShapeDtypeStruct, pltpu.VMEM
    full, low = S((rows, width), f32), S((rows, width), bf16)
    scratch = [V((rows, width), f32), V((2, rows, half), bf16), V((2, half, width), bf16), V((cut, width, step), bf16),
               V((cut, step, width), bf16), V((rows, width), bf16), V((cut, rows, step), bf16), V((rows, width), f32),
               V((rows, width), bf16)]
    args = (info, x, ctx, got, w_out, bias_out, gain_one, shift_one, w_up, bias_up, w_down, bias_down, gain_two, shift_two)
    specs = [SM, ANY, ANY, ANY, HBM, VM, VM, VM, HBM, VM, HBM, VM, VM, VM]
    if turn:
        outs = (low, S((2, rows, width), bf16), low, full, S((8, width), f32), S((1, ff), f32))
        out_specs = (ANY, ANY, ANY, ANY, VM, VM)
        scratch += [V((rows, width), bf16), V((rows, width), bf16), V((rows, width), f32)]
        args, specs = args + (gy,), specs + [ANY]
    else:
        outs, out_specs = (low, pltpu.HBM((rows, ff), bf16), pltpu.HBM((rows, width), f32), full, low), (ANY,) * 5
    return kernel_call(
        body, "ffn_turn" if turn else "ffn_fwd", args, specs, outs, out_specs, scratch, 14 + 3 * cut, 0, 12 << 20,
    )


def ffn_bwd(info, l, flow, summed, mixed, dg, weights, cut=6):
    w_up, w_down, gain_one, gain_two = weights
    rows, width = summed.shape
    half = width // 2
    ff = w_up.shape[2]
    step = ff // cut
    chained = len(flow) > 1

    def body(*refs):
        info = refs[0]
        fl = refs[1 : 1 + len(flow)]
        (sm, mi, dgr, wu, wd, g1, g2, gf_o, ga_o, gm_o, small_o, gbup_o,
         gy_v, sm_v, mi_v, dg_v, wu_v, wd_v, gf_v, ga_v, gm_v) = refs[1 + len(flow) : 22 + len(flow)]
        sems = refs[-1]
        mv = Mover(sems)
        if chained:
            gp_v, wq_v = refs[22 + len(flow) : 24 + len(flow)]
            c = info[0]
            fc = [mv.go(fl[0], gy_v), mv.go(fl[1].at[pl.ds(0, rows)], gp_v.at[0])]
            wq = []
            for i in range(2):
                who = c if i == 0 else 1 - c
                for p in range(3):
                    at = pl.multiple_of(p * width + who * half, 128)
                    wq.append(mv.go(fl[3].at[l + 1, :, pl.ds(at, half)], wq_v.at[i, p]))
            fc.append(mv.go(fl[2], gp_v.at[1]))
        else:
            fc = [mv.go(fl[0], gf_v)]
        fc += [mv.go(sm, sm_v)]
        cd, cu, cg = [], [], []
        for j in range(cut):
            cols = pl.ds(j * step, step)
            cd.append(mv.go(wd.at[l, cols], wd_v.at[j]))
            cg.append(mv.go(dgr.at[:, cols], dg_v.at[j]))
            cu.append(mv.go(wu.at[l, :, cols], wu_v.at[j]))
        cm = mv.go(mi, mi_v)
        for k in fc:
            k.wait()
        if chained:
            gy = gy_v[...]
            for i in range(2):
                for p in range(3):
                    wq[3 * i + p].wait()
                    gy = gy + mm(gp_v[i, :, p * half : (p + 1) * half], wq_v[i, p], NT)
        else:
            gy = gf_v[...].astype(f32)
        gsum, gterm = norm_back(gy, sm_v[...], g2[pl.ds(l, 1)].astype(f32))
        small_o[1:2] = jnp.sum(gterm, 0, keepdims=True)
        small_o[2:3] = jnp.sum(gy, 0, keepdims=True)
        gf = gsum.astype(bf16)
        gf_v[...] = gf
        small_o[0:1] = jnp.sum(gf.astype(f32), 0, keepdims=True)
        out = [mv.go(gf_v, gf_o)]
        gm_v[...] = gsum
        acc = None
        for j in range(cut):
            cd[j].wait()
            cg[j].wait()
            gpre = (mm(gf_v[...], wd_v[j], NT) * dg_v[j].astype(f32)).astype(bf16)
            gbup_o[:, j * step : (j + 1) * step] = jnp.sum(gpre.astype(f32), 0, keepdims=True)
            cu[j].wait()
            part = mm(gpre, wu_v[j], NT)
            acc = part if acc is None else acc + part
        ghid = gm_v[...] + acc
        cm.wait()
        gmix, gterm = norm_back(ghid, mi_v[...], g1[pl.ds(l, 1)].astype(f32))
        ga = gmix.astype(bf16)
        ga_v[...] = ga
        out.append(mv.go(ga_v, ga_o))
        gm_v[...] = gmix
        out.append(mv.go(gm_v, gm_o))
        small_o[3:4] = jnp.sum(gterm, 0, keepdims=True)
        small_o[4:5] = jnp.sum(ghid, 0, keepdims=True)
        small_o[5:6] = jnp.sum(ga.astype(f32), 0, keepdims=True)
        small_o[6:8] = jnp.zeros((2, width), f32)
        for k in out:
            k.wait()

    S, V = jax.ShapeDtypeStruct, pltpu.VMEM
    low = S((rows, width), bf16)
    outs = (low, low, S((rows, width), f32), S((8, width), f32), S((1, ff), f32))
    scratch = [V((rows, width), f32), V((rows, width), f32), V((rows, width), f32), V((cut, rows, step), bf16),
               V((cut, width, step), bf16), V((cut, step, width), bf16), V((rows, width), bf16), V((rows, width), bf16),
               V((rows, width), f32)]
    if chained:
        scratch += [V((2, rows, 3 * half), bf16), V((2, 3, width, half), bf16)]
    return kernel_call(
        body, "ffn_bwd", (info,) + tuple(flow) + (summed, mixed, dg, w_up, w_down, gain_one, gain_two),
        [SM] + [ANY, ANY, ANY, HBM][: len(flow)] + [ANY, HBM, HBM, HBM, HBM, VM, VM], outs, (ANY, ANY, ANY, VM, VM), scratch,
        15 + 3 * cut, 2 * rows * width * (2 * ff + (3 * width if chained else 0)), 15 << 20,
    )


def chain_end(info, l, flow):
    gmix, gproj, got, w_qkv = flow
    rows, width = gmix.shape
    half = width // 2

    def body(info, gm, gp, gt, w, o_ref, gy_v, gp_v, wq_v, o_v, sems):
        mv = Mover(sems)
        c = info[0]
        wq = []
        fc = [mv.go(gm, gy_v), mv.go(gp.at[pl.ds(0, rows)], gp_v.at[0]), mv.go(gt, gp_v.at[1])]
        for i in range(2):
            who = c if i == 0 else 1 - c
            for p in range(3):
                at = pl.multiple_of(p * width + who * half, 128)
                wq.append(mv.go(w.at[l, :, pl.ds(at, half)], wq_v.at[i, p]))
        for k in fc:
            k.wait()
        gy = gy_v[...]
        for i in range(2):
            for p in range(3):
                wq[3 * i + p].wait()
                gy = gy + mm(gp_v[i, :, p * half : (p + 1) * half], wq_v[i, p], NT)
        o_v[...] = gy.astype(bf16)
        k = mv.go(o_v, o_ref)
        k.wait()

    S, V = jax.ShapeDtypeStruct, pltpu.VMEM
    return kernel_call(
        body, "chain_end", (info,) + tuple(flow), [SM, ANY, ANY, ANY, HBM], S((rows, width), bf16), ANY,
        [V((rows, width), f32), V((2, rows, 3 * half), bf16), V((2, 3, width, half), bf16), V((rows, width), bf16)],
        10, 2 * rows * width * 3 * width, 5 << 20,
    )


def attn_bwd(info, l, go, gt, w_out, qkv, pt):
    rows, width = go.shape
    half = width // 2
    heads = half // HEAD_DIM
    toks = 2 * rows

    def body(info, go, gt, wo, qkv, pt, gp_o, gt_o, gb_o, ga_v, wo_v, qkv_v, pt_v, gc_v, gp_v, sems):
        mv = Mover(sems)
        c = info[0]
        at = pl.multiple_of(c * half, 128)
        fc = [mv.go(wo.at[l, pl.ds(at, half)], wo_v), mv.go(go, ga_v.at[pl.ds(0, rows)]), mv.go(gt, ga_v.at[pl.ds(rows, rows)])]
        cq = mv.go(qkv, qkv_v)
        cp = [mv.go(pt.at[pl.ds(2 * i, 2)], pt_v.at[pl.ds(2 * i, 2)]) for i in range(heads // 2)]
        for k in fc:
            k.wait()
        gc_v[...] = mm(ga_v[...], wo_v[...], NT).astype(bf16)
        cq.wait()
        lane = lax.broadcasted_iota(jnp.int32, (toks, 2 * HEAD_DIM), 1) < HEAD_DIM

        for i in range(heads // 2):
            cp[i].wait()
            at = i * 2 * HEAD_DIM
            at_k, at_v = half + at, 2 * half + at
            q = qkv_v[:, pl.ds(at, 128)]
            k = qkv_v[:, pl.ds(at_k, 128)]
            v = qkv_v[:, pl.ds(at_v, 128)]
            gc = gc_v[:, pl.ds(at, 128)]
            res = []
            for h in range(2):
                gm = jnp.where(lane == (h == 0), gc, jnp.zeros_like(gc))
                pb = pt_v[2 * i + h]
                t = mm(v, gm, NT)
                p = pb.astype(f32)
                inner = jnp.sum(p * t, 0, keepdims=True)
                gs = (p * (t - inner)).astype(bf16)
                res.append((mm(gs, k, TN), mm(gs, q), mm(pb, gc)))
            gq = jnp.where(lane, res[0][0], res[1][0]) * HEAD_DIM ** (-0.5)
            gk = jnp.where(lane, res[0][1], res[1][1])
            gv = jnp.where(lane, res[0][2], res[1][2])
            gq, gk, gv = gq.astype(bf16), gk.astype(bf16), gv.astype(bf16)
            gp_v[:, pl.ds(at, 128)] = gq
            gp_v[:, pl.ds(at_k, 128)] = gk
            gp_v[:, pl.ds(at_v, 128)] = gv
            gb_o[0:1, pl.ds(at, 128)] = jnp.sum(gq.astype(f32), 0, keepdims=True)
            gb_o[1:2, pl.ds(at, 128)] = jnp.sum(gv.astype(f32), 0, keepdims=True)
        low = pl.ds(rows, rows)
        for k in [mv.go(gp_v, gp_o), mv.go(gp_v.at[low], gt_o)]:
            k.wait()

    S, V = jax.ShapeDtypeStruct, pltpu.VMEM
    return kernel_call(
        body, "attn_bwd", (info, go, gt, w_out, qkv, pt), [SM, ANY, ANY, HBM, HBM, HBM],
        (S((toks, 3 * half), bf16), S((rows, 3 * half), bf16), S((2, half), f32)), (ANY, ANY, VM),
        [V((toks, width), bf16), V((half, width), bf16), V((toks, 3 * half), bf16), V((heads, toks, toks), bf16),
         V((toks, half), bf16), V((toks, 3 * half), bf16)],
        8 + heads, 2 * toks * width * half + 20 * heads * toks * toks * 128, 7 << 20,
    )


def place(j, me, order):
    d = jnp.bitwise_xor(j, me)
    n = len(order)
    p = 0
    for i, k in enumerate(order):
        p = p + (jnp.bitwise_and(jnp.right_shift(d, k), 1) << (n - 1 - i))
    return p


def arranged(v, me, order):
    n = len(order)
    rest = v.shape[1:]
    v = v.reshape((2,) * n + rest)
    for k in range(n):
        ax = n - 1 - k
        v = jnp.where(((me >> k) & 1) == 1, jnp.flip(v, ax), v)
    v = v.transpose([n - 1 - k for k in order] + list(range(n, n + len(rest))))
    return v.reshape((2**n,) + rest)


def own_units(info, l, w_up, chips):
    _, width, ff = w_up.shape
    part = ff // chips // 4
    fo = ff // 4
    strip = 128

    def body(info, w, o_ref, w_v, o_v, sems):
        mv = Mover(sems)
        mv.go(w.at[l], w_v).wait()
        for s in range(4):

            @pl.when(info[3] == s)
            def _():
                def some(r, _):
                    at = pl.ds(pl.multiple_of(r * strip, strip), strip)
                    for i in range(chips):
                        o_v[at, i * part : (i + 1) * part] = w_v[at, (4 * i + s) * part : (4 * i + s + 1) * part]
                    return 0

                lax.fori_loop(0, width // strip, some, 0)

        mv.go(o_v, o_ref).wait()

    S, V = jax.ShapeDtypeStruct, pltpu.VMEM
    return kernel_call(
        body, "own_units", (info, w_up), [SM, HBM], S((width, fo), bf16), ANY,
        [V((width, ff), bf16), V((width, fo), bf16)], 2, 0, 6 << 20,
    )


def ffn_grads(info, l, hs, gs, wu_own, w_down, b_own, small, gbup, gqv, orders, fast):
    rows, width = hs[0].shape[-2:]
    fo = wu_own.shape[1]
    n = len(hs)
    paired = gs is None
    gs = () if paired else tuple(gs)
    m = n + len(gs)
    chips = 2 ** len(orders[0])
    part, unit = width // chips, fo // chips
    split = len(orders) == 2

    def body(*refs):
        info = refs[0]
        if paired:
            hr, gr = [r.at[0] for r in refs[1 : 1 + n]], [r.at[1] for r in refs[1 : 1 + n]]
        else:
            hr, gr = refs[1 : 1 + n], refs[1 + n : 1 + 2 * n]
        wu, wd, b, sm, bup, gqv = refs[1 + m : 7 + m]
        ends = refs[7 + m : 7 + m + 2 * len(orders)] if fast else refs[7 + m : 9 + m]
        h_v, g_v, wu_v, wd_v, act_v, gp_v, *o_vs, sm_v, sems = refs[7 + m + len(ends) :]
        o_v = o_vs[0]
        mv = Mover(sems)
        cu = mv.go(wu, wu_v)
        ch = [mv.go(hr[i], h_v.at[pl.ds(i * rows, rows)]) for i in range(n)]
        if fast:
            cd = []
            for i in range(chips):
                at = pl.multiple_of((4 * i + info[3]) * unit, unit)
                cd.append(mv.go(wd.at[l, pl.ds(at, unit)], wd_v.at[pl.ds(i * unit, unit)]))
        else:
            cd = [mv.go(wd.at[l], wd_v)]
        cg = [mv.go(gr[i], g_v.at[pl.ds(i * rows, rows)]) for i in range(n)]
        cu.wait()
        for i in range(n):
            at = pl.ds(i * rows, rows)
            ch[i].wait()
            u = mm(h_v[at], wu_v[...]) + b[l].astype(f32)
            cdf, slope = phi_parts(u)
            act_v[at] = (u * cdf).astype(bf16)
            if i == 0:
                for k in cd:
                    k.wait()
            cg[i].wait()
            gp_v[at] = (mm(g_v[at], wd_v[...], NT) * slope).astype(bf16)
        up = mm(h_v[...], gp_v[...], TN).astype(bf16)
        if fast:
            for j in range(chips):
                o_v[place(j, info[1], orders[0]), :part] = up[j * part : (j + 1) * part]
            if split:
                halfway = chips // 2
                out = [mv.go(o_v.at[pl.ds(halfway, halfway)], ends[0]), mv.go(o_v.at[pl.ds(0, halfway)], ends[1])]
        else:
            o_v[:width] = up
        down = mm(act_v[...], g_v[...], TN).astype(bf16)
        if fast:
            sm_v[...] = sm[...]
            sm_v[6:8, pl.ds(pl.multiple_of(info[0] * (width // 2), 128), width // 2)] = gqv[...]
            whole = sm_v[...]
            low_v, top = o_vs[-1], 0 if split else part
            for j in range(chips):
                p = place(j, info[1], orders[-1])
                low_v[p, top : top + unit] = down[j * unit : (j + 1) * unit]
                low_v[p, top + unit :] = jnp.concatenate(
                    [
                        jnp.concatenate([whole[:, j * part : (j + 1) * part], jnp.zeros((8, width - part), f32)], 1),
                        jnp.concatenate([bup[:, 4 * j * unit : 4 * (j + 1) * unit], jnp.zeros((1, width - 4 * unit), f32)], 1),
                        jnp.zeros((7, width), f32),
                    ]
                ).astype(bf16)
            halfway = chips // 2
            out = out if split else []
            out += [mv.go(low_v.at[pl.ds(halfway, halfway)], ends[-2]), mv.go(low_v.at[pl.ds(0, halfway)], ends[-1])]
        else:
            o_v[width:] = down
            out = [mv.go(o_v.at[pl.ds(0, width)], ends[0]), mv.go(o_v.at[pl.ds(width, fo)], ends[1])]
        for k in out:
            k.wait()

    S, V = jax.ShapeDtypeStruct, pltpu.VMEM
    tok = V((n * rows, width), bf16)
    hid = V((n * rows, fo), bf16)
    if fast:
        sizes = (part, unit + 16) if split else (part + unit + 16,)
        outs = tuple(S((chips // 2, n_rows, width), bf16) for n_rows in sizes for _ in range(2))
        o_vs = [V((chips, n_rows, width), bf16) for n_rows in sizes]
    else:
        outs = (S((width, fo), bf16), S((fo, width), bf16))
        o_vs = [V((width + fo, width), bf16)]
    got = kernel_call(
        body, "ffn_grads", (info,) + tuple(hs) + gs + (wu_own, w_down, b_own, small, gbup, gqv), [SM] + [ANY] * m + [HBM, HBM] + [VM] * 4,
        outs, (ANY,) * len(outs), [tok, tok, V((width, fo), bf16), V((fo, width), bf16), hid, hid] + o_vs + [V((8, width), f32)],
        2 * n + 6 + chips, 8 * n * rows * width * fo, 8 << 20,
    )
    if fast:
        return [(got[2 * i], got[2 * i + 1]) for i in range(len(orders))]
    zero = jnp.zeros_like(gqv)
    gqv = jnp.where(info[0] == 0, jnp.concatenate([gqv, zero], 1), jnp.concatenate([zero, gqv], 1))
    small = jnp.concatenate([small[:6], gqv]).reshape(8, chips, part).transpose(1, 0, 2)
    small = jnp.concatenate([jnp.pad(small, ((0, 0), (0, 0), (0, width - part))),
                             jnp.pad(gbup.reshape(chips, 1, 4 * unit), ((0, 0), (0, 7), (0, width - 4 * unit)))], 1)
    both = [[got[0].reshape(chips, part, fo)], [got[1].reshape(chips, unit, width), small.astype(bf16)]]
    if not split:
        both = [both[0] + both[1]]
    both = [arranged(jnp.concatenate(v, 1), info[1], order) for v, order in zip(both, orders)]
    return [(v[chips // 2 :], v[: chips // 2]) for v in both]


def proj_grads(info, xo, xt, ctx, got, go, gt, gproj, order, fast):
    rows, width = xo.shape
    half = width // 2
    toks = 2 * rows
    chips = 2 ** len(order)
    part = width // chips

    def body(info, xo, xt, ctx, got, go, gt, gp, *refs):
        outs, (x_v, gp_v, c_v, ga_v, o_v, sems) = refs[:-6], refs[-6:]
        mv = Mover(sems)
        c, me, y = info[0], info[1], info[2]
        top, low = pl.ds(0, rows), pl.ds(rows, rows)
        cols = pl.ds(pl.multiple_of(c * half, 128), half)
        cx = [mv.go(xo, x_v.at[top]), mv.go(xt, x_v.at[low]), mv.go(gp, gp_v)]
        cc = [mv.go(ctx, c_v.at[0]), mv.go(got.at[low], c_v.at[1, top]), mv.go(got.at[top], c_v.at[1, low]),
              mv.go(go.at[:, cols], ga_v.at[top]), mv.go(gt.at[:, cols], ga_v.at[low])]
        for k in cx:
            k.wait()
        for g in range(4):
            if g < 3:
                blocks = [(0, mm(x_v[...], gp_v[:, g * half : (g + 1) * half], TN).astype(bf16))]
            else:
                for k in cc:
                    k.wait()
                blocks = [(c if i == 0 else 1 - c, mm(c_v[i], ga_v[...], TN).astype(bf16)) for i in range(2)]
            at = slice(g % 2 * half, (g % 2 + 1) * half)
            for who, val in blocks:
                if fast:
                    for j in range(val.shape[0] // part):
                        p = place(who * (chips // 2) + j, me, order)
                        o_v[jnp.bitwise_xor(g // 2, y), p, :, at] = val[j * part : (j + 1) * part]
                elif g < 3:
                    o_v[g // 2, :, at] = val
                else:
                    o_v[1, pl.ds(pl.multiple_of(who * half, 128), half), at] = val
        out = [mv.go(o_v.at[1], outs[0]), mv.go(o_v.at[0], outs[1])] if fast else [mv.go(o_v, outs[0])]
        for k in out:
            k.wait()

    S, V = jax.ShapeDtypeStruct, pltpu.VMEM
    shape = (2, chips, part, width) if fast else (2, width, width)
    res = kernel_call(
        body, "proj_grads", (info, xo, xt, ctx, got, go, gt, gproj), [SM] + [ANY] * 7,
        (S(shape[1:], bf16),) * 2 if fast else S(shape, bf16), (ANY, ANY) if fast else ANY,
        [V((toks, width), bf16), V((toks, 3 * half), bf16), V((2, toks, half), bf16), V((toks, half), bf16), V(shape, bf16)],
        10, 2 * toks * width * 4 * half, 6 << 20,
    )
    if fast:
        return res
    v = res.reshape(2, chips, part, width)
    v = jnp.where(info[2] == 1, v[::-1], v)
    return arranged(v[1], info[1], order), arranged(v[0], info[1], order)


def pack(info, ends, part, unit, fast):
    width = ends[0][0].shape[-1]
    hp = part // 2
    if not fast:
        v = jnp.concatenate([add(k[0], g[0]).astype(bf16) for k, g in ends])
        up, low, proj = v[:part].reshape(2, hp, width), v[part : part + unit + 16], v[part + unit + 16 :].reshape(2, hp, width)
        mine, other = pick(up, info[0], 0), pick(up, 1 - info[0], 0)
        return (jnp.concatenate([mine, low, pick(proj, info[0], 0)]), jnp.concatenate([other, low[unit:], pick(proj, 1 - info[0], 0)]))
    n = len(ends)

    def body(info, *refs):
        ks, gs, row_o, col_o = refs[:n], refs[n : 2 * n], refs[2 * n], refs[2 * n + 1]
        k_v, g_v, row_v, col_v, sems = refs[2 * n + 2 :]
        mv = Mover(sems)
        at, come = 0, []
        for k, g in zip(ks, gs):
            now = pl.ds(at, k.shape[1])
            come += [mv.go(k.at[0], k_v.at[now]), mv.go(g.at[0], g_v.at[now])]
            at += k.shape[1]
        for c in come:
            c.wait()
        v = (k_v[...].astype(f32) + g_v[...].astype(f32)).astype(bf16)
        first = info[0] == 0
        lo = part + unit + 16
        up0, up1, pr0, pr1 = v[:hp], v[hp:part], v[lo : lo + hp], v[lo + hp :]
        row_v[:hp] = jnp.where(first, up0, up1)
        row_v[hp : hp + unit + 16] = v[part:lo]
        row_v[hp + unit + 16 :] = jnp.where(first, pr0, pr1)
        col_v[:hp] = jnp.where(first, up1, up0)
        col_v[hp : hp + 16] = v[lo - 16 : lo]
        col_v[hp + 16 :] = jnp.where(first, pr1, pr0)
        for c in [mv.go(col_v, col_o), mv.go(row_v, row_o)]:
            c.wait()

    total = sum(k.shape[1] for k, _ in ends)
    S, V = jax.ShapeDtypeStruct, pltpu.VMEM
    shapes = [(part + unit + 16, width), (part + 16, width)]
    return kernel_call(
        body, "pack", (info,) + tuple(k for k, _ in ends) + tuple(g for _, g in ends), [SM] + [ANY] * (2 * n),
        tuple(S(v, bf16) for v in shapes), (ANY, ANY), [V((total, width), bf16)] * 2 + [V(v, bf16) for v in shapes], 2 * n + 2, 0, 0,
    )


def unpack(info, rounds, part, unit, chips, fast):
    layers = len(rounds)
    width = rounds[0][0].shape[-1]
    hp, half = part // 2, width // 2
    lo = hp + unit + 16
    if not fast:
        res = []
        for own, row, core, diag in rounds:
            def quarters(a, b):
                mine = order_two(info[2], own[a], row[a], 0)
                other = order_two(info[2], core[b], diag[b], 0)
                return order_two(info[0], mine, other, 0)

            up = quarters(slice(0, hp), slice(0, hp)).reshape(2, 2, hp, chips, unit)
            up = up.transpose(2, 3, 0, 1, 4).reshape(hp, 4 * width).astype(f32)
            proj = quarters(slice(lo, lo + hp), slice(hp + 16, part + 16)).reshape(2, 2, hp, 2, half)
            proj = proj.transpose(2, 1, 3, 0, 4).reshape(hp, 4 * width).astype(f32)
            down = order_two(info[2], own[hp : hp + unit], row[hp : hp + unit], 0).reshape(2 * unit, width).astype(f32)
            small = add(own[lo - 16 : lo], row[lo - 16 : lo]) + add(core[hp : hp + 16], diag[hp : hp + 16])
            vecs = pick(small[:8, :part].reshape(8, 2, hp), info[0], 1)
            bup = pick(small[8, : 4 * unit].reshape(2, 2 * unit), info[0], 0)
            res.append((proj[:, : 3 * width], proj[:, 3 * width :], up, down, bup, vecs[6:8]) + tuple(vecs[i] for i in range(6)))
        return tuple(jnp.stack([r[i] for r in res]) for i in range(12))

    def body(info, *refs):
        src, outs = refs[: 4 * layers], refs[4 * layers : 4 * layers + 12]
        big_v, small_v, q_v, d_v, sems = refs[4 * layers + 12 :]
        mv = Mover(sems)
        come = []
        for l in range(layers):
            for i in range(4):
                to = big_v.at[l, i] if i < 2 else small_v.at[l, i - 2]
                come.append(mv.go(src[4 * l + i], to))
        qkv, out, up, down, bup, gqv = outs[:6]
        c, y, share = info[0], info[2], info[3]
        first = c == 0
        for l in range(layers):
            for k in come[4 * l : 4 * l + 4]:
                k.wait()
            diag = 3 - share
            for p, (a, b) in enumerate(((0, 0), (lo, hp + 16))):
                q_v[p, share] = big_v[l, 0, a : a + hp]
                q_v[p, 2 * c + 1 - y] = big_v[l, 1, a : a + hp]
                q_v[p, 2 * (1 - c) + y] = small_v[l, 0, b : b + hp]
                q_v[p, diag] = small_v[l, 1, b : b + hp]
            d_v[y] = big_v[l, 0, hp : hp + unit]
            d_v[1 - y] = big_v[l, 1, hp : hp + unit]
            for q in range(4):
                whole = q_v[0, q].astype(f32)
                for i in range(chips):
                    up[l, :, (4 * i + q) * unit : (4 * i + q + 1) * unit] = whole[:, i * unit : (i + 1) * unit]
                whole = q_v[1, q].astype(f32)
                at = q // 2 * half
                if q % 2 == 0:
                    qkv[l, :, at : at + half] = whole[:, :half]
                    qkv[l, :, width + at : width + at + half] = whole[:, half:]
                else:
                    qkv[l, :, 2 * width + at : 2 * width + at + half] = whole[:, :half]
                    out[l, :, at : at + half] = whole[:, half:]
            for i in range(2):
                down[l, i * unit : (i + 1) * unit] = d_v[i].astype(f32)
            small = (big_v[l, 0, lo - 16 : lo].astype(f32) + big_v[l, 1, lo - 16 : lo].astype(f32)) + (
                small_v[l, 0, hp : hp + 16].astype(f32) + small_v[l, 1, hp : hp + 16].astype(f32))
            vecs = jnp.where(first, small[:8, :hp], small[:8, hp:part])
            bup[l : l + 1] = jnp.where(first, small[8:9, : 2 * unit], small[8:9, 2 * unit : 4 * unit])
            gqv[l] = vecs[6:8]
            for i in range(6):
                outs[6 + i][l : l + 1] = vecs[i : i + 1]

    S, V = jax.ShapeDtypeStruct, pltpu.VMEM
    outs = [(layers, hp, 3 * width), (layers, hp, width), (layers, hp, 4 * width), (layers, 2 * unit, width), (layers, 2 * unit), (layers, 2, hp)]
    outs += [(layers, hp)] * 6
    args = (info,) + tuple(v for r in rounds for v in r)
    return kernel_call(
        body, "unpack", args, [SM] + [ANY] * (4 * layers), tuple(S(v, f32) for v in outs), (VM,) * 12,
        [V((layers, 2, part + unit + 16, width), bf16), V((layers, 2, part + 16, width), bf16), V((2, 4, hp, width), bf16), V((2, unit, width), bf16)],
        4 * layers, 0, 0,
    )


class Wires:
    def __init__(self, batch, seq):
        self.batch, self.seq = batch, seq
        self.chips = batch // 2
        self.bits = self.chips.bit_length() - 1
        where = [(i, j) for i in range(batch) for j in range(seq)]

        def table(move):
            out = []
            for i, j in where:
                p, q = move(i, j)
                out.append((i * seq + j, p * seq + q))
            return out

        self.core = table(lambda i, j: (i ^ 1, j))
        self.row = table(lambda i, j: (i, 1 - j))
        self.diag = table(lambda i, j: (i ^ 1, 1 - j))
        self.turn = table(lambda i, j: (i - i % 2 + j, i % 2))
        self.chip = [table(lambda i, j, k=k: (i ^ (2 << k), j)) for k in range(self.bits)]
        self.b = lax.axis_index("batch")
        self.y = lax.axis_index("seq")
        self.c = self.b % 2

    def swap_core(self, v):
        return lax.ppermute(v, AXES, self.core)

    def swap_row(self, v):
        return lax.ppermute(v, AXES, self.row)

    def swap_diag(self, v):
        return lax.ppermute(v, AXES, self.diag)

    def swap_turn(self, v):
        return lax.ppermute(v, AXES, self.turn)

    def swap_chip(self, v, k):
        return lax.ppermute(v, AXES, self.chip[k])

    def bit(self, k):
        return (self.b >> (k + 1)) & 1


def pick(v, idx, axis):
    return lax.dynamic_index_in_dim(v, idx, axis, keepdims=False)


def add(a, b):
    return a.astype(f32) + b.astype(f32)


def order_two(flag, mine, got, axis):
    return jnp.stack([jnp.where(flag == 0, mine, got), jnp.where(flag == 0, got, mine)], axis)


class Clock:
    def __init__(self):
        self.now, self.free, self.alive = 0.0, {}, []

    def busy(self, link, us):
        begin = max(self.now, self.free.get(link, 0.0))
        self.free[link] = begin + us
        return begin + us

    def work(self, us):
        self.now += us

    def catch_up(self):
        for s in sorted(self.alive, key=lambda s: s.ready):
            if s.ready <= self.now:
                s.step()

    def drain(self):
        while self.alive:
            min(self.alive, key=lambda s: s.ready).step()


class Stream:
    def __init__(self, wires, clock, send, keep, order, row_first):
        self.wires, self.clock, self.keep, self.end = wires, clock, keep, None
        self.todo = list(order)
        clock.alive.append(self)
        self.send(send, row_first)

    def send(self, v, row=False):
        us = v.size * 2 / 1e6 * 22.0
        if row:
            self.got, link = self.wires.swap_row(v), "y"
        else:
            k = self.todo.pop(0)
            self.got = self.wires.swap_chip(v, k)
            link = "x" if k == 0 else "z"
            us *= max(1, 1 << (k - 1)) if k else 1
        self.clock.work(1.4)
        self.ready = self.clock.busy(link, us) + 2.0

    def step(self):
        clock = self.clock
        clock.now = max(clock.now, self.ready)
        if not self.todo:
            self.end = (self.keep, self.got)
            clock.alive.remove(self)
            return
        clock.work(1.2 + self.keep.size * 2 / 1e6)
        send, self.keep = merge(self.keep, self.got)
        self.send(send)


def local(inputs, out_grad, masked, w_qkv, bias_qv, w_out, bias_out, gain_one, shift_one, w_up, bias_up, w_down, bias_down, gain_two, shift_two):
    wires = Wires(lax.axis_size("batch"), lax.axis_size("seq"))
    layers, width, ff = w_up.shape
    half = width // 2
    chips, bits = wires.chips, wires.bits
    fo, unit, part = ff // 4, ff // chips // 4, width // chips
    fast = part % 32 == 0
    share = wires.c * 2 + wires.y
    info = jnp.stack([wires.c, wires.b // 2, wires.y, share]).astype(jnp.int32)
    rows = inputs.shape[1]
    ROW.extra = []
    xb = wires.swap_turn(inputs[0])
    b_own = pick(bias_up.reshape(layers, chips, 4, unit), share, 2).reshape(layers, 1, fo)
    if fast:
        wu_own, wd_own = [own_units(info, l, w_up, chips) for l in range(layers)], w_down
    else:
        wu_own = pick(w_up.reshape(layers, width, chips, 4, unit), share, 3).reshape(layers, width, fo)
        wd_own = pick(w_down.reshape(layers, chips, 4, unit, width), share, 2).reshape(layers, fo, width)
    x = xb
    saved, outs, hs = [], [], []
    tail = (w_out, bias_out, gain_one, shift_one, w_up, bias_up, w_down, bias_down, gain_two, shift_two)
    clock = Clock()
    for l in range(layers):
        xt = wires.swap_core(xb)
        qkv, pt, ctx = attn_fwd(info, l, xb, xt, w_qkv, bias_qv)
        if l == 0:
            gy = wires.swap_turn(masked_grad(out_grad[0], masked))
        got = wires.swap_core(ctx)
        last = l == layers - 1
        if last:
            yb, pair, ga, gm, small, gbup = ffn_fwd(info, l, x, ctx, got, tail, gy)
            saved.append((xb, xt, qkv, pt, ctx, got))
            turned_back = (pair, ga, gm, small, gbup)
        else:
            hb, dg, mixed, x, yb = ffn_fwd(info, l, x, ctx, got, tail)
            hy = wires.swap_row(hb)
            hs.append((hb, hy, wires.swap_core(hb), wires.swap_core(hy)))
            saved.append((xb, xt, qkv, pt, ctx, got, dg, mixed, x))
        outs.append(wires.swap_turn(yb)[None])
        xb = yb
    low = list(range(bits))
    turned = low[1:2] + low[:1] + low[2:]
    plan = [((low, turned), low)] + [((turned,), low)] * (layers - 1)
    streams = [None] * layers
    for l in reversed(range(layers)):
        xb, xt, qkv, pt, ctx, got = saved[l][:6]
        if l == layers - 1:
            pair, ga, gm, small, gbup = turned_back
            gat = wires.swap_core(ga)
            py = wires.swap_row(pair)
            both = (pair, py, wires.swap_core(pair), wires.swap_core(py)), None
        else:
            dg, mixed, summed = saved[l][6:]
            gf, ga, gm, small, gbup = ffn_bwd(info, l, flow, summed, mixed, dg, (w_up, w_down, gain_one, gain_two))
            gat = wires.swap_core(ga)
            gfy = wires.swap_row(gf)
            both = hs[l], (gf, gfy, wires.swap_core(gf), wires.swap_core(gfy))
        gproj, gptail, gqv = attn_bwd(info, l, ga, gat, w_out, qkv, pt)
        if l == layers - 1:
            ROW.before_next(*hs[-1], *outs)
        flow = (gm, gproj, wires.swap_core(gptail), w_qkv)
        clock.work(28.0 if l < layers - 1 else 0.0)
        clock.catch_up()
        send, keep = proj_grads(info, xb, xt, ctx, got, ga, gat, gproj, plan[l][1], fast)
        clock.work(4.5)
        ps = [Stream(wires, clock, send, keep, plan[l][1], True)]
        clock.catch_up()
        res = ffn_grads(info, l, *both, wu_own[l], wd_own, b_own, small, gbup, gqv, plan[l][0], fast)
        clock.work(10.5)
        fs = [Stream(wires, clock, s, k, order, False) for (s, k), order in zip(res, plan[l][0])]
        clock.catch_up()
        streams[l] = fs + ps
    end = chain_end(info, 0, flow)
    clock.work(5.5)
    grad_in = wires.swap_turn(end)[None]
    rounds = [None] * layers
    while not all(rounds):
        if clock.alive:
            min(clock.alive, key=lambda s: s.ready).step()
        for l in range(layers):
            if rounds[l] is None and all(s.end for s in streams[l]):
                row, col = pack(info, [s.end for s in streams[l]], part, unit, fast)
                rounds[l] = (row, wires.swap_row(row), wires.swap_core(col), wires.swap_diag(col))
                clock.work(5.0)
                clock.busy("y", 11.0)
    qkv, out, up, down, bup, gqv, gdn, gg2, gs2, gg1, gs1, gbo = unpack(info, rounds, part, unit, chips, fast)
    return (outs[0], outs[-1], grad_in, qkv, gqv, out, gbo, gg1, gs1, up, bup, down, gdn, gg2, gs2)


def solution(mesh):
    tok = P("batch", "seq", None)
    in_specs = (tok, tok, P("batch", "seq")) + (P(),) * 12
    mat, vec = P(None, "batch", None), P(None, "batch")
    out_specs = (tok, tok, tok, mat, P(None, None, "batch"), mat, vec, vec, vec, mat, vec, mat, vec, vec, vec)
    return jax.shard_map(local, mesh=mesh, in_specs=in_specs, out_specs=out_specs, check_vma=False)
```

```python
import math

import jax
import jax.numpy as jnp
from jax import lax
from jax.experimental import pallas as pl
from jax.experimental.pallas import tpu as pltpu
from jax.sharding import PartitionSpec as P

HEAD_DIM = 64
AXES = ("batch", "seq")
norm_eps = 1e-06
f32 = jnp.float32
bf16 = jnp.bfloat16
ANY = pl.BlockSpec(memory_space=pl.ANY)
HBM = pl.BlockSpec(memory_space=pltpu.HBM)
VM = pl.BlockSpec(memory_space=pltpu.VMEM)
SM = pl.BlockSpec(memory_space=pltpu.SMEM)
ROOT_HALF = 0.7071067811865476
INV_ROOT_TAU = 0.3989422804014327
TAKES = {"own_units": 24.0, "attn_fwd": 7.5, "ffn_fwd": 9.0, "ffn_turn": 13.0, "ffn_bwd": 12.0, "attn_bwd": 7.5, "ffn_grads": 10.5, "proj_grads": 18, "chain_end": 4.5, "merge": 7.0, "masked_grad": 2.0, "pack": 3.0, "unpack": 5.0}
PACE = 0.5


def mm(a, b, dims=((1,), (0,))):
    return lax.dot_general(a, b, (dims, ((), ())), preferred_element_type=f32)


NT = ((1,), (1,))
TN = ((0,), (0,))


class Mover:
    def __init__(self, sems):
        self.sems, self.used = sems, 0

    def go(self, src, dst):
        copy = pltpu.make_async_copy(src, dst, self.sems.at[self.used])
        self.used += 1
        copy.start()
        return copy


class Row:
    def __init__(self):
        self.extra = []

    def before_next(self, *values):
        self.extra.extend(values)


ROW = Row()


def kernel_call(body, name, args, specs, outs, out_specs, scratch, sems, flops, moved):
    extra = tuple(ROW.extra)
    n, m = len(args), len(args) + len(extra)
    held = sum(math.prod(v.shape) * jnp.dtype(v.dtype).itemsize for v in scratch)
    limit = held + ((2 << 20) if name == "merge" else (12 << 20))
    args = tuple(
        pltpu.with_memory_space_constraint(a, pltpu.HBM) if spec is HBM else a for a, spec in zip(args, specs)
    )
    out = pl.pallas_call(
        lambda *refs: body(*refs[:n], *refs[m:]),
        name=name,
        out_shape=outs,
        in_specs=specs + [ANY] * len(extra),
        out_specs=out_specs,
        scratch_shapes=list(scratch) + [pltpu.SemaphoreType.DMA((sems,))],
        compiler_params=pltpu.CompilerParams(vmem_limit_bytes=limit),
        cost_estimate=pl.CostEstimate(flops=int(PACE * TAKES[name] * 1.15e9), bytes_accessed=moved, transcendentals=0),
    )(*args, *extra)
    ROW.extra = [out[0] if isinstance(out, (tuple, list)) else out]
    return out


def merge(keep, got):
    n = max(keep.shape[0] // 2, 1)
    rest = keep.shape[1:]
    parts = keep.shape[0] // n

    def body(k, g, *refs):
        outs, (k_v, g_v, sems) = refs[:parts], refs[parts:]
        mv = Mover(sems)
        at = [pl.ds((parts - 1 - i) * n, n) for i in range(parts)]
        come = [(mv.go(k.at[a], k_v.at[a]), mv.go(g.at[a], g_v.at[a])) for a in at]
        gone = []
        for i, a in enumerate(at):
            for c in come[i]:
                c.wait()

            def one(j, _):
                j = j + (parts - 1 - i) * n
                k_v[j] = (k_v[j].astype(f32) + g_v[j].astype(f32)).astype(bf16)
                return 0

            lax.fori_loop(0, n, one, 0)
            gone.append(mv.go(k_v.at[a], outs[i]))
        for c in gone:
            c.wait()

    outs = (jax.ShapeDtypeStruct((n,) + rest, bf16),) * parts
    return kernel_call(body, "merge", (keep, got), [ANY, ANY], outs, (ANY,) * parts, [pltpu.VMEM(keep.shape, bf16)] * 2, 3 * parts, 5 * 10**9, 0)


def normed(z):
    center = z - jnp.mean(z, -1, keepdims=True)
    rstd = lax.rsqrt(jnp.mean(center * center, -1, keepdims=True) + norm_eps)
    return center * rstd, rstd


def norm_back(g, z, gain):
    xhat, rstd = normed(z)
    gx = g * gain
    m1 = jnp.mean(gx, -1, keepdims=True)
    m2 = jnp.mean(gx * xhat, -1, keepdims=True)
    return rstd * (gx - m1 - xhat * m2), g * xhat


def phi_parts(u):
    cdf = 0.5 * (1.0 + lax.erf(u * ROOT_HALF))
    return cdf, cdf + u * (jnp.exp(-0.5 * u * u) * INV_ROOT_TAU)


def masked_grad(grad, masked):
    rows, width = grad.shape

    def body(g, m, o, sems):
        col = jnp.broadcast_to(m[...].astype(f32), (8, rows)).T[:, :1]
        o[...] = (g[...].astype(f32) * col).astype(bf16)

    return kernel_call(body, "masked_grad", (grad, masked), [VM, VM], jax.ShapeDtypeStruct((rows, width), bf16), VM, [], 1, 0, 0)


def attn_fwd(info, l, xo, xt, w_qkv, bias_qv):
    rows, width = xo.shape
    half = width // 2
    heads = half // HEAD_DIM
    toks = 2 * rows

    def body(info, xo, xt, w, bias, qkv_o, pt_o, ctx_o, x_v, w_v, qkv_v, pt_v, ctx_v, sems):
        mv = Mover(sems)
        c = info[0]
        cx = [mv.go(xo, x_v.at[pl.ds(0, rows)]), mv.go(xt, x_v.at[pl.ds(rows, rows)])]
        cw = []
        for p in range(3):
            at = pl.multiple_of(p * width + c * half, 128)
            cw.append(mv.go(w.at[l, :, pl.ds(at, half)], w_v.at[p]))
        for k in cx:
            k.wait()
        at = pl.multiple_of(c * half, 128)
        for p in range(3):
            cw[p].wait()
            val = mm(x_v[...], w_v[p])
            if p != 1:
                val = val + bias[l, pl.ds(p // 2, 1), pl.ds(at, half)].astype(f32)
            val = val.astype(bf16)
            if p == 0:
                val = (val.astype(f32) * HEAD_DIM ** (-0.5)).astype(bf16)
            qkv_v[:, p * half : (p + 1) * half] = val
        out = [mv.go(qkv_v, qkv_o)]
        lane = lax.broadcasted_iota(jnp.int32, (toks, 2 * HEAD_DIM), 1) < HEAD_DIM

        for i in range(heads // 2):
            at = i * 2 * HEAD_DIM
            q = qkv_v[:, at : at + 128]
            k = qkv_v[:, half + at : half + at + 128]
            v = qkv_v[:, 2 * half + at : 2 * half + at + 128]
            both = []
            for h in range(2):
                qm = jnp.where(lane == (h == 0), q, jnp.zeros_like(q))
                st = mm(k, qm, NT)
                top = jnp.max(st, 0, keepdims=True)
                e = jnp.exp(st - top)
                p = (e / jnp.sum(e, 0, keepdims=True)).astype(bf16)
                pt_v[2 * i + h] = p
                both.append(mm(p, v, TN))
            ctx_v[:, at : at + 128] = jnp.where(lane, both[0], both[1]).astype(bf16)
            now = pl.ds(2 * i, 2)
            out.append(mv.go(pt_v.at[now], pt_o.at[now]))
        out.append(mv.go(ctx_v, ctx_o))
        for k in out:
            k.wait()

    S = jax.ShapeDtypeStruct
    outs = (pltpu.HBM((toks, 3 * half), bf16), pltpu.HBM((heads, toks, toks), bf16), S((toks, half), bf16))
    return kernel_call(
        body, "attn_fwd", (info, xo, xt, w_qkv, bias_qv), [SM, ANY, ANY, HBM, VM], outs, (ANY,) * 3,
        [pltpu.VMEM((toks, width), bf16), pltpu.VMEM((3, width, half), bf16), pltpu.VMEM((toks, 3 * half), bf16),
         pltpu.VMEM((heads, toks, toks), bf16), pltpu.VMEM((toks, half), bf16)],
        8 + heads // 2, 2 * toks * width * 3 * half + 8 * heads * toks * toks * 128, 8 << 20,
    )


def ffn_fwd(info, l, x, ctx, got, weights, gy=None, cut=6):
    w_out, bias_out, gain_one, shift_one, w_up, bias_up, w_down, bias_down, gain_two, shift_two = weights
    rows, width = x.shape
    half = width // 2
    ff = w_up.shape[2]
    step = ff // cut
    turn = gy is not None

    def body(info, x, ctx, got, wo, bo, g1, s1, wu, bu, wd, bd, g2, s2, *refs):
        if turn:
            gy_r, yb_o, pair_o, ga_o, gm_o, small_o, gbup_o = refs[:7]
            x_v, c_v, wo_v, wu_v, wd_v, hb_v, dg_v, mixed_v, yb_v, low_v, gf_v, gm_v, sems = refs[7:]
        else:
            hb_o, dg_o, mixed_o, summed_o, yb_o = refs[:5]
            x_v, c_v, wo_v, wu_v, wd_v, hb_v, dg_v, mixed_v, yb_v, sems = refs[5:]
        mv = Mover(sems)
        c = info[0]
        cx = mv.go(x, hb_v if l == 0 else x_v)
        first = [mv.go(ctx.at[pl.ds(0, rows)], c_v.at[0])]
        at = [pl.multiple_of(c * half, 128), pl.multiple_of((1 - c) * half, 128)]
        first += [mv.go(wo.at[l, pl.ds(at[i], half)], wo_v.at[i]) for i in range(2)]
        first += [mv.go(got.at[pl.ds(rows, rows)], c_v.at[1])]
        cu, cd = [], []
        for j in range(cut):
            cu.append(mv.go(wu.at[l, :, pl.ds(j * step, step)], wu_v.at[j]))
            cd.append(mv.go(wd.at[l, pl.ds(j * step, step)], wd_v.at[j]))
        if turn:
            cg = mv.go(gy_r, low_v)
        cx.wait()
        if l == 0:
            xin = hb_v[...].astype(f32)
        else:
            xin = normed(x_v[...])[0] * g2[l - 1 : l].astype(f32) + s2[l - 1 : l].astype(f32)
        for k in first:
            k.wait()
        mixed = xin + mm(c_v[0], wo_v[0]) + mm(c_v[1], wo_v[1]) + bo[l : l + 1].astype(f32)
        mixed_v[...] = mixed
        out = [] if turn else [mv.go(mixed_v, mixed_o)]
        hid = normed(mixed)[0] * g1[l : l + 1].astype(f32) + s1[l : l + 1].astype(f32)
        x_v[...] = hid
        hb_v[...] = hid.astype(bf16)
        out.append(mv.go(hb_v, pair_o.at[0] if turn else hb_o))
        acc = None
        for j in range(cut):
            cols = slice(j * step, (j + 1) * step)
            cu[j].wait()
            u = mm(hb_v[...], wu_v[j]) + bu[l : l + 1, cols].astype(f32)
            cdf, slope = phi_parts(u)
            dg_v[j] = slope.astype(dg_v.dtype)
            if not turn:
                out.append(mv.go(dg_v.at[j], dg_o.at[:, pl.ds(j * step, step)]))
            cd[j].wait()
            part = mm((u * cdf).astype(bf16), wd_v[j])
            acc = part if acc is None else acc + part
        summed = x_v[...] + acc + bd[l : l + 1].astype(f32)
        x_v[...] = summed
        if not turn:
            out.append(mv.go(x_v, summed_o))
        gain = g2[l : l + 1].astype(f32)
        y = normed(summed)[0] * gain + s2[l : l + 1].astype(f32)
        yb_v[...] = y.astype(bf16)
        out.append(mv.go(yb_v, yb_o))
        if turn:
            cg.wait()
            gy = low_v[...].astype(f32)
            gsum, gterm = norm_back(gy, x_v[...], gain)
            small_o[1:2] = jnp.sum(gterm, 0, keepdims=True)
            small_o[2:3] = jnp.sum(gy, 0, keepdims=True)
            gf = gsum.astype(bf16)
            gf_v[...] = gf
            small_o[0:1] = jnp.sum(gf.astype(f32), 0, keepdims=True)
            out.append(mv.go(gf_v, pair_o.at[1]))
            gm_v[...] = gsum
            acc = None
            for j in range(cut):
                gpre = (mm(gf_v[...], wd_v[j], NT) * dg_v[j].astype(f32)).astype(bf16)
                gbup_o[:, j * step : (j + 1) * step] = jnp.sum(gpre.astype(f32), 0, keepdims=True)
                part = mm(gpre, wu_v[j], NT)
                acc = part if acc is None else acc + part
            ghid = gm_v[...] + acc
            gmix, gterm = norm_back(ghid, mixed_v[...], g1[l : l + 1].astype(f32))
            ga = gmix.astype(bf16)
            low_v[...] = ga
            out.append(mv.go(low_v, ga_o))
            gm_v[...] = gmix
            out.append(mv.go(gm_v, gm_o))
            small_o[3:4] = jnp.sum(gterm, 0, keepdims=True)
            small_o[4:5] = jnp.sum(ghid, 0, keepdims=True)
            small_o[5:6] = jnp.sum(ga.astype(f32), 0, keepdims=True)
            small_o[6:8] = jnp.zeros((2, width), f32)
        for k in out:
            k.wait()

    S, V = jax.ShapeDtypeStruct, pltpu.VMEM
    full, low = S((rows, width), f32), S((rows, width), bf16)
    scratch = [V((rows, width), f32), V((2, rows, half), bf16), V((2, half, width), bf16), V((cut, width, step), bf16),
               V((cut, step, width), bf16), V((rows, width), bf16), V((cut, rows, step), bf16), V((rows, width), f32),
               V((rows, width), bf16)]
    args = (info, x, ctx, got, w_out, bias_out, gain_one, shift_one, w_up, bias_up, w_down, bias_down, gain_two, shift_two)
    specs = [SM, ANY, ANY, ANY, HBM, VM, VM, VM, HBM, VM, HBM, VM, VM, VM]
    if turn:
        outs = (low, S((2, rows, width), bf16), low, full, S((8, width), f32), S((1, ff), f32))
        out_specs = (ANY, ANY, ANY, ANY, VM, VM)
        scratch += [V((rows, width), bf16), V((rows, width), bf16), V((rows, width), f32)]
        args, specs = args + (gy,), specs + [ANY]
    else:
        outs, out_specs = (low, pltpu.HBM((rows, ff), bf16), pltpu.HBM((rows, width), f32), full, low), (ANY,) * 5
    return kernel_call(
        body, "ffn_turn" if turn else "ffn_fwd", args, specs, outs, out_specs, scratch, 14 + 3 * cut, 0, 12 << 20,
    )


def ffn_bwd(info, l, flow, summed, mixed, dg, weights, cut=6):
    w_up, w_down, gain_one, gain_two = weights
    rows, width = summed.shape
    half = width // 2
    ff = w_up.shape[2]
    step = ff // cut
    chained = len(flow) > 1

    def body(*refs):
        info = refs[0]
        fl = refs[1 : 1 + len(flow)]
        (sm, mi, dgr, wu, wd, g1, g2, gf_o, ga_o, gm_o, small_o, gbup_o,
         gy_v, sm_v, mi_v, dg_v, wu_v, wd_v, gf_v, ga_v, gm_v) = refs[1 + len(flow) : 22 + len(flow)]
        sems = refs[-1]
        mv = Mover(sems)
        if chained:
            gp_v, wq_v = refs[22 + len(flow) : 24 + len(flow)]
            c = info[0]
            fc = [mv.go(fl[0], gy_v), mv.go(fl[1].at[pl.ds(0, rows)], gp_v.at[0])]
            wq = []
            for i in range(2):
                who = c if i == 0 else 1 - c
                for p in range(3):
                    at = pl.multiple_of(p * width + who * half, 128)
                    wq.append(mv.go(fl[3].at[l + 1, :, pl.ds(at, half)], wq_v.at[i, p]))
            fc.append(mv.go(fl[2], gp_v.at[1]))
        else:
            fc = [mv.go(fl[0], gf_v)]
        fc += [mv.go(sm, sm_v)]
        cd, cu, cg = [], [], []
        for j in range(cut):
            cols = pl.ds(j * step, step)
            cd.append(mv.go(wd.at[l, cols], wd_v.at[j]))
            cg.append(mv.go(dgr.at[:, cols], dg_v.at[j]))
            cu.append(mv.go(wu.at[l, :, cols], wu_v.at[j]))
        cm = mv.go(mi, mi_v)
        for k in fc:
            k.wait()
        if chained:
            gy = gy_v[...]
            for i in range(2):
                for p in range(3):
                    wq[3 * i + p].wait()
                    gy = gy + mm(gp_v[i, :, p * half : (p + 1) * half], wq_v[i, p], NT)
        else:
            gy = gf_v[...].astype(f32)
        gsum, gterm = norm_back(gy, sm_v[...], g2[pl.ds(l, 1)].astype(f32))
        small_o[1:2] = jnp.sum(gterm, 0, keepdims=True)
        small_o[2:3] = jnp.sum(gy, 0, keepdims=True)
        gf = gsum.astype(bf16)
        gf_v[...] = gf
        small_o[0:1] = jnp.sum(gf.astype(f32), 0, keepdims=True)
        out = [mv.go(gf_v, gf_o)]
        gm_v[...] = gsum
        acc = None
        for j in range(cut):
            cd[j].wait()
            cg[j].wait()
            gpre = (mm(gf_v[...], wd_v[j], NT) * dg_v[j].astype(f32)).astype(bf16)
            gbup_o[:, j * step : (j + 1) * step] = jnp.sum(gpre.astype(f32), 0, keepdims=True)
            cu[j].wait()
            part = mm(gpre, wu_v[j], NT)
            acc = part if acc is None else acc + part
        ghid = gm_v[...] + acc
        cm.wait()
        gmix, gterm = norm_back(ghid, mi_v[...], g1[pl.ds(l, 1)].astype(f32))
        ga = gmix.astype(bf16)
        ga_v[...] = ga
        out.append(mv.go(ga_v, ga_o))
        gm_v[...] = gmix
        out.append(mv.go(gm_v, gm_o))
        small_o[3:4] = jnp.sum(gterm, 0, keepdims=True)
        small_o[4:5] = jnp.sum(ghid, 0, keepdims=True)
        small_o[5:6] = jnp.sum(ga.astype(f32), 0, keepdims=True)
        small_o[6:8] = jnp.zeros((2, width), f32)
        for k in out:
            k.wait()

    S, V = jax.ShapeDtypeStruct, pltpu.VMEM
    low = S((rows, width), bf16)
    outs = (low, low, S((rows, width), f32), S((8, width), f32), S((1, ff), f32))
    scratch = [V((rows, width), f32), V((rows, width), f32), V((rows, width), f32), V((cut, rows, step), bf16),
               V((cut, width, step), bf16), V((cut, step, width), bf16), V((rows, width), bf16), V((rows, width), bf16),
               V((rows, width), f32)]
    if chained:
        scratch += [V((2, rows, 3 * half), bf16), V((2, 3, width, half), bf16)]
    return kernel_call(
        body, "ffn_bwd", (info,) + tuple(flow) + (summed, mixed, dg, w_up, w_down, gain_one, gain_two),
        [SM] + [ANY, ANY, ANY, HBM][: len(flow)] + [ANY, HBM, HBM, HBM, HBM, VM, VM], outs, (ANY, ANY, ANY, VM, VM), scratch,
        15 + 3 * cut, 2 * rows * width * (2 * ff + (3 * width if chained else 0)), 15 << 20,
    )


def chain_end(info, l, flow):
    gmix, gproj, got, w_qkv = flow
    rows, width = gmix.shape
    half = width // 2

    def body(info, gm, gp, gt, w, o_ref, gy_v, gp_v, wq_v, o_v, sems):
        mv = Mover(sems)
        c = info[0]
        wq = []
        fc = [mv.go(gm, gy_v), mv.go(gp.at[pl.ds(0, rows)], gp_v.at[0]), mv.go(gt, gp_v.at[1])]
        for i in range(2):
            who = c if i == 0 else 1 - c
            for p in range(3):
                at = pl.multiple_of(p * width + who * half, 128)
                wq.append(mv.go(w.at[l, :, pl.ds(at, half)], wq_v.at[i, p]))
        for k in fc:
            k.wait()
        gy = gy_v[...]
        for i in range(2):
            for p in range(3):
                wq[3 * i + p].wait()
                gy = gy + mm(gp_v[i, :, p * half : (p + 1) * half], wq_v[i, p], NT)
        o_v[...] = gy.astype(bf16)
        k = mv.go(o_v, o_ref)
        k.wait()

    S, V = jax.ShapeDtypeStruct, pltpu.VMEM
    return kernel_call(
        body, "chain_end", (info,) + tuple(flow), [SM, ANY, ANY, ANY, HBM], S((rows, width), bf16), ANY,
        [V((rows, width), f32), V((2, rows, 3 * half), bf16), V((2, 3, width, half), bf16), V((rows, width), bf16)],
        10, 2 * rows * width * 3 * width, 5 << 20,
    )


def attn_bwd(info, l, go, gt, w_out, qkv, pt):
    rows, width = go.shape
    half = width // 2
    heads = half // HEAD_DIM
    toks = 2 * rows

    def body(info, go, gt, wo, qkv, pt, gp_o, gt_o, gb_o, ga_v, wo_v, qkv_v, pt_v, gc_v, gp_v, sems):
        mv = Mover(sems)
        c = info[0]
        at = pl.multiple_of(c * half, 128)
        fc = [mv.go(wo.at[l, pl.ds(at, half)], wo_v), mv.go(go, ga_v.at[pl.ds(0, rows)]), mv.go(gt, ga_v.at[pl.ds(rows, rows)])]
        cq = mv.go(qkv, qkv_v)
        cp = [mv.go(pt.at[pl.ds(2 * i, 2)], pt_v.at[pl.ds(2 * i, 2)]) for i in range(heads // 2)]
        for k in fc:
            k.wait()
        gc_v[...] = mm(ga_v[...], wo_v[...], NT).astype(bf16)
        cq.wait()
        lane = lax.broadcasted_iota(jnp.int32, (toks, 2 * HEAD_DIM), 1) < HEAD_DIM

        for i in range(heads // 2):
            cp[i].wait()
            at = i * 2 * HEAD_DIM
            at_k, at_v = half + at, 2 * half + at
            q = qkv_v[:, pl.ds(at, 128)]
            k = qkv_v[:, pl.ds(at_k, 128)]
            v = qkv_v[:, pl.ds(at_v, 128)]
            gc = gc_v[:, pl.ds(at, 128)]
            res = []
            for h in range(2):
                gm = jnp.where(lane == (h == 0), gc, jnp.zeros_like(gc))
                pb = pt_v[2 * i + h]
                t = mm(v, gm, NT)
                p = pb.astype(f32)
                inner = jnp.sum(p * t, 0, keepdims=True)
                gs = (p * (t - inner)).astype(bf16)
                res.append((mm(gs, k, TN), mm(gs, q), mm(pb, gc)))
            gq = jnp.where(lane, res[0][0], res[1][0]) * HEAD_DIM ** (-0.5)
            gk = jnp.where(lane, res[0][1], res[1][1])
            gv = jnp.where(lane, res[0][2], res[1][2])
            gq, gk, gv = gq.astype(bf16), gk.astype(bf16), gv.astype(bf16)
            gp_v[:, pl.ds(at, 128)] = gq
            gp_v[:, pl.ds(at_k, 128)] = gk
            gp_v[:, pl.ds(at_v, 128)] = gv
            gb_o[0:1, pl.ds(at, 128)] = jnp.sum(gq.astype(f32), 0, keepdims=True)
            gb_o[1:2, pl.ds(at, 128)] = jnp.sum(gv.astype(f32), 0, keepdims=True)
        low = pl.ds(rows, rows)
        for k in [mv.go(gp_v, gp_o), mv.go(gp_v.at[low], gt_o)]:
            k.wait()

    S, V = jax.ShapeDtypeStruct, pltpu.VMEM
    return kernel_call(
        body, "attn_bwd", (info, go, gt, w_out, qkv, pt), [SM, ANY, ANY, HBM, HBM, HBM],
        (S((toks, 3 * half), bf16), S((rows, 3 * half), bf16), S((2, half), f32)), (ANY, ANY, VM),
        [V((toks, width), bf16), V((half, width), bf16), V((toks, 3 * half), bf16), V((heads, toks, toks), bf16),
         V((toks, half), bf16), V((toks, 3 * half), bf16)],
        8 + heads, 2 * toks * width * half + 20 * heads * toks * toks * 128, 7 << 20,
    )


def place(j, me, order):
    d = jnp.bitwise_xor(j, me)
    n = len(order)
    p = 0
    for i, k in enumerate(order):
        p = p + (jnp.bitwise_and(jnp.right_shift(d, k), 1) << (n - 1 - i))
    return p


def arranged(v, me, order):
    n = len(order)
    rest = v.shape[1:]
    v = v.reshape((2,) * n + rest)
    for k in range(n):
        ax = n - 1 - k
        v = jnp.where(((me >> k) & 1) == 1, jnp.flip(v, ax), v)
    v = v.transpose([n - 1 - k for k in order] + list(range(n, n + len(rest))))
    return v.reshape((2**n,) + rest)


def own_units(info, l, w_up, chips):
    _, width, ff = w_up.shape
    part = ff // chips // 4
    fo = ff // 4
    strip = 128

    def body(info, w, o_ref, w_v, o_v, sems):
        mv = Mover(sems)
        mv.go(w.at[l], w_v).wait()
        for s in range(4):

            @pl.when(info[3] == s)
            def _():
                def some(r, _):
                    at = pl.ds(pl.multiple_of(r * strip, strip), strip)
                    for i in range(chips):
                        o_v[at, i * part : (i + 1) * part] = w_v[at, (4 * i + s) * part : (4 * i + s + 1) * part]
                    return 0

                lax.fori_loop(0, width // strip, some, 0)

        mv.go(o_v, o_ref).wait()

    S, V = jax.ShapeDtypeStruct, pltpu.VMEM
    return kernel_call(
        body, "own_units", (info, w_up), [SM, HBM], S((width, fo), bf16), ANY,
        [V((width, ff), bf16), V((width, fo), bf16)], 2, 0, 6 << 20,
    )


def ffn_grads(info, l, hs, gs, wu_own, w_down, b_own, small, gbup, gqv, orders, fast):
    rows, width = hs[0].shape[-2:]
    fo = wu_own.shape[1]
    n = len(hs)
    paired = gs is None
    gs = () if paired else tuple(gs)
    m = n + len(gs)
    chips = 2 ** len(orders[0])
    part, unit = width // chips, fo // chips
    split = len(orders) == 2

    def body(*refs):
        info = refs[0]
        if paired:
            hr, gr = [r.at[0] for r in refs[1 : 1 + n]], [r.at[1] for r in refs[1 : 1 + n]]
        else:
            hr, gr = refs[1 : 1 + n], refs[1 + n : 1 + 2 * n]
        wu, wd, b, sm, bup, gqv = refs[1 + m : 7 + m]
        ends = refs[7 + m : 7 + m + 2 * len(orders)] if fast else refs[7 + m : 9 + m]
        h_v, g_v, wu_v, wd_v, act_v, gp_v, *o_vs, sm_v, sems = refs[7 + m + len(ends) :]
        o_v = o_vs[0]
        mv = Mover(sems)
        cu = mv.go(wu, wu_v)
        ch = [mv.go(hr[i], h_v.at[pl.ds(i * rows, rows)]) for i in range(n)]
        if fast:
            cd = []
            for i in range(chips):
                at = pl.multiple_of((4 * i + info[3]) * unit, unit)
                cd.append(mv.go(wd.at[l, pl.ds(at, unit)], wd_v.at[pl.ds(i * unit, unit)]))
        else:
            cd = [mv.go(wd.at[l], wd_v)]
        cg = [mv.go(gr[i], g_v.at[pl.ds(i * rows, rows)]) for i in range(n)]
        cu.wait()
        for i in range(n):
            at = pl.ds(i * rows, rows)
            ch[i].wait()
            u = mm(h_v[at], wu_v[...]) + b[l].astype(f32)
            cdf, slope = phi_parts(u)
            act_v[at] = (u * cdf).astype(bf16)
            if i == 0:
                for k in cd:
                    k.wait()
            cg[i].wait()
            gp_v[at] = (mm(g_v[at], wd_v[...], NT) * slope).astype(bf16)
        up = mm(h_v[...], gp_v[...], TN).astype(bf16)
        if fast:
            for j in range(chips):
                o_v[place(j, info[1], orders[0]), :part] = up[j * part : (j + 1) * part]
            if split:
                halfway = chips // 2
                out = [mv.go(o_v.at[pl.ds(halfway, halfway)], ends[0]), mv.go(o_v.at[pl.ds(0, halfway)], ends[1])]
        else:
            o_v[:width] = up
        down = mm(act_v[...], g_v[...], TN).astype(bf16)
        if fast:
            sm_v[...] = sm[...]
            sm_v[6:8, pl.ds(pl.multiple_of(info[0] * (width // 2), 128), width // 2)] = gqv[...]
            whole = sm_v[...]
            low_v, top = o_vs[-1], 0 if split else part
            for j in range(chips):
                p = place(j, info[1], orders[-1])
                low_v[p, top : top + unit] = down[j * unit : (j + 1) * unit]
                low_v[p, top + unit :] = jnp.concatenate(
                    [
                        jnp.concatenate([whole[:, j * part : (j + 1) * part], jnp.zeros((8, width - part), f32)], 1),
                        jnp.concatenate([bup[:, 4 * j * unit : 4 * (j + 1) * unit], jnp.zeros((1, width - 4 * unit), f32)], 1),
                        jnp.zeros((7, width), f32),
                    ]
                ).astype(bf16)
            halfway = chips // 2
            out = out if split else []
            out += [mv.go(low_v.at[pl.ds(halfway, halfway)], ends[-2]), mv.go(low_v.at[pl.ds(0, halfway)], ends[-1])]
        else:
            o_v[width:] = down
            out = [mv.go(o_v.at[pl.ds(0, width)], ends[0]), mv.go(o_v.at[pl.ds(width, fo)], ends[1])]
        for k in out:
            k.wait()

    S, V = jax.ShapeDtypeStruct, pltpu.VMEM
    tok = V((n * rows, width), bf16)
    hid = V((n * rows, fo), bf16)
    if fast:
        sizes = (part, unit + 16) if split else (part + unit + 16,)
        outs = tuple(S((chips // 2, n_rows, width), bf16) for n_rows in sizes for _ in range(2))
        o_vs = [V((chips, n_rows, width), bf16) for n_rows in sizes]
    else:
        outs = (S((width, fo), bf16), S((fo, width), bf16))
        o_vs = [V((width + fo, width), bf16)]
    got = kernel_call(
        body, "ffn_grads", (info,) + tuple(hs) + gs + (wu_own, w_down, b_own, small, gbup, gqv), [SM] + [ANY] * m + [HBM, HBM] + [VM] * 4,
        outs, (ANY,) * len(outs), [tok, tok, V((width, fo), bf16), V((fo, width), bf16), hid, hid] + o_vs + [V((8, width), f32)],
        2 * n + 6 + chips, 8 * n * rows * width * fo, 8 << 20,
    )
    if fast:
        return [(got[2 * i], got[2 * i + 1]) for i in range(len(orders))]
    zero = jnp.zeros_like(gqv)
    gqv = jnp.where(info[0] == 0, jnp.concatenate([gqv, zero], 1), jnp.concatenate([zero, gqv], 1))
    small = jnp.concatenate([small[:6], gqv]).reshape(8, chips, part).transpose(1, 0, 2)
    small = jnp.concatenate([jnp.pad(small, ((0, 0), (0, 0), (0, width - part))),
                             jnp.pad(gbup.reshape(chips, 1, 4 * unit), ((0, 0), (0, 7), (0, width - 4 * unit)))], 1)
    both = [[got[0].reshape(chips, part, fo)], [got[1].reshape(chips, unit, width), small.astype(bf16)]]
    if not split:
        both = [both[0] + both[1]]
    both = [arranged(jnp.concatenate(v, 1), info[1], order) for v, order in zip(both, orders)]
    return [(v[chips // 2 :], v[: chips // 2]) for v in both]


def proj_grads(info, xo, xt, ctx, got, go, gt, gproj, order, fast):
    rows, width = xo.shape
    half = width // 2
    toks = 2 * rows
    chips = 2 ** len(order)
    part = width // chips

    def body(info, xo, xt, ctx, got, go, gt, gp, *refs):
        outs, (x_v, gp_v, c_v, ga_v, o_v, sems) = refs[:-6], refs[-6:]
        mv = Mover(sems)
        c, me, y = info[0], info[1], info[2]
        top, low = pl.ds(0, rows), pl.ds(rows, rows)
        cols = pl.ds(pl.multiple_of(c * half, 128), half)
        cx = [mv.go(xo, x_v.at[top]), mv.go(xt, x_v.at[low]), mv.go(gp, gp_v)]
        cc = [mv.go(ctx, c_v.at[0]), mv.go(got.at[low], c_v.at[1, top]), mv.go(got.at[top], c_v.at[1, low]),
              mv.go(go.at[:, cols], ga_v.at[top]), mv.go(gt.at[:, cols], ga_v.at[low])]
        for k in cx:
            k.wait()
        for g in range(4):
            if g < 3:
                blocks = [(0, mm(x_v[...], gp_v[:, g * half : (g + 1) * half], TN).astype(bf16))]
            else:
                for k in cc:
                    k.wait()
                blocks = [(c if i == 0 else 1 - c, mm(c_v[i], ga_v[...], TN).astype(bf16)) for i in range(2)]
            at = slice(g % 2 * half, (g % 2 + 1) * half)
            for who, val in blocks:
                if fast:
                    for j in range(val.shape[0] // part):
                        p = place(who * (chips // 2) + j, me, order)
                        o_v[jnp.bitwise_xor(g // 2, y), p, :, at] = val[j * part : (j + 1) * part]
                elif g < 3:
                    o_v[g // 2, :, at] = val
                else:
                    o_v[1, pl.ds(pl.multiple_of(who * half, 128), half), at] = val
        out = [mv.go(o_v.at[1], outs[0]), mv.go(o_v.at[0], outs[1])] if fast else [mv.go(o_v, outs[0])]
        for k in out:
            k.wait()

    S, V = jax.ShapeDtypeStruct, pltpu.VMEM
    shape = (2, chips, part, width) if fast else (2, width, width)
    res = kernel_call(
        body, "proj_grads", (info, xo, xt, ctx, got, go, gt, gproj), [SM] + [ANY] * 7,
        (S(shape[1:], bf16),) * 2 if fast else S(shape, bf16), (ANY, ANY) if fast else ANY,
        [V((toks, width), bf16), V((toks, 3 * half), bf16), V((2, toks, half), bf16), V((toks, half), bf16), V(shape, bf16)],
        10, 2 * toks * width * 4 * half, 6 << 20,
    )
    if fast:
        return res
    v = res.reshape(2, chips, part, width)
    v = jnp.where(info[2] == 1, v[::-1], v)
    return arranged(v[1], info[1], order), arranged(v[0], info[1], order)


def pack(info, ends, part, unit, fast):
    width = ends[0][0].shape[-1]
    hp = part // 2
    if not fast:
        v = jnp.concatenate([add(k[0], g[0]).astype(bf16) for k, g in ends])
        up, low, proj = v[:part].reshape(2, hp, width), v[part : part + unit + 16], v[part + unit + 16 :].reshape(2, hp, width)
        mine, other = pick(up, info[0], 0), pick(up, 1 - info[0], 0)
        return (jnp.concatenate([mine, low, pick(proj, info[0], 0)]), jnp.concatenate([other, low[unit:], pick(proj, 1 - info[0], 0)]))
    n = len(ends)

    def body(info, *refs):
        ks, gs, row_o, col_o = refs[:n], refs[n : 2 * n], refs[2 * n], refs[2 * n + 1]
        k_v, g_v, row_v, col_v, sems = refs[2 * n + 2 :]
        mv = Mover(sems)
        at, come = 0, []
        for k, g in zip(ks, gs):
            now = pl.ds(at, k.shape[1])
            come += [mv.go(k.at[0], k_v.at[now]), mv.go(g.at[0], g_v.at[now])]
            at += k.shape[1]
        for c in come:
            c.wait()
        v = (k_v[...].astype(f32) + g_v[...].astype(f32)).astype(bf16)
        first = info[0] == 0
        lo = part + unit + 16
        up0, up1, pr0, pr1 = v[:hp], v[hp:part], v[lo : lo + hp], v[lo + hp :]
        row_v[:hp] = jnp.where(first, up0, up1)
        row_v[hp : hp + unit + 16] = v[part:lo]
        row_v[hp + unit + 16 :] = jnp.where(first, pr0, pr1)
        col_v[:hp] = jnp.where(first, up1, up0)
        col_v[hp : hp + 16] = v[lo - 16 : lo]
        col_v[hp + 16 :] = jnp.where(first, pr1, pr0)
        for c in [mv.go(col_v, col_o), mv.go(row_v, row_o)]:
            c.wait()

    total = sum(k.shape[1] for k, _ in ends)
    S, V = jax.ShapeDtypeStruct, pltpu.VMEM
    shapes = [(part + unit + 16, width), (part + 16, width)]
    return kernel_call(
        body, "pack", (info,) + tuple(k for k, _ in ends) + tuple(g for _, g in ends), [SM] + [ANY] * (2 * n),
        tuple(S(v, bf16) for v in shapes), (ANY, ANY), [V((total, width), bf16)] * 2 + [V(v, bf16) for v in shapes], 2 * n + 2, 0, 0,
    )


def unpack(info, rounds, part, unit, chips, fast):
    layers = len(rounds)
    width = rounds[0][0].shape[-1]
    hp, half = part // 2, width // 2
    lo = hp + unit + 16
    if not fast:
        res = []
        for own, row, core, diag in rounds:
            def quarters(a, b):
                mine = order_two(info[2], own[a], row[a], 0)
                other = order_two(info[2], core[b], diag[b], 0)
                return order_two(info[0], mine, other, 0)

            up = quarters(slice(0, hp), slice(0, hp)).reshape(2, 2, hp, chips, unit)
            up = up.transpose(2, 3, 0, 1, 4).reshape(hp, 4 * width).astype(f32)
            proj = quarters(slice(lo, lo + hp), slice(hp + 16, part + 16)).reshape(2, 2, hp, 2, half)
            proj = proj.transpose(2, 1, 3, 0, 4).reshape(hp, 4 * width).astype(f32)
            down = order_two(info[2], own[hp : hp + unit], row[hp : hp + unit], 0).reshape(2 * unit, width).astype(f32)
            small = add(own[lo - 16 : lo], row[lo - 16 : lo]) + add(core[hp : hp + 16], diag[hp : hp + 16])
            vecs = pick(small[:8, :part].reshape(8, 2, hp), info[0], 1)
            bup = pick(small[8, : 4 * unit].reshape(2, 2 * unit), info[0], 0)
            res.append((proj[:, : 3 * width], proj[:, 3 * width :], up, down, bup, vecs[6:8]) + tuple(vecs[i] for i in range(6)))
        return tuple(jnp.stack([r[i] for r in res]) for i in range(12))

    def body(info, *refs):
        src, outs = refs[: 4 * layers], refs[4 * layers : 4 * layers + 12]
        big_v, small_v, q_v, d_v, sems = refs[4 * layers + 12 :]
        mv = Mover(sems)
        come = []
        for l in range(layers):
            for i in range(4):
                to = big_v.at[l, i] if i < 2 else small_v.at[l, i - 2]
                come.append(mv.go(src[4 * l + i], to))
        qkv, out, up, down, bup, gqv = outs[:6]
        c, y, share = info[0], info[2], info[3]
        first = c == 0
        for l in range(layers):
            for k in come[4 * l : 4 * l + 4]:
                k.wait()
            diag = 3 - share
            for p, (a, b) in enumerate(((0, 0), (lo, hp + 16))):
                q_v[p, share] = big_v[l, 0, a : a + hp]
                q_v[p, 2 * c + 1 - y] = big_v[l, 1, a : a + hp]
                q_v[p, 2 * (1 - c) + y] = small_v[l, 0, b : b + hp]
                q_v[p, diag] = small_v[l, 1, b : b + hp]
            d_v[y] = big_v[l, 0, hp : hp + unit]
            d_v[1 - y] = big_v[l, 1, hp : hp + unit]
            for q in range(4):
                whole = q_v[0, q].astype(f32)
                for i in range(chips):
                    up[l, :, (4 * i + q) * unit : (4 * i + q + 1) * unit] = whole[:, i * unit : (i + 1) * unit]
                whole = q_v[1, q].astype(f32)
                at = q // 2 * half
                if q % 2 == 0:
                    qkv[l, :, at : at + half] = whole[:, :half]
                    qkv[l, :, width + at : width + at + half] = whole[:, half:]
                else:
                    qkv[l, :, 2 * width + at : 2 * width + at + half] = whole[:, :half]
                    out[l, :, at : at + half] = whole[:, half:]
            for i in range(2):
                down[l, i * unit : (i + 1) * unit] = d_v[i].astype(f32)
            small = (big_v[l, 0, lo - 16 : lo].astype(f32) + big_v[l, 1, lo - 16 : lo].astype(f32)) + (
                small_v[l, 0, hp : hp + 16].astype(f32) + small_v[l, 1, hp : hp + 16].astype(f32))
            vecs = jnp.where(first, small[:8, :hp], small[:8, hp:part])
            bup[l : l + 1] = jnp.where(first, small[8:9, : 2 * unit], small[8:9, 2 * unit : 4 * unit])
            gqv[l] = vecs[6:8]
            for i in range(6):
                outs[6 + i][l : l + 1] = vecs[i : i + 1]

    S, V = jax.ShapeDtypeStruct, pltpu.VMEM
    outs = [(layers, hp, 3 * width), (layers, hp, width), (layers, hp, 4 * width), (layers, 2 * unit, width), (layers, 2 * unit), (layers, 2, hp)]
    outs += [(layers, hp)] * 6
    args = (info,) + tuple(v for r in rounds for v in r)
    return kernel_call(
        body, "unpack", args, [SM] + [ANY] * (4 * layers), tuple(S(v, f32) for v in outs), (VM,) * 12,
        [V((layers, 2, part + unit + 16, width), bf16), V((layers, 2, part + 16, width), bf16), V((2, 4, hp, width), bf16), V((2, unit, width), bf16)],
        4 * layers, 0, 0,
    )


class Wires:
    def __init__(self, batch, seq):
        self.batch, self.seq = batch, seq
        self.chips = batch // 2
        self.bits = self.chips.bit_length() - 1
        where = [(i, j) for i in range(batch) for j in range(seq)]

        def table(move):
            out = []
            for i, j in where:
                p, q = move(i, j)
                out.append((i * seq + j, p * seq + q))
            return out

        self.core = table(lambda i, j: (i ^ 1, j))
        self.row = table(lambda i, j: (i, 1 - j))
        self.diag = table(lambda i, j: (i ^ 1, 1 - j))
        self.turn = table(lambda i, j: (i - i % 2 + j, i % 2))
        self.chip = [table(lambda i, j, k=k: (i ^ (2 << k), j)) for k in range(self.bits)]
        self.b = lax.axis_index("batch")
        self.y = lax.axis_index("seq")
        self.c = self.b % 2

    def swap_core(self, v):
        return lax.ppermute(v, AXES, self.core)

    def swap_row(self, v):
        return lax.ppermute(v, AXES, self.row)

    def swap_diag(self, v):
        return lax.ppermute(v, AXES, self.diag)

    def swap_turn(self, v):
        return lax.ppermute(v, AXES, self.turn)

    def swap_chip(self, v, k):
        return lax.ppermute(v, AXES, self.chip[k])

    def bit(self, k):
        return (self.b >> (k + 1)) & 1


def pick(v, idx, axis):
    return lax.dynamic_index_in_dim(v, idx, axis, keepdims=False)


def add(a, b):
    return a.astype(f32) + b.astype(f32)


def order_two(flag, mine, got, axis):
    return jnp.stack([jnp.where(flag == 0, mine, got), jnp.where(flag == 0, got, mine)], axis)


class Clock:
    def __init__(self):
        self.now, self.free, self.alive = 0.0, {}, []

    def busy(self, link, us):
        begin = max(self.now, self.free.get(link, 0.0))
        self.free[link] = begin + us
        return begin + us

    def work(self, us):
        self.now += us

    def catch_up(self):
        for s in sorted(self.alive, key=lambda s: s.ready):
            if s.ready <= self.now + 3.0:
                s.step()

    def drain(self):
        while self.alive:
            min(self.alive, key=lambda s: s.ready).step()


class Stream:
    def __init__(self, wires, clock, send, keep, order, row_first):
        self.wires, self.clock, self.keep, self.end = wires, clock, keep, None
        self.todo = list(order)
        clock.alive.append(self)
        self.send(send, row_first)

    def send(self, v, row=False):
        us = v.size * 2 / 1e6 * 22.0
        if row:
            self.got, link = self.wires.swap_row(v), "y"
        else:
            k = self.todo.pop(0)
            self.got = self.wires.swap_chip(v, k)
            link = "x" if k == 0 else "z"
            us *= max(1, 1 << (k - 1)) if k else 1
        self.clock.work(1.4)
        self.ready = self.clock.busy(link, us) + 2.0

    def step(self):
        clock = self.clock
        clock.now = max(clock.now, self.ready)
        if not self.todo:
            self.end = (self.keep, self.got)
            clock.alive.remove(self)
            return
        clock.work(1.2 + self.keep.size * 2 / 1e6)
        send, self.keep = merge(self.keep, self.got)
        self.send(send)


def local(inputs, out_grad, masked, w_qkv, bias_qv, w_out, bias_out, gain_one, shift_one, w_up, bias_up, w_down, bias_down, gain_two, shift_two):
    wires = Wires(lax.axis_size("batch"), lax.axis_size("seq"))
    layers, width, ff = w_up.shape
    half = width // 2
    chips, bits = wires.chips, wires.bits
    fo, unit, part = ff // 4, ff // chips // 4, width // chips
    fast = part % 32 == 0
    share = wires.c * 2 + wires.y
    info = jnp.stack([wires.c, wires.b // 2, wires.y, share]).astype(jnp.int32)
    rows = inputs.shape[1]
    ROW.extra = []
    xb = wires.swap_turn(inputs[0])
    b_own = pick(bias_up.reshape(layers, chips, 4, unit), share, 2).reshape(layers, 1, fo)
    if fast:
        wu_own, wd_own = [own_units(info, l, w_up, chips) for l in range(layers)], w_down
    else:
        wu_own = pick(w_up.reshape(layers, width, chips, 4, unit), share, 3).reshape(layers, width, fo)
        wd_own = pick(w_down.reshape(layers, chips, 4, unit, width), share, 2).reshape(layers, fo, width)
    x = xb
    saved, outs, hs = [], [], []
    tail = (w_out, bias_out, gain_one, shift_one, w_up, bias_up, w_down, bias_down, gain_two, shift_two)
    clock = Clock()
    for l in range(layers):
        xt = wires.swap_core(xb)
        qkv, pt, ctx = attn_fwd(info, l, xb, xt, w_qkv, bias_qv)
        if l == 0:
            gy = wires.swap_turn(masked_grad(out_grad[0], masked))
        else:
            ROW.before_next(outs[-1])
        got = wires.swap_core(ctx)
        last = l == layers - 1
        if last:
            yb, pair, ga, gm, small, gbup = ffn_fwd(info, l, x, ctx, got, tail, gy)
            saved.append((xb, xt, qkv, pt, ctx, got))
            turned_back = (pair, ga, gm, small, gbup)
        else:
            hb, dg, mixed, x, yb = ffn_fwd(info, l, x, ctx, got, tail)
            hy = wires.swap_row(hb)
            hs.append((hb, hy, wires.swap_core(hb), wires.swap_core(hy)))
            saved.append((xb, xt, qkv, pt, ctx, got, dg, mixed, x))
        outs.append(wires.swap_turn(yb)[None])
        xb = yb
        if l == 0:
            ROW.before_next(gy)
    low = list(range(bits))
    turned = low[1:2] + low[:1] + low[2:]
    plan = [((low, turned), low)] + [((turned,), low)] * (layers - 1)
    streams = [None] * layers
    for l in reversed(range(layers)):
        xb, xt, qkv, pt, ctx, got = saved[l][:6]
        if l == layers - 1:
            pair, ga, gm, small, gbup = turned_back
            gat = wires.swap_core(ga)
            py = wires.swap_row(pair)
            both = (pair, py, wires.swap_core(pair), wires.swap_core(py)), None
        else:
            dg, mixed, summed = saved[l][6:]
            gf, ga, gm, small, gbup = ffn_bwd(info, l, flow, summed, mixed, dg, (w_up, w_down, gain_one, gain_two))
            gat = wires.swap_core(ga)
            gfy = wires.swap_row(gf)
            both = hs[l], (gf, gfy, wires.swap_core(gf), wires.swap_core(gfy))
        gproj, gptail, gqv = attn_bwd(info, l, ga, gat, w_out, qkv, pt)
        if l == layers - 1:
            ROW.before_next(*hs[-1])
        flow = (gm, gproj, wires.swap_core(gptail), w_qkv)
        clock.work(28.0 if l < layers - 1 else 0.0)
        clock.catch_up()
        send, keep = proj_grads(info, xb, xt, ctx, got, ga, gat, gproj, plan[l][1], fast)
        clock.work(4.5)
        ps = [Stream(wires, clock, send, keep, plan[l][1], True)]
        if l == layers - 1:
            ROW.before_next(outs[-1])
        clock.catch_up()
        res = ffn_grads(info, l, *both, wu_own[l], wd_own, b_own, small, gbup, gqv, plan[l][0], fast)
        clock.work(10.5)
        fs = [Stream(wires, clock, s, k, order, False) for (s, k), order in zip(res, plan[l][0])]
        clock.catch_up()
        streams[l] = fs + ps
    end = chain_end(info, 0, flow)
    clock.work(5.5)
    grad_in = wires.swap_turn(end)[None]
    rounds = [None] * layers
    while not all(rounds):
        if clock.alive:
            min(clock.alive, key=lambda s: s.ready).step()
        for l in range(layers):
            if rounds[l] is None and all(s.end for s in streams[l]):
                row, col = pack(info, [s.end for s in streams[l]], part, unit, fast)
                rounds[l] = (row, wires.swap_row(row), wires.swap_core(col), wires.swap_diag(col))
                clock.work(5.0)
                clock.busy("y", 11.0)
    qkv, out, up, down, bup, gqv, gdn, gg2, gs2, gg1, gs1, gbo = unpack(info, rounds, part, unit, chips, fast)
    return (outs[0], outs[-1], grad_in, qkv, gqv, out, gbo, gg1, gs1, up, bup, down, gdn, gg2, gs2)


def solution(mesh):
    tok = P("batch", "seq", None)
    in_specs = (tok, tok, P("batch", "seq")) + (P(),) * 12
    mat, vec = P(None, "batch", None), P(None, "batch")
    out_specs = (tok, tok, tok, mat, P(None, None, "batch"), mat, vec, vec, vec, mat, vec, mat, vec, vec, vec)
    return jax.shard_map(local, mesh=mesh, in_specs=in_specs, out_specs=out_specs, check_vma=False)
```

```python
import math

import jax
import jax.numpy as jnp
from jax import lax
from jax.experimental import pallas as pl
from jax.experimental.pallas import tpu as pltpu
from jax.sharding import PartitionSpec as P

HEAD_DIM = 64
AXES = ("batch", "seq")
norm_eps = 1e-06
f32 = jnp.float32
bf16 = jnp.bfloat16
ANY = pl.BlockSpec(memory_space=pl.ANY)
HBM = pl.BlockSpec(memory_space=pltpu.HBM)
VM = pl.BlockSpec(memory_space=pltpu.VMEM)
SM = pl.BlockSpec(memory_space=pltpu.SMEM)
ROOT_HALF = 0.7071067811865476
INV_ROOT_TAU = 0.3989422804014327
TAKES = {"own_units": 24.0, "attn_fwd": 7.5, "ffn_fwd": 9.0, "ffn_turn": 13.0, "ffn_bwd": 12.0, "attn_bwd": 7.5, "ffn_grads": 10.5, "proj_grads": 18, "chain_end": 4.5, "merge": 7.0, "masked_grad": 2.0, "pack": 3.0, "unpack": 5.0}
PACE = 0.5


def mm(a, b, dims=((1,), (0,))):
    return lax.dot_general(a, b, (dims, ((), ())), preferred_element_type=f32)


NT = ((1,), (1,))
TN = ((0,), (0,))


class Mover:
    def __init__(self, sems):
        self.sems, self.used = sems, 0

    def go(self, src, dst):
        copy = pltpu.make_async_copy(src, dst, self.sems.at[self.used])
        self.used += 1
        copy.start()
        return copy


class Row:
    def __init__(self):
        self.extra = []

    def before_next(self, *values):
        self.extra.extend(values)


ROW = Row()


def kernel_call(body, name, args, specs, outs, out_specs, scratch, sems, flops, moved):
    extra = tuple(ROW.extra)
    n, m = len(args), len(args) + len(extra)
    held = sum(math.prod(v.shape) * jnp.dtype(v.dtype).itemsize for v in scratch)
    limit = held + ((2 << 20) if name == "merge" else (12 << 20))
    args = tuple(
        pltpu.with_memory_space_constraint(a, pltpu.HBM) if spec is HBM else a for a, spec in zip(args, specs)
    )
    out = pl.pallas_call(
        lambda *refs: body(*refs[:n], *refs[m:]),
        name=name,
        out_shape=outs,
        in_specs=specs + [ANY] * len(extra),
        out_specs=out_specs,
        scratch_shapes=list(scratch) + [pltpu.SemaphoreType.DMA((sems,))],
        compiler_params=pltpu.CompilerParams(vmem_limit_bytes=limit),
        cost_estimate=pl.CostEstimate(flops=int(PACE * TAKES[name] * 1.15e9), bytes_accessed=moved, transcendentals=0),
    )(*args, *extra)
    ROW.extra = [out[0] if isinstance(out, (tuple, list)) else out]
    return out


def merge(keep, got):
    n = max(keep.shape[0] // 2, 1)
    rest = keep.shape[1:]
    parts = keep.shape[0] // n

    def body(k, g, *refs):
        outs, (k_v, g_v, sems) = refs[:parts], refs[parts:]
        mv = Mover(sems)
        at = [pl.ds((parts - 1 - i) * n, n) for i in range(parts)]
        come = [(mv.go(k.at[a], k_v.at[a]), mv.go(g.at[a], g_v.at[a])) for a in at]
        gone = []
        for i, a in enumerate(at):
            for c in come[i]:
                c.wait()

            def one(j, _):
                j = j + (parts - 1 - i) * n
                k_v[j] = (k_v[j].astype(f32) + g_v[j].astype(f32)).astype(bf16)
                return 0

            lax.fori_loop(0, n, one, 0)
            gone.append(mv.go(k_v.at[a], outs[i]))
        for c in gone:
            c.wait()

    outs = (jax.ShapeDtypeStruct((n,) + rest, bf16),) * parts
    return kernel_call(body, "merge", (keep, got), [ANY, ANY], outs, (ANY,) * parts, [pltpu.VMEM(keep.shape, bf16)] * 2, 3 * parts, 5 * 10**9, 0)


def normed(z):
    center = z - jnp.mean(z, -1, keepdims=True)
    rstd = lax.rsqrt(jnp.mean(center * center, -1, keepdims=True) + norm_eps)
    return center * rstd, rstd


def norm_back(g, z, gain):
    xhat, rstd = normed(z)
    gx = g * gain
    m1 = jnp.mean(gx, -1, keepdims=True)
    m2 = jnp.mean(gx * xhat, -1, keepdims=True)
    return rstd * (gx - m1 - xhat * m2), g * xhat


def phi_parts(u):
    cdf = 0.5 * (1.0 + lax.erf(u * ROOT_HALF))
    return cdf, cdf + u * (jnp.exp(-0.5 * u * u) * INV_ROOT_TAU)


def masked_grad(grad, masked):
    rows, width = grad.shape

    def body(g, m, o, sems):
        col = jnp.broadcast_to(m[...].astype(f32), (8, rows)).T[:, :1]
        o[...] = (g[...].astype(f32) * col).astype(bf16)

    return kernel_call(body, "masked_grad", (grad, masked), [VM, VM], jax.ShapeDtypeStruct((rows, width), bf16), VM, [], 1, 0, 0)


def attn_fwd(info, l, xo, xt, w_qkv, bias_qv):
    rows, width = xo.shape
    half = width // 2
    heads = half // HEAD_DIM
    toks = 2 * rows

    def body(info, xo, xt, w, bias, qkv_o, pt_o, ctx_o, x_v, w_v, qkv_v, pt_v, ctx_v, sems):
        mv = Mover(sems)
        c = info[0]
        cx = [mv.go(xo, x_v.at[pl.ds(0, rows)]), mv.go(xt, x_v.at[pl.ds(rows, rows)])]
        cw = []
        for p in range(3):
            at = pl.multiple_of(p * width + c * half, 128)
            cw.append(mv.go(w.at[l, :, pl.ds(at, half)], w_v.at[p]))
        for k in cx:
            k.wait()
        at = pl.multiple_of(c * half, 128)
        for p in range(3):
            cw[p].wait()
            val = mm(x_v[...], w_v[p])
            if p != 1:
                val = val + bias[l, pl.ds(p // 2, 1), pl.ds(at, half)].astype(f32)
            val = val.astype(bf16)
            if p == 0:
                val = (val.astype(f32) * HEAD_DIM ** (-0.5)).astype(bf16)
            qkv_v[:, p * half : (p + 1) * half] = val
        out = [mv.go(qkv_v, qkv_o)]
        lane = lax.broadcasted_iota(jnp.int32, (toks, 2 * HEAD_DIM), 1) < HEAD_DIM

        for i in range(heads // 2):
            at = i * 2 * HEAD_DIM
            q = qkv_v[:, at : at + 128]
            k = qkv_v[:, half + at : half + at + 128]
            v = qkv_v[:, 2 * half + at : 2 * half + at + 128]
            both = []
            for h in range(2):
                qm = jnp.where(lane == (h == 0), q, jnp.zeros_like(q))
                st = mm(k, qm, NT)
                top = jnp.max(st, 0, keepdims=True)
                e = jnp.exp(st - top)
                p = (e / jnp.sum(e, 0, keepdims=True)).astype(bf16)
                pt_v[2 * i + h] = p
                both.append(mm(p, v, TN))
            ctx_v[:, at : at + 128] = jnp.where(lane, both[0], both[1]).astype(bf16)
            now = pl.ds(2 * i, 2)
            out.append(mv.go(pt_v.at[now], pt_o.at[now]))
        out.append(mv.go(ctx_v, ctx_o))
        for k in out:
            k.wait()

    S = jax.ShapeDtypeStruct
    outs = (pltpu.HBM((toks, 3 * half), bf16), pltpu.HBM((heads, toks, toks), bf16), S((toks, half), bf16))
    return kernel_call(
        body, "attn_fwd", (info, xo, xt, w_qkv, bias_qv), [SM, ANY, ANY, HBM, VM], outs, (ANY,) * 3,
        [pltpu.VMEM((toks, width), bf16), pltpu.VMEM((3, width, half), bf16), pltpu.VMEM((toks, 3 * half), bf16),
         pltpu.VMEM((heads, toks, toks), bf16), pltpu.VMEM((toks, half), bf16)],
        8 + heads // 2, 2 * toks * width * 3 * half + 8 * heads * toks * toks * 128, 8 << 20,
    )


def ffn_fwd(info, l, x, ctx, got, weights, gy=None, cut=6):
    w_out, bias_out, gain_one, shift_one, w_up, bias_up, w_down, bias_down, gain_two, shift_two = weights
    rows, width = x.shape
    half = width // 2
    ff = w_up.shape[2]
    step = ff // cut
    turn = gy is not None

    def body(info, x, ctx, got, wo, bo, g1, s1, wu, bu, wd, bd, g2, s2, *refs):
        if turn:
            gy_r, yb_o, pair_o, ga_o, gm_o, small_o, gbup_o = refs[:7]
            x_v, c_v, wo_v, wu_v, wd_v, hb_v, dg_v, mixed_v, yb_v, low_v, gf_v, gm_v, sems = refs[7:]
        else:
            hb_o, dg_o, mixed_o, summed_o, yb_o = refs[:5]
            x_v, c_v, wo_v, wu_v, wd_v, hb_v, dg_v, mixed_v, yb_v, sems = refs[5:]
        mv = Mover(sems)
        c = info[0]
        cx = mv.go(x, hb_v if l == 0 else x_v)
        first = [mv.go(ctx.at[pl.ds(0, rows)], c_v.at[0])]
        at = [pl.multiple_of(c * half, 128), pl.multiple_of((1 - c) * half, 128)]
        first += [mv.go(wo.at[l, pl.ds(at[i], half)], wo_v.at[i]) for i in range(2)]
        first += [mv.go(got.at[pl.ds(rows, rows)], c_v.at[1])]
        cu, cd = [], []
        for j in range(cut):
            cu.append(mv.go(wu.at[l, :, pl.ds(j * step, step)], wu_v.at[j]))
            cd.append(mv.go(wd.at[l, pl.ds(j * step, step)], wd_v.at[j]))
        if turn:
            cg = mv.go(gy_r, low_v)
        cx.wait()
        if l == 0:
            xin = hb_v[...].astype(f32)
        else:
            xin = normed(x_v[...])[0] * g2[l - 1 : l].astype(f32) + s2[l - 1 : l].astype(f32)
        for k in first:
            k.wait()
        mixed = xin + mm(c_v[0], wo_v[0]) + mm(c_v[1], wo_v[1]) + bo[l : l + 1].astype(f32)
        mixed_v[...] = mixed
        out = [] if turn else [mv.go(mixed_v, mixed_o)]
        hid = normed(mixed)[0] * g1[l : l + 1].astype(f32) + s1[l : l + 1].astype(f32)
        x_v[...] = hid
        hb_v[...] = hid.astype(bf16)
        out.append(mv.go(hb_v, pair_o.at[0] if turn else hb_o))
        acc = None
        for j in range(cut):
            cols = slice(j * step, (j + 1) * step)
            cu[j].wait()
            u = mm(hb_v[...], wu_v[j]) + bu[l : l + 1, cols].astype(f32)
            cdf, slope = phi_parts(u)
            dg_v[j] = slope.astype(dg_v.dtype)
            if not turn:
                out.append(mv.go(dg_v.at[j], dg_o.at[:, pl.ds(j * step, step)]))
            cd[j].wait()
            part = mm((u * cdf).astype(bf16), wd_v[j])
            acc = part if acc is None else acc + part
        summed = x_v[...] + acc + bd[l : l + 1].astype(f32)
        x_v[...] = summed
        if not turn:
            out.append(mv.go(x_v, summed_o))
        gain = g2[l : l + 1].astype(f32)
        y = normed(summed)[0] * gain + s2[l : l + 1].astype(f32)
        yb_v[...] = y.astype(bf16)
        out.append(mv.go(yb_v, yb_o))
        if turn:
            cg.wait()
            gy = low_v[...].astype(f32)
            gsum, gterm = norm_back(gy, x_v[...], gain)
            small_o[1:2] = jnp.sum(gterm, 0, keepdims=True)
            small_o[2:3] = jnp.sum(gy, 0, keepdims=True)
            gf = gsum.astype(bf16)
            gf_v[...] = gf
            small_o[0:1] = jnp.sum(gf.astype(f32), 0, keepdims=True)
            out.append(mv.go(gf_v, pair_o.at[1]))
            gm_v[...] = gsum
            acc = None
            for j in range(cut):
                gpre = (mm(gf_v[...], wd_v[j], NT) * dg_v[j].astype(f32)).astype(bf16)
                gbup_o[:, j * step : (j + 1) * step] = jnp.sum(gpre.astype(f32), 0, keepdims=True)
                part = mm(gpre, wu_v[j], NT)
                acc = part if acc is None else acc + part
            ghid = gm_v[...] + acc
            gmix, gterm = norm_back(ghid, mixed_v[...], g1[l : l + 1].astype(f32))
            ga = gmix.astype(bf16)
            low_v[...] = ga
            out.append(mv.go(low_v, ga_o))
            gm_v[...] = gmix
            out.append(mv.go(gm_v, gm_o))
            small_o[3:4] = jnp.sum(gterm, 0, keepdims=True)
            small_o[4:5] = jnp.sum(ghid, 0, keepdims=True)
            small_o[5:6] = jnp.sum(ga.astype(f32), 0, keepdims=True)
            small_o[6:8] = jnp.zeros((2, width), f32)
        for k in out:
            k.wait()

    S, V = jax.ShapeDtypeStruct, pltpu.VMEM
    full, low = S((rows, width), f32), S((rows, width), bf16)
    scratch = [V((rows, width), f32), V((2, rows, half), bf16), V((2, half, width), bf16), V((cut, width, step), bf16),
               V((cut, step, width), bf16), V((rows, width), bf16), V((cut, rows, step), bf16), V((rows, width), f32),
               V((rows, width), bf16)]
    args = (info, x, ctx, got, w_out, bias_out, gain_one, shift_one, w_up, bias_up, w_down, bias_down, gain_two, shift_two)
    specs = [SM, ANY, ANY, ANY, HBM, VM, VM, VM, HBM, VM, HBM, VM, VM, VM]
    if turn:
        outs = (low, S((2, rows, width), bf16), low, full, S((8, width), f32), S((1, ff), f32))
        out_specs = (ANY, ANY, ANY, ANY, VM, VM)
        scratch += [V((rows, width), bf16), V((rows, width), bf16), V((rows, width), f32)]
        args, specs = args + (gy,), specs + [ANY]
    else:
        outs, out_specs = (low, pltpu.HBM((rows, ff), bf16), pltpu.HBM((rows, width), f32), full, low), (ANY,) * 5
    return kernel_call(
        body, "ffn_turn" if turn else "ffn_fwd", args, specs, outs, out_specs, scratch, 14 + 3 * cut, 0, 12 << 20,
    )


def ffn_bwd(info, l, flow, summed, mixed, dg, weights, cut=6):
    w_up, w_down, gain_one, gain_two = weights
    rows, width = summed.shape
    half = width // 2
    ff = w_up.shape[2]
    step = ff // cut
    chained = len(flow) > 1

    def body(*refs):
        info = refs[0]
        fl = refs[1 : 1 + len(flow)]
        (sm, mi, dgr, wu, wd, g1, g2, gf_o, ga_o, gm_o, small_o, gbup_o,
         gy_v, sm_v, mi_v, dg_v, wu_v, wd_v, gf_v, ga_v, gm_v) = refs[1 + len(flow) : 22 + len(flow)]
        sems = refs[-1]
        mv = Mover(sems)
        if chained:
            gp_v, wq_v = refs[22 + len(flow) : 24 + len(flow)]
            c = info[0]
            fc = [mv.go(fl[0], gy_v), mv.go(fl[1].at[pl.ds(0, rows)], gp_v.at[0])]
            wq = []
            for i in range(2):
                who = c if i == 0 else 1 - c
                for p in range(3):
                    at = pl.multiple_of(p * width + who * half, 128)
                    wq.append(mv.go(fl[3].at[l + 1, :, pl.ds(at, half)], wq_v.at[i, p]))
            fc.append(mv.go(fl[2], gp_v.at[1]))
        else:
            fc = [mv.go(fl[0], gf_v)]
        fc += [mv.go(sm, sm_v)]
        cd, cu, cg = [], [], []
        for j in range(cut):
            cols = pl.ds(j * step, step)
            cd.append(mv.go(wd.at[l, cols], wd_v.at[j]))
            cg.append(mv.go(dgr.at[:, cols], dg_v.at[j]))
            cu.append(mv.go(wu.at[l, :, cols], wu_v.at[j]))
        cm = mv.go(mi, mi_v)
        for k in fc:
            k.wait()
        if chained:
            gy = gy_v[...]
            for i in range(2):
                for p in range(3):
                    wq[3 * i + p].wait()
                    gy = gy + mm(gp_v[i, :, p * half : (p + 1) * half], wq_v[i, p], NT)
        else:
            gy = gf_v[...].astype(f32)
        gsum, gterm = norm_back(gy, sm_v[...], g2[pl.ds(l, 1)].astype(f32))
        small_o[1:2] = jnp.sum(gterm, 0, keepdims=True)
        small_o[2:3] = jnp.sum(gy, 0, keepdims=True)
        gf = gsum.astype(bf16)
        gf_v[...] = gf
        small_o[0:1] = jnp.sum(gf.astype(f32), 0, keepdims=True)
        out = [mv.go(gf_v, gf_o)]
        gm_v[...] = gsum
        acc = None
        for j in range(cut):
            cd[j].wait()
            cg[j].wait()
            gpre = (mm(gf_v[...], wd_v[j], NT) * dg_v[j].astype(f32)).astype(bf16)
            gbup_o[:, j * step : (j + 1) * step] = jnp.sum(gpre.astype(f32), 0, keepdims=True)
            cu[j].wait()
            part = mm(gpre, wu_v[j], NT)
            acc = part if acc is None else acc + part
        ghid = gm_v[...] + acc
        cm.wait()
        gmix, gterm = norm_back(ghid, mi_v[...], g1[pl.ds(l, 1)].astype(f32))
        ga = gmix.astype(bf16)
        ga_v[...] = ga
        out.append(mv.go(ga_v, ga_o))
        gm_v[...] = gmix
        out.append(mv.go(gm_v, gm_o))
        small_o[3:4] = jnp.sum(gterm, 0, keepdims=True)
        small_o[4:5] = jnp.sum(ghid, 0, keepdims=True)
        small_o[5:6] = jnp.sum(ga.astype(f32), 0, keepdims=True)
        small_o[6:8] = jnp.zeros((2, width), f32)
        for k in out:
            k.wait()

    S, V = jax.ShapeDtypeStruct, pltpu.VMEM
    low = S((rows, width), bf16)
    outs = (low, low, S((rows, width), f32), S((8, width), f32), S((1, ff), f32))
    scratch = [V((rows, width), f32), V((rows, width), f32), V((rows, width), f32), V((cut, rows, step), bf16),
               V((cut, width, step), bf16), V((cut, step, width), bf16), V((rows, width), bf16), V((rows, width), bf16),
               V((rows, width), f32)]
    if chained:
        scratch += [V((2, rows, 3 * half), bf16), V((2, 3, width, half), bf16)]
    return kernel_call(
        body, "ffn_bwd", (info,) + tuple(flow) + (summed, mixed, dg, w_up, w_down, gain_one, gain_two),
        [SM] + [ANY, ANY, ANY, HBM][: len(flow)] + [ANY, HBM, HBM, HBM, HBM, VM, VM], outs, (ANY, ANY, ANY, VM, VM), scratch,
        15 + 3 * cut, 2 * rows * width * (2 * ff + (3 * width if chained else 0)), 15 << 20,
    )


def chain_end(info, l, flow):
    gmix, gproj, got, w_qkv = flow
    rows, width = gmix.shape
    half = width // 2

    def body(info, gm, gp, gt, w, o_ref, gy_v, gp_v, wq_v, o_v, sems):
        mv = Mover(sems)
        c = info[0]
        wq = []
        fc = [mv.go(gm, gy_v), mv.go(gp.at[pl.ds(0, rows)], gp_v.at[0]), mv.go(gt, gp_v.at[1])]
        for i in range(2):
            who = c if i == 0 else 1 - c
            for p in range(3):
                at = pl.multiple_of(p * width + who * half, 128)
                wq.append(mv.go(w.at[l, :, pl.ds(at, half)], wq_v.at[i, p]))
        for k in fc:
            k.wait()
        gy = gy_v[...]
        for i in range(2):
            for p in range(3):
                wq[3 * i + p].wait()
                gy = gy + mm(gp_v[i, :, p * half : (p + 1) * half], wq_v[i, p], NT)
        o_v[...] = gy.astype(bf16)
        k = mv.go(o_v, o_ref)
        k.wait()

    S, V = jax.ShapeDtypeStruct, pltpu.VMEM
    return kernel_call(
        body, "chain_end", (info,) + tuple(flow), [SM, ANY, ANY, ANY, HBM], S((rows, width), bf16), ANY,
        [V((rows, width), f32), V((2, rows, 3 * half), bf16), V((2, 3, width, half), bf16), V((rows, width), bf16)],
        10, 2 * rows * width * 3 * width, 5 << 20,
    )


def attn_bwd(info, l, go, gt, w_out, qkv, pt):
    rows, width = go.shape
    half = width // 2
    heads = half // HEAD_DIM
    toks = 2 * rows

    def body(info, go, gt, wo, qkv, pt, gp_o, gt_o, gb_o, ga_v, wo_v, qkv_v, pt_v, gc_v, gp_v, sems):
        mv = Mover(sems)
        c = info[0]
        at = pl.multiple_of(c * half, 128)
        fc = [mv.go(wo.at[l, pl.ds(at, half)], wo_v), mv.go(go, ga_v.at[pl.ds(0, rows)]), mv.go(gt, ga_v.at[pl.ds(rows, rows)])]
        cq = mv.go(qkv, qkv_v)
        cp = [mv.go(pt.at[pl.ds(2 * i, 2)], pt_v.at[pl.ds(2 * i, 2)]) for i in range(heads // 2)]
        for k in fc:
            k.wait()
        gc_v[...] = mm(ga_v[...], wo_v[...], NT).astype(bf16)
        cq.wait()
        lane = lax.broadcasted_iota(jnp.int32, (toks, 2 * HEAD_DIM), 1) < HEAD_DIM

        for i in range(heads // 2):
            cp[i].wait()
            at = i * 2 * HEAD_DIM
            at_k, at_v = half + at, 2 * half + at
            q = qkv_v[:, pl.ds(at, 128)]
            k = qkv_v[:, pl.ds(at_k, 128)]
            v = qkv_v[:, pl.ds(at_v, 128)]
            gc = gc_v[:, pl.ds(at, 128)]
            res = []
            for h in range(2):
                gm = jnp.where(lane == (h == 0), gc, jnp.zeros_like(gc))
                pb = pt_v[2 * i + h]
                t = mm(v, gm, NT)
                p = pb.astype(f32)
                inner = jnp.sum(p * t, 0, keepdims=True)
                gs = (p * (t - inner)).astype(bf16)
                res.append((mm(gs, k, TN), mm(gs, q), mm(pb, gc)))
            gq = jnp.where(lane, res[0][0], res[1][0]) * HEAD_DIM ** (-0.5)
            gk = jnp.where(lane, res[0][1], res[1][1])
            gv = jnp.where(lane, res[0][2], res[1][2])
            gq, gk, gv = gq.astype(bf16), gk.astype(bf16), gv.astype(bf16)
            gp_v[:, pl.ds(at, 128)] = gq
            gp_v[:, pl.ds(at_k, 128)] = gk
            gp_v[:, pl.ds(at_v, 128)] = gv
            gb_o[0:1, pl.ds(at, 128)] = jnp.sum(gq.astype(f32), 0, keepdims=True)
            gb_o[1:2, pl.ds(at, 128)] = jnp.sum(gv.astype(f32), 0, keepdims=True)
        low = pl.ds(rows, rows)
        for k in [mv.go(gp_v, gp_o), mv.go(gp_v.at[low], gt_o)]:
            k.wait()

    S, V = jax.ShapeDtypeStruct, pltpu.VMEM
    return kernel_call(
        body, "attn_bwd", (info, go, gt, w_out, qkv, pt), [SM, ANY, ANY, HBM, HBM, HBM],
        (S((toks, 3 * half), bf16), S((rows, 3 * half), bf16), S((2, half), f32)), (ANY, ANY, VM),
        [V((toks, width), bf16), V((half, width), bf16), V((toks, 3 * half), bf16), V((heads, toks, toks), bf16),
         V((toks, half), bf16), V((toks, 3 * half), bf16)],
        8 + heads, 2 * toks * width * half + 20 * heads * toks * toks * 128, 7 << 20,
    )


def place(j, me, order):
    d = jnp.bitwise_xor(j, me)
    n = len(order)
    p = 0
    for i, k in enumerate(order):
        p = p + (jnp.bitwise_and(jnp.right_shift(d, k), 1) << (n - 1 - i))
    return p


def arranged(v, me, order):
    n = len(order)
    rest = v.shape[1:]
    v = v.reshape((2,) * n + rest)
    for k in range(n):
        ax = n - 1 - k
        v = jnp.where(((me >> k) & 1) == 1, jnp.flip(v, ax), v)
    v = v.transpose([n - 1 - k for k in order] + list(range(n, n + len(rest))))
    return v.reshape((2**n,) + rest)


def own_units(info, l, w_up, chips):
    _, width, ff = w_up.shape
    part = ff // chips // 4
    fo = ff // 4
    strip = 128

    def body(info, w, o_ref, w_v, o_v, sems):
        mv = Mover(sems)
        mv.go(w.at[l], w_v).wait()
        for s in range(4):

            @pl.when(info[3] == s)
            def _():
                def some(r, _):
                    at = pl.ds(pl.multiple_of(r * strip, strip), strip)
                    for i in range(chips):
                        o_v[at, i * part : (i + 1) * part] = w_v[at, (4 * i + s) * part : (4 * i + s + 1) * part]
                    return 0

                lax.fori_loop(0, width // strip, some, 0)

        mv.go(o_v, o_ref).wait()

    S, V = jax.ShapeDtypeStruct, pltpu.VMEM
    return kernel_call(
        body, "own_units", (info, w_up), [SM, HBM], S((width, fo), bf16), ANY,
        [V((width, ff), bf16), V((width, fo), bf16)], 2, 0, 6 << 20,
    )


def ffn_grads(info, l, hs, gs, wu_own, w_down, b_own, small, gbup, gqv, orders, fast):
    rows, width = hs[0].shape[-2:]
    fo = wu_own.shape[1]
    n = len(hs)
    paired = gs is None
    gs = () if paired else tuple(gs)
    m = n + len(gs)
    chips = 2 ** len(orders[0])
    part, unit = width // chips, fo // chips
    split = len(orders) == 2

    def body(*refs):
        info = refs[0]
        if paired:
            hr, gr = [r.at[0] for r in refs[1 : 1 + n]], [r.at[1] for r in refs[1 : 1 + n]]
        else:
            hr, gr = refs[1 : 1 + n], refs[1 + n : 1 + 2 * n]
        wu, wd, b, sm, bup, gqv = refs[1 + m : 7 + m]
        ends = refs[7 + m : 7 + m + 2 * len(orders)] if fast else refs[7 + m : 9 + m]
        h_v, g_v, wu_v, wd_v, act_v, gp_v, *o_vs, sm_v, sems = refs[7 + m + len(ends) :]
        o_v = o_vs[0]
        mv = Mover(sems)
        cu = mv.go(wu, wu_v)
        ch = [mv.go(hr[i], h_v.at[pl.ds(i * rows, rows)]) for i in range(n)]
        if fast:
            cd = []
            for i in range(chips):
                at = pl.multiple_of((4 * i + info[3]) * unit, unit)
                cd.append(mv.go(wd.at[l, pl.ds(at, unit)], wd_v.at[pl.ds(i * unit, unit)]))
        else:
            cd = [mv.go(wd.at[l], wd_v)]
        cg = [mv.go(gr[i], g_v.at[pl.ds(i * rows, rows)]) for i in range(n)]
        cu.wait()
        for i in range(n):
            at = pl.ds(i * rows, rows)
            ch[i].wait()
            u = mm(h_v[at], wu_v[...]) + b[l].astype(f32)
            cdf, slope = phi_parts(u)
            act_v[at] = (u * cdf).astype(bf16)
            if i == 0:
                for k in cd:
                    k.wait()
            cg[i].wait()
            gp_v[at] = (mm(g_v[at], wd_v[...], NT) * slope).astype(bf16)
        up = mm(h_v[...], gp_v[...], TN).astype(bf16)
        if fast:
            for j in range(chips):
                o_v[place(j, info[1], orders[0]), :part] = up[j * part : (j + 1) * part]
            if split:
                halfway = chips // 2
                out = [mv.go(o_v.at[pl.ds(halfway, halfway)], ends[0]), mv.go(o_v.at[pl.ds(0, halfway)], ends[1])]
        else:
            o_v[:width] = up
        down = mm(act_v[...], g_v[...], TN).astype(bf16)
        if fast:
            sm_v[...] = sm[...]
            sm_v[6:8, pl.ds(pl.multiple_of(info[0] * (width // 2), 128), width // 2)] = gqv[...]
            whole = sm_v[...]
            low_v, top = o_vs[-1], 0 if split else part
            for j in range(chips):
                p = place(j, info[1], orders[-1])
                low_v[p, top : top + unit] = down[j * unit : (j + 1) * unit]
                low_v[p, top + unit :] = jnp.concatenate(
                    [
                        jnp.concatenate([whole[:, j * part : (j + 1) * part], jnp.zeros((8, width - part), f32)], 1),
                        jnp.concatenate([bup[:, 4 * j * unit : 4 * (j + 1) * unit], jnp.zeros((1, width - 4 * unit), f32)], 1),
                        jnp.zeros((7, width), f32),
                    ]
                ).astype(bf16)
            halfway = chips // 2
            out = out if split else []
            out += [mv.go(low_v.at[pl.ds(halfway, halfway)], ends[-2]), mv.go(low_v.at[pl.ds(0, halfway)], ends[-1])]
        else:
            o_v[width:] = down
            out = [mv.go(o_v.at[pl.ds(0, width)], ends[0]), mv.go(o_v.at[pl.ds(width, fo)], ends[1])]
        for k in out:
            k.wait()

    S, V = jax.ShapeDtypeStruct, pltpu.VMEM
    tok = V((n * rows, width), bf16)
    hid = V((n * rows, fo), bf16)
    if fast:
        sizes = (part, unit + 16) if split else (part + unit + 16,)
        outs = tuple(S((chips // 2, n_rows, width), bf16) for n_rows in sizes for _ in range(2))
        o_vs = [V((chips, n_rows, width), bf16) for n_rows in sizes]
    else:
        outs = (S((width, fo), bf16), S((fo, width), bf16))
        o_vs = [V((width + fo, width), bf16)]
    got = kernel_call(
        body, "ffn_grads", (info,) + tuple(hs) + gs + (wu_own, w_down, b_own, small, gbup, gqv), [SM] + [ANY] * m + [HBM, HBM] + [VM] * 4,
        outs, (ANY,) * len(outs), [tok, tok, V((width, fo), bf16), V((fo, width), bf16), hid, hid] + o_vs + [V((8, width), f32)],
        2 * n + 6 + chips, 8 * n * rows * width * fo, 8 << 20,
    )
    if fast:
        return [(got[2 * i], got[2 * i + 1]) for i in range(len(orders))]
    zero = jnp.zeros_like(gqv)
    gqv = jnp.where(info[0] == 0, jnp.concatenate([gqv, zero], 1), jnp.concatenate([zero, gqv], 1))
    small = jnp.concatenate([small[:6], gqv]).reshape(8, chips, part).transpose(1, 0, 2)
    small = jnp.concatenate([jnp.pad(small, ((0, 0), (0, 0), (0, width - part))),
                             jnp.pad(gbup.reshape(chips, 1, 4 * unit), ((0, 0), (0, 7), (0, width - 4 * unit)))], 1)
    both = [[got[0].reshape(chips, part, fo)], [got[1].reshape(chips, unit, width), small.astype(bf16)]]
    if not split:
        both = [both[0] + both[1]]
    both = [arranged(jnp.concatenate(v, 1), info[1], order) for v, order in zip(both, orders)]
    return [(v[chips // 2 :], v[: chips // 2]) for v in both]


def proj_grads(info, xo, xt, ctx, got, go, gt, gproj, order, fast):
    rows, width = xo.shape
    half = width // 2
    toks = 2 * rows
    chips = 2 ** len(order)
    part = width // chips

    def body(info, xo, xt, ctx, got, go, gt, gp, *refs):
        outs, (x_v, gp_v, c_v, ga_v, o_v, sems) = refs[:-6], refs[-6:]
        mv = Mover(sems)
        c, me, y = info[0], info[1], info[2]
        top, low = pl.ds(0, rows), pl.ds(rows, rows)
        cols = pl.ds(pl.multiple_of(c * half, 128), half)
        cx = [mv.go(xo, x_v.at[top]), mv.go(xt, x_v.at[low]), mv.go(gp, gp_v)]
        cc = [mv.go(ctx, c_v.at[0]), mv.go(got.at[low], c_v.at[1, top]), mv.go(got.at[top], c_v.at[1, low]),
              mv.go(go.at[:, cols], ga_v.at[top]), mv.go(gt.at[:, cols], ga_v.at[low])]
        for k in cx:
            k.wait()
        for g in range(4):
            if g < 3:
                blocks = [(0, mm(x_v[...], gp_v[:, g * half : (g + 1) * half], TN).astype(bf16))]
            else:
                for k in cc:
                    k.wait()
                blocks = [(c if i == 0 else 1 - c, mm(c_v[i], ga_v[...], TN).astype(bf16)) for i in range(2)]
            at = slice(g % 2 * half, (g % 2 + 1) * half)
            for who, val in blocks:
                if fast:
                    for j in range(val.shape[0] // part):
                        p = place(who * (chips // 2) + j, me, order)
                        o_v[jnp.bitwise_xor(g // 2, y), p, :, at] = val[j * part : (j + 1) * part]
                elif g < 3:
                    o_v[g // 2, :, at] = val
                else:
                    o_v[1, pl.ds(pl.multiple_of(who * half, 128), half), at] = val
        out = [mv.go(o_v.at[1], outs[0]), mv.go(o_v.at[0], outs[1])] if fast else [mv.go(o_v, outs[0])]
        for k in out:
            k.wait()

    S, V = jax.ShapeDtypeStruct, pltpu.VMEM
    shape = (2, chips, part, width) if fast else (2, width, width)
    res = kernel_call(
        body, "proj_grads", (info, xo, xt, ctx, got, go, gt, gproj), [SM] + [ANY] * 7,
        (S(shape[1:], bf16),) * 2 if fast else S(shape, bf16), (ANY, ANY) if fast else ANY,
        [V((toks, width), bf16), V((toks, 3 * half), bf16), V((2, toks, half), bf16), V((toks, half), bf16), V(shape, bf16)],
        10, 2 * toks * width * 4 * half, 6 << 20,
    )
    if fast:
        return res
    v = res.reshape(2, chips, part, width)
    v = jnp.where(info[2] == 1, v[::-1], v)
    return arranged(v[1], info[1], order), arranged(v[0], info[1], order)


def pack(info, ends, part, unit, fast):
    width = ends[0][0].shape[-1]
    hp = part // 2
    if not fast:
        v = jnp.concatenate([add(k[0], g[0]).astype(bf16) for k, g in ends])
        up, low, proj = v[:part].reshape(2, hp, width), v[part : part + unit + 16], v[part + unit + 16 :].reshape(2, hp, width)
        mine, other = pick(up, info[0], 0), pick(up, 1 - info[0], 0)
        return (jnp.concatenate([mine, low, pick(proj, info[0], 0)]), jnp.concatenate([other, low[unit:], pick(proj, 1 - info[0], 0)]))
    n = len(ends)

    def body(info, *refs):
        ks, gs, row_o, col_o = refs[:n], refs[n : 2 * n], refs[2 * n], refs[2 * n + 1]
        k_v, g_v, row_v, col_v, sems = refs[2 * n + 2 :]
        mv = Mover(sems)
        at, come = 0, []
        for k, g in zip(ks, gs):
            now = pl.ds(at, k.shape[1])
            come += [mv.go(k.at[0], k_v.at[now]), mv.go(g.at[0], g_v.at[now])]
            at += k.shape[1]
        for c in come:
            c.wait()
        v = (k_v[...].astype(f32) + g_v[...].astype(f32)).astype(bf16)
        first = info[0] == 0
        lo = part + unit + 16
        up0, up1, pr0, pr1 = v[:hp], v[hp:part], v[lo : lo + hp], v[lo + hp :]
        row_v[:hp] = jnp.where(first, up0, up1)
        row_v[hp : hp + unit + 16] = v[part:lo]
        row_v[hp + unit + 16 :] = jnp.where(first, pr0, pr1)
        col_v[:hp] = jnp.where(first, up1, up0)
        col_v[hp : hp + 16] = v[lo - 16 : lo]
        col_v[hp + 16 :] = jnp.where(first, pr1, pr0)
        for c in [mv.go(col_v, col_o), mv.go(row_v, row_o)]:
            c.wait()

    total = sum(k.shape[1] for k, _ in ends)
    S, V = jax.ShapeDtypeStruct, pltpu.VMEM
    shapes = [(part + unit + 16, width), (part + 16, width)]
    return kernel_call(
        body, "pack", (info,) + tuple(k for k, _ in ends) + tuple(g for _, g in ends), [SM] + [ANY] * (2 * n),
        tuple(S(v, bf16) for v in shapes), (ANY, ANY), [V((total, width), bf16)] * 2 + [V(v, bf16) for v in shapes], 2 * n + 2, 0, 0,
    )


def unpack(info, rounds, part, unit, chips, fast):
    layers = len(rounds)
    width = rounds[0][0].shape[-1]
    hp, half = part // 2, width // 2
    lo = hp + unit + 16
    if not fast:
        res = []
        for own, row, core, diag in rounds:
            def quarters(a, b):
                mine = order_two(info[2], own[a], row[a], 0)
                other = order_two(info[2], core[b], diag[b], 0)
                return order_two(info[0], mine, other, 0)

            up = quarters(slice(0, hp), slice(0, hp)).reshape(2, 2, hp, chips, unit)
            up = up.transpose(2, 3, 0, 1, 4).reshape(hp, 4 * width).astype(f32)
            proj = quarters(slice(lo, lo + hp), slice(hp + 16, part + 16)).reshape(2, 2, hp, 2, half)
            proj = proj.transpose(2, 1, 3, 0, 4).reshape(hp, 4 * width).astype(f32)
            down = order_two(info[2], own[hp : hp + unit], row[hp : hp + unit], 0).reshape(2 * unit, width).astype(f32)
            small = add(own[lo - 16 : lo], row[lo - 16 : lo]) + add(core[hp : hp + 16], diag[hp : hp + 16])
            vecs = pick(small[:8, :part].reshape(8, 2, hp), info[0], 1)
            bup = pick(small[8, : 4 * unit].reshape(2, 2 * unit), info[0], 0)
            res.append((proj[:, : 3 * width], proj[:, 3 * width :], up, down, bup, vecs[6:8]) + tuple(vecs[i] for i in range(6)))
        return tuple(jnp.stack([r[i] for r in res]) for i in range(12))

    def body(info, *refs):
        src, outs = refs[: 4 * layers], refs[4 * layers : 4 * layers + 12]
        big_v, small_v, q_v, d_v, sems = refs[4 * layers + 12 :]
        mv = Mover(sems)
        come = []
        for l in range(layers):
            for i in range(4):
                to = big_v.at[l, i] if i < 2 else small_v.at[l, i - 2]
                come.append(mv.go(src[4 * l + i], to))
        qkv, out, up, down, bup, gqv = outs[:6]
        c, y, share = info[0], info[2], info[3]
        first = c == 0
        for l in range(layers):
            for k in come[4 * l : 4 * l + 4]:
                k.wait()
            diag = 3 - share
            for p, (a, b) in enumerate(((0, 0), (lo, hp + 16))):
                q_v[p, share] = big_v[l, 0, a : a + hp]
                q_v[p, 2 * c + 1 - y] = big_v[l, 1, a : a + hp]
                q_v[p, 2 * (1 - c) + y] = small_v[l, 0, b : b + hp]
                q_v[p, diag] = small_v[l, 1, b : b + hp]
            d_v[y] = big_v[l, 0, hp : hp + unit]
            d_v[1 - y] = big_v[l, 1, hp : hp + unit]
            for q in range(4):
                whole = q_v[0, q].astype(f32)
                for i in range(chips):
                    up[l, :, (4 * i + q) * unit : (4 * i + q + 1) * unit] = whole[:, i * unit : (i + 1) * unit]
                whole = q_v[1, q].astype(f32)
                at = q // 2 * half
                if q % 2 == 0:
                    qkv[l, :, at : at + half] = whole[:, :half]
                    qkv[l, :, width + at : width + at + half] = whole[:, half:]
                else:
                    qkv[l, :, 2 * width + at : 2 * width + at + half] = whole[:, :half]
                    out[l, :, at : at + half] = whole[:, half:]
            for i in range(2):
                down[l, i * unit : (i + 1) * unit] = d_v[i].astype(f32)
            small = (big_v[l, 0, lo - 16 : lo].astype(f32) + big_v[l, 1, lo - 16 : lo].astype(f32)) + (
                small_v[l, 0, hp : hp + 16].astype(f32) + small_v[l, 1, hp : hp + 16].astype(f32))
            vecs = jnp.where(first, small[:8, :hp], small[:8, hp:part])
            bup[l : l + 1] = jnp.where(first, small[8:9, : 2 * unit], small[8:9, 2 * unit : 4 * unit])
            gqv[l] = vecs[6:8]
            for i in range(6):
                outs[6 + i][l : l + 1] = vecs[i : i + 1]

    S, V = jax.ShapeDtypeStruct, pltpu.VMEM
    outs = [(layers, hp, 3 * width), (layers, hp, width), (layers, hp, 4 * width), (layers, 2 * unit, width), (layers, 2 * unit), (layers, 2, hp)]
    outs += [(layers, hp)] * 6
    args = (info,) + tuple(v for r in rounds for v in r)
    return kernel_call(
        body, "unpack", args, [SM] + [ANY] * (4 * layers), tuple(S(v, f32) for v in outs), (VM,) * 12,
        [V((layers, 2, part + unit + 16, width), bf16), V((layers, 2, part + 16, width), bf16), V((2, 4, hp, width), bf16), V((2, unit, width), bf16)],
        4 * layers, 0, 0,
    )


class Wires:
    def __init__(self, batch, seq):
        self.batch, self.seq = batch, seq
        self.chips = batch // 2
        self.bits = self.chips.bit_length() - 1
        where = [(i, j) for i in range(batch) for j in range(seq)]

        def table(move):
            out = []
            for i, j in where:
                p, q = move(i, j)
                out.append((i * seq + j, p * seq + q))
            return out

        self.core = table(lambda i, j: (i ^ 1, j))
        self.row = table(lambda i, j: (i, 1 - j))
        self.diag = table(lambda i, j: (i ^ 1, 1 - j))
        self.turn = table(lambda i, j: (i - i % 2 + j, i % 2))
        self.chip = [table(lambda i, j, k=k: (i ^ (2 << k), j)) for k in range(self.bits)]
        self.b = lax.axis_index("batch")
        self.y = lax.axis_index("seq")
        self.c = self.b % 2

    def swap_core(self, v):
        return lax.ppermute(v, AXES, self.core)

    def swap_row(self, v):
        return lax.ppermute(v, AXES, self.row)

    def swap_diag(self, v):
        return lax.ppermute(v, AXES, self.diag)

    def swap_turn(self, v):
        return lax.ppermute(v, AXES, self.turn)

    def swap_chip(self, v, k):
        return lax.ppermute(v, AXES, self.chip[k])

    def bit(self, k):
        return (self.b >> (k + 1)) & 1


def pick(v, idx, axis):
    return lax.dynamic_index_in_dim(v, idx, axis, keepdims=False)


def add(a, b):
    return a.astype(f32) + b.astype(f32)


def order_two(flag, mine, got, axis):
    return jnp.stack([jnp.where(flag == 0, mine, got), jnp.where(flag == 0, got, mine)], axis)


class Clock:
    def __init__(self):
        self.now, self.free, self.alive = 0.0, {}, []

    def busy(self, link, us):
        begin = max(self.now, self.free.get(link, 0.0))
        self.free[link] = begin + us
        return begin + us

    def work(self, us):
        self.now += us

    def catch_up(self):
        for s in sorted(self.alive, key=lambda s: s.ready):
            if s.ready <= self.now + 3.0:
                s.step()

    def drain(self):
        while self.alive:
            min(self.alive, key=lambda s: s.ready).step()


class Stream:
    def __init__(self, wires, clock, send, keep, order, row_first):
        self.wires, self.clock, self.keep, self.end = wires, clock, keep, None
        self.todo = list(order)
        clock.alive.append(self)
        self.send(send, row_first)

    def send(self, v, row=False):
        us = v.size * 2 / 1e6 * 22.0
        if row:
            self.got, link = self.wires.swap_row(v), "y"
        else:
            k = self.todo.pop(0)
            self.got = self.wires.swap_chip(v, k)
            link = "x" if k == 0 else "z"
            us *= max(1, 1 << (k - 1)) if k else 1
        self.clock.work(1.4)
        self.ready = self.clock.busy(link, us) + 2.0

    def step(self):
        clock = self.clock
        clock.now = max(clock.now, self.ready)
        if not self.todo:
            self.end = (self.keep, self.got)
            clock.alive.remove(self)
            return
        clock.work(1.2 + self.keep.size * 2 / 1e6)
        send, self.keep = merge(self.keep, self.got)
        self.send(send)


def local(inputs, out_grad, masked, w_qkv, bias_qv, w_out, bias_out, gain_one, shift_one, w_up, bias_up, w_down, bias_down, gain_two, shift_two):
    wires = Wires(lax.axis_size("batch"), lax.axis_size("seq"))
    layers, width, ff = w_up.shape
    half = width // 2
    chips, bits = wires.chips, wires.bits
    fo, unit, part = ff // 4, ff // chips // 4, width // chips
    fast = part % 32 == 0
    share = wires.c * 2 + wires.y
    info = jnp.stack([wires.c, wires.b // 2, wires.y, share]).astype(jnp.int32)
    rows = inputs.shape[1]
    ROW.extra = []
    xb = wires.swap_turn(inputs[0])
    b_own = pick(bias_up.reshape(layers, chips, 4, unit), share, 2).reshape(layers, 1, fo)
    if fast:
        wu_own, wd_own = [own_units(info, l, w_up, chips) for l in range(layers)], w_down
    else:
        wu_own = pick(w_up.reshape(layers, width, chips, 4, unit), share, 3).reshape(layers, width, fo)
        wd_own = pick(w_down.reshape(layers, chips, 4, unit, width), share, 2).reshape(layers, fo, width)
    x = xb
    saved, outs, hs = [], [], []
    tail = (w_out, bias_out, gain_one, shift_one, w_up, bias_up, w_down, bias_down, gain_two, shift_two)
    clock = Clock()
    for l in range(layers):
        xt = wires.swap_core(xb)
        qkv, pt, ctx = attn_fwd(info, l, xb, xt, w_qkv, bias_qv)
        if l == 0:
            gy = wires.swap_turn(masked_grad(out_grad[0], masked))
        else:
            ROW.before_next(outs[-1])
        got = wires.swap_core(ctx)
        last = l == layers - 1
        if last:
            yb, pair, ga, gm, small, gbup = ffn_fwd(info, l, x, ctx, got, tail, gy)
            saved.append((xb, xt, qkv, pt, ctx, got))
            turned_back = (pair, ga, gm, small, gbup)
        else:
            hb, dg, mixed, x, yb = ffn_fwd(info, l, x, ctx, got, tail)
            hy = wires.swap_row(hb)
            hs.append((hb, hy, wires.swap_core(hb), wires.swap_core(hy)))
            saved.append((xb, xt, qkv, pt, ctx, got, dg, mixed, x))
        outs.append(wires.swap_turn(yb)[None])
        xb = yb
        if l == 0:
            ROW.before_next(gy)
    low = list(range(bits))
    turned = low[1:2] + low[:1] + low[2:]
    plan = [((low, turned), low)] + [((turned,), turned)] * (layers - 1)
    streams = [None] * layers
    for l in reversed(range(layers)):
        xb, xt, qkv, pt, ctx, got = saved[l][:6]
        if l == layers - 1:
            pair, ga, gm, small, gbup = turned_back
            gat = wires.swap_core(ga)
            py = wires.swap_row(pair)
            both = (pair, py, wires.swap_core(pair), wires.swap_core(py)), None
        else:
            dg, mixed, summed = saved[l][6:]
            gf, ga, gm, small, gbup = ffn_bwd(info, l, flow, summed, mixed, dg, (w_up, w_down, gain_one, gain_two))
            gat = wires.swap_core(ga)
            gfy = wires.swap_row(gf)
            both = hs[l], (gf, gfy, wires.swap_core(gf), wires.swap_core(gfy))
        gproj, gptail, gqv = attn_bwd(info, l, ga, gat, w_out, qkv, pt)
        if l == layers - 1:
            ROW.before_next(*hs[-1])
        flow = (gm, gproj, wires.swap_core(gptail), w_qkv)
        clock.work(28.0 if l < layers - 1 else 0.0)
        clock.catch_up()
        send, keep = proj_grads(info, xb, xt, ctx, got, ga, gat, gproj, plan[l][1], fast)
        clock.work(4.5)
        ps = [Stream(wires, clock, send, keep, plan[l][1], True)]
        if l == layers - 1:
            ROW.before_next(outs[-1])
        clock.catch_up()
        res = ffn_grads(info, l, *both, wu_own[l], wd_own, b_own, small, gbup, gqv, plan[l][0], fast)
        clock.work(10.5)
        fs = [Stream(wires, clock, s, k, order, False) for (s, k), order in zip(res, plan[l][0])]
        clock.catch_up()
        streams[l] = fs + ps
    end = chain_end(info, 0, flow)
    clock.work(5.5)
    grad_in = wires.swap_turn(end)[None]
    rounds = [None] * layers
    while not all(rounds):
        if clock.alive:
            min(clock.alive, key=lambda s: s.ready).step()
        for l in range(layers):
            if rounds[l] is None and all(s.end for s in streams[l]):
                row, col = pack(info, [s.end for s in streams[l]], part, unit, fast)
                rounds[l] = (row, wires.swap_row(row), wires.swap_core(col), wires.swap_diag(col))
                clock.work(5.0)
                clock.busy("y", 11.0)
    qkv, out, up, down, bup, gqv, gdn, gg2, gs2, gg1, gs1, gbo = unpack(info, rounds, part, unit, chips, fast)
    return (outs[0], outs[-1], grad_in, qkv, gqv, out, gbo, gg1, gs1, up, bup, down, gdn, gg2, gs2)


def solution(mesh):
    tok = P("batch", "seq", None)
    in_specs = (tok, tok, P("batch", "seq")) + (P(),) * 12
    mat, vec = P(None, "batch", None), P(None, "batch")
    out_specs = (tok, tok, tok, mat, P(None, None, "batch"), mat, vec, vec, vec, mat, vec, mat, vec, vec, vec)
    return jax.shard_map(local, mesh=mesh, in_specs=in_specs, out_specs=out_specs, check_vma=False)
```
